128 devices in a mesh: seq: 4 (over x), tensor: 32 (over z, y, core).
Axes of the slice: x: 4, y: 4, z: 4, core: 2. Of those that a mesh axis runs over, the one named last changes fastest.
Arguments:
- states: bfloat16 [64, 2048], P('tensor'), may hold values from -6 to 6
- attn_gain: bfloat16 [2048], replicated, may hold values from 0.5 to 1.5
- w_qkv: bfloat16 [2048, 3, 2048], P(None, None, 'tensor'), may hold values from -0.125 to 0.125
- w_out: bfloat16 [2048, 2048], P('tensor'), may hold values from -0.125 to 0.125
- mlp_gain: bfloat16 [2048], replicated, may hold values from 0.5 to 1.5
- w_gate_up: bfloat16 [2048, 2, 8192], P(None, None, 'tensor'), may hold values from -0.125 to 0.125
- w_down: bfloat16 [8192, 2048], P('tensor'), may hold values from -0.0625 to 0.0625
- key_cache: bfloat16 [64, 2048, 4096], P('tensor', None, 'seq')
- value_cache: bfloat16 [64, 2048, 4096], P('tensor', None, 'seq')
- sink_keys: bfloat16 [64, 2048, 4], P('tensor'), may hold values from -8 to 8
- sink_values: bfloat16 [64, 2048, 4], P('tensor'), may hold values from -6 to 6
- cache_len: int32 [64], replicated, may hold values from 1 to 4096, as said below
- slot_mask: int32 [64, 4096], P('tensor', 'seq'), may hold values 0 or 1
- slot_pos: int32 [64, 4096], P('tensor', 'seq'), may hold values from 0 to 8191
- new_pos: int32 [64], replicated, may hold values from 4096 to 8191
Outputs:
- out_states: bfloat16 [64, 2048], P('tensor')
- new_keys: bfloat16 [64, 2048], P(None, 'tensor')
- new_values: bfloat16 [64, 2048], P(None, 'tensor')
The draws below stay inside these ranges and needn't reach their ends.
Inputs may be any that keep to these rules, and one draw needn't show every extreme that they name: `cache_len`: at least one request has all 4096 slots filled in every draw.
All inputs are finite; a program needn't handle non-finite values. No bound on the sum of `slot_mask` on one device may be relied on, other than what follows from the above.
Results may differ from the reference program's by a relative error of at most 0.02.
The reference program's roundings to bfloat16 on the way count: a program that leaves them out, or rounds other values in their place, can miss the bound.
Values may be sent and summed in bfloat16 or wider, within the bound.
A program may use at most 64 MiB of HBM per device.

```python
import jax
import jax.numpy as jnp
from jax import lax

D = 2048
ATTENTION_HEADS = 32
HEAD_SIZE = 64
FF = 8192
SINK_COUNT = 4
WINDOW = 4096
REQ = 64


def draw_key_cache(key, part):
    first = jax.random.fold_in(jax.random.fold_in(key, 11), 0)
    shape = (REQ, ATTENTION_HEADS * HEAD_SIZE, WINDOW)
    base = jax.random.normal(first, shape, jnp.float32)
    return base.astype(jnp.bfloat16)


def draw_value_cache(key, part):
    first = jax.random.fold_in(jax.random.fold_in(key, 23), 0)
    shape = (REQ, ATTENTION_HEADS * HEAD_SIZE, WINDOW)
    base = jax.random.normal(first, shape, jnp.float32)
    return base.astype(jnp.bfloat16)


def draw_cache_len(key, part):
    first, second, third = jax.random.split(jax.random.fold_in(key, 37), 3)
    left = jax.random.randint(first, (REQ,), 1, WINDOW + 1)
    right = jax.random.randint(second, (REQ,), 1, WINDOW + 1)
    lengths = jnp.maximum(left * right // WINDOW, 1)
    chosen = jax.random.randint(third, (), 0, REQ)
    lengths = jnp.where(jnp.arange(REQ) == chosen, WINDOW, lengths)
    return lengths.astype(jnp.int32)


def with_ends(values, key, smallest, largest):
    extent = values.shape
    place = [jax.random.randint(jax.random.fold_in(key, axis), (), 0, extent[axis]) for axis in range(len(extent))]
    values = values.at[tuple(place)].set(smallest)
    longest = extent.index(max(extent))
    place[longest] = (place[longest] + 1) % extent[longest]
    return values.at[tuple(place)].set(largest)


def levels(key, shape, shards, least, high):
    loudness = 1.0
    for axis_at, blocks in shards:
        heights = jax.random.uniform(jax.random.fold_in(jax.random.fold_in(key, 6), axis_at), (blocks,), jnp.float32, least / len(shards), high / len(shards))
        loudness = loudness * jnp.repeat(jnp.exp(heights), shape[axis_at] // blocks).reshape((-1,) + (1,) * (len(shape) - 1 - axis_at))
    return loudness


def scatter_about(own_key, shape, spread, reach, pieces=(), kind=jnp.bfloat16):
    result = spread * jax.random.normal(own_key, shape, jnp.float32)
    if pieces:
        result = result * levels(own_key, shape, pieces, -0.22, 0.18)
    return jnp.clip(result, -reach, reach).astype(kind)


def setup_inputs(seed: int = 0) -> dict:
    streams_of = jax.random.split(jax.random.key(seed), 16)
    return {
        "states": scatter_about(streams_of[0], (REQ, D), 1.0, 6.0, ((0, 32),)),
        "attn_gain": jnp.clip(1.0 + 0.1 * jax.random.normal(streams_of[1], (D,), jnp.float32), 0.5, 1.5).astype(jnp.bfloat16),
        "w_qkv": scatter_about(streams_of[2], (D, 3, ATTENTION_HEADS * HEAD_SIZE), D ** -0.5, 0.125, ((2, 32),)),
        "w_out": scatter_about(streams_of[3], (ATTENTION_HEADS * HEAD_SIZE, D), (ATTENTION_HEADS * HEAD_SIZE) ** -0.5, 0.125, ((0, 32),)),
        "mlp_gain": jnp.clip(1.0 + 0.1 * jax.random.normal(streams_of[4], (D,), jnp.float32), 0.5, 1.5).astype(jnp.bfloat16),
        "w_gate_up": scatter_about(streams_of[5], (D, 2, FF), D ** -0.5, 0.125, ((2, 32),)),
        "w_down": scatter_about(streams_of[6], (FF, D), FF ** -0.5, 0.0625, ((0, 32),)),
        "key_cache": draw_key_cache(jax.random.fold_in(streams_of[15], 71), 0),
        "value_cache": draw_value_cache(jax.random.fold_in(streams_of[15], 71), 0),
        "sink_keys": scatter_about(streams_of[9], (REQ, ATTENTION_HEADS * HEAD_SIZE, SINK_COUNT), 2.0, 8.0, ((0, 32),)),
        "sink_values": scatter_about(streams_of[10], (REQ, ATTENTION_HEADS * HEAD_SIZE, SINK_COUNT), 1.0, 6.0, ((0, 32),)),
        "cache_len": draw_cache_len(jax.random.fold_in(streams_of[15], 71), 0),
        "slot_mask": with_ends((jax.random.randint(streams_of[12], (REQ, WINDOW), 0, 4) < 3).astype(jnp.int32), jax.random.fold_in(streams_of[12], 1), 0, 1),
        "slot_pos": with_ends(jax.random.randint(streams_of[13], (REQ, WINDOW), 0, 2 * WINDOW), jax.random.fold_in(streams_of[13], 1), 0, (2 * WINDOW) - 1).astype(jnp.int32),
        "new_pos": with_ends(jax.random.randint(streams_of[14], (REQ,), WINDOW, 2 * WINDOW), jax.random.fold_in(streams_of[14], 1), WINDOW, (2 * WINDOW) - 1).astype(jnp.int32),
    }


NEG = -1e+30

def rms_norm(values, gain):
    meansq = lax.optimization_barrier(jnp.mean(values * values, axis=-1, keepdims=True))
    return (values * lax.rsqrt(meansq + 1e-05) * gain.astype(jnp.float32)).astype(jnp.bfloat16)

def rotary(tensor, cosine, sine):
    half = tensor.shape[-1] // 2
    turned = jnp.concatenate([-tensor[..., half:], tensor[..., :half]], axis=-1)
    return tensor * cosine + turned * sine

def undo_round(weights):
    rounded = lax.optimization_barrier(weights.astype(jnp.bfloat16))
    return rounded.astype(jnp.float32)

def reference(states, attn_gain, w_qkv, w_out, mlp_gain, w_gate_up, w_down, key_cache, value_cache, sink_keys, sink_values, cache_len, slot_mask, slot_pos, new_pos):
    floats = states.astype(jnp.float32)
    normed = rms_norm(floats, attn_gain)
    projected = jnp.dot(normed, w_qkv.reshape(D, 3 * ATTENTION_HEADS * HEAD_SIZE), preferred_element_type=jnp.float32)
    projected = projected.reshape(REQ, 3, ATTENTION_HEADS, HEAD_SIZE)
    half = HEAD_SIZE // 2
    inverse = jnp.exp(-jnp.log(jnp.float32(130000.0)) * jnp.arange(half, dtype=jnp.float32) * (2.0 / HEAD_SIZE))
    angle = new_pos.astype(jnp.float32)[:, None] * inverse[None, :]
    angle = jnp.concatenate([angle, angle], axis=-1)[:, None, :]
    cosine = jnp.cos(angle)
    sine = jnp.sin(angle)
    queries = rotary(projected[:, 0], cosine, sine).astype(jnp.bfloat16)
    keys_new = rotary(projected[:, 1], cosine, sine).astype(jnp.bfloat16)
    values_new = projected[:, 2].astype(jnp.bfloat16)
    slots = jnp.arange(WINDOW, dtype=jnp.int32)
    live = (slots[None, :] < cache_len[:, None]) & (slot_mask == 1)
    live = live & (slot_pos < new_pos[:, None]) & (new_pos[:, None] - slot_pos < WINDOW)

    def one_request(entry_list):
        query_vector, single_key, single_value, window_key_cache, window_value_cache, sink_key_block, sink_value_block, valid_mask = entry_list
        qfloat = query_vector.astype(jnp.float32)
        kwin = window_key_cache.astype(jnp.float32).reshape(ATTENTION_HEADS, HEAD_SIZE, WINDOW)
        vwin = window_value_cache.astype(jnp.float32).reshape(ATTENTION_HEADS, HEAD_SIZE, WINDOW)
        sink_key_rows = sink_key_block.astype(jnp.float32).reshape(ATTENTION_HEADS, HEAD_SIZE, SINK_COUNT)
        vsink = sink_value_block.astype(jnp.float32).reshape(ATTENTION_HEADS, HEAD_SIZE, SINK_COUNT)
        score_win = jnp.einsum('hd,hds->hs', qfloat, kwin) * 0.125
        score_win = jnp.where(valid_mask[None, :], score_win, NEG)
        score_sink = jnp.einsum('hd,hds->hs', qfloat, sink_key_rows) * 0.125
        score_new = lax.optimization_barrier(jnp.sum(qfloat * single_key.astype(jnp.float32), axis=-1)) * 0.125
        top = jnp.maximum(jnp.maximum(lax.optimization_barrier(jnp.max(score_win, axis=-1)), lax.optimization_barrier(jnp.max(score_sink, axis=-1))), score_new)
        weight_win = jnp.where(valid_mask[None, :], jnp.exp(score_win - top[:, None]), 0.0)
        weight_sink = jnp.exp(score_sink - top[:, None])
        weight_new = jnp.exp(score_new - top)
        total = lax.optimization_barrier(jnp.sum(weight_win, axis=-1)) + lax.optimization_barrier(jnp.sum(weight_sink, axis=-1)) + weight_new
        mixture = jnp.einsum('hs,hds->hd', undo_round(weight_win), vwin)
        mixture = mixture + jnp.einsum('hs,hds->hd', undo_round(weight_sink), vsink)
        mixture = mixture + undo_round(weight_new)[:, None] * single_value.astype(jnp.float32)
        return (mixture / total[:, None]).astype(jnp.bfloat16).reshape(ATTENTION_HEADS * HEAD_SIZE)
    attended = lax.map(one_request, (queries, keys_new, values_new, key_cache, value_cache, sink_keys, sink_values, live))
    resid = (floats + jnp.dot(attended, w_out, preferred_element_type=jnp.float32)).astype(jnp.bfloat16)
    resid_f = resid.astype(jnp.float32)
    normed2 = rms_norm(resid_f, mlp_gain)
    gate_up = jnp.dot(normed2, w_gate_up.reshape(D, 2 * FF), preferred_element_type=jnp.float32)
    hidden = (jax.nn.silu(gate_up[:, :FF]) * gate_up[:, FF:]).astype(jnp.bfloat16)
    out_states = (resid_f + jnp.dot(hidden, w_down, preferred_element_type=jnp.float32)).astype(jnp.bfloat16)
    return (out_states, keys_new.reshape(REQ, ATTENTION_HEADS * HEAD_SIZE), values_new.reshape(REQ, ATTENTION_HEADS * HEAD_SIZE))
```

```python
import functools

import jax
import jax.numpy as jnp
from jax import lax
from jax.experimental import pallas as pl
from jax.experimental.pallas import tpu as pltpu
from jax.sharding import PartitionSpec as P

HEAD_SIZE = 64
WINDOW = 4096


NEG = -1e30
MESH_ID = pl.DeviceIdType.MESH


def rms_norm(values, gain):
    meansq = jnp.mean(values * values, axis=-1, keepdims=True)
    return (values * lax.rsqrt(meansq + 1e-05) * gain.astype(jnp.float32)).astype(jnp.bfloat16)


def rotary(tensor, cosine, sine):
    half = tensor.shape[-1] // 2
    turned = jnp.concatenate([-tensor[..., half:], tensor[..., :half]], axis=-1)
    return tensor * cosine + turned * sine


def undo_round(weights):
    rounded = lax.optimization_barrier(weights.astype(jnp.bfloat16))
    return rounded.astype(jnp.float32)


def _exchange_kernel(n, axis, gather, x_ref, y_ref, send_sem, recv_sem, local_sem):
    me = lax.axis_index(axis)
    barrier = pltpu.get_barrier_semaphore()

    def greet(d, carry):
        peer = lax.rem(me + d, n)
        pl.semaphore_signal(barrier, 1, device_id={axis: peer}, device_id_type=MESH_ID)
        return carry

    lax.fori_loop(1, n, greet, 0)
    pl.semaphore_wait(barrier, n - 1)

    def source(j):
        return x_ref if gather else x_ref.at[j]

    def outgoing(d):
        j = lax.rem(me + d, n)
        return pltpu.make_async_remote_copy(
            src_ref=source(j),
            dst_ref=y_ref.at[me],
            send_sem=send_sem.at[j],
            recv_sem=recv_sem.at[me],
            device_id={axis: j},
            device_id_type=MESH_ID,
        )

    def incoming(d):
        k = lax.rem(me + n - d, n)
        return pltpu.make_async_remote_copy(
            src_ref=source(k),
            dst_ref=y_ref.at[k],
            send_sem=send_sem.at[k],
            recv_sem=recv_sem.at[k],
            device_id={axis: k},
            device_id_type=MESH_ID,
        )

    local = pltpu.make_async_copy(source(me), y_ref.at[me], local_sem)
    local.start()

    def start(d, carry):
        outgoing(d).start()
        return carry

    lax.fori_loop(1, n, start, 0)

    def finish(d, carry):
        outgoing(d).wait_send()
        incoming(d).wait_recv()
        return carry

    lax.fori_loop(1, n, finish, 0)
    local.wait()


def exchange(x, axis, n, cid, gather=False):
    piece = x.shape if gather else x.shape[1:]
    return pl.pallas_call(
        functools.partial(_exchange_kernel, n, axis, gather),
        out_shape=jax.ShapeDtypeStruct((n,) + tuple(piece), x.dtype),
        in_specs=[pl.BlockSpec(memory_space=pl.ANY)],
        out_specs=pl.BlockSpec(memory_space=pl.ANY),
        scratch_shapes=[
            pltpu.SemaphoreType.DMA((n,)),
            pltpu.SemaphoreType.DMA((n,)),
            pltpu.SemaphoreType.DMA(()),
        ],
        compiler_params=pltpu.CompilerParams(collective_id=cid, has_side_effects=True),
    )(x)


def per_device(
    states,
    attn_gain,
    w_qkv,
    w_out,
    mlp_gain,
    w_gate_up,
    w_down,
    key_cache,
    value_cache,
    sink_keys,
    sink_values,
    cache_len,
    slot_mask,
    slot_pos,
    new_pos,
    tn,
    sn,
):
    rows = states.shape[0]
    width = states.shape[1]
    row_start = lax.axis_index("tensor") * rows
    floats = states.astype(jnp.float32)
    normed = rms_norm(floats, attn_gain)
    lanes = w_qkv.shape[2]
    heads_here = lanes // HEAD_SIZE
    qkv_matrix = w_qkv.reshape(width, 3 * lanes)
    normed_all = exchange(normed, "tensor", tn, 0, gather=True).reshape(tn * rows, width)
    projected = jnp.dot(normed_all, qkv_matrix, preferred_element_type=jnp.float32)
    batch = projected.shape[0]
    projected = projected.reshape(batch, 3, heads_here, HEAD_SIZE)
    half = HEAD_SIZE // 2
    inverse = jnp.exp(
        -jnp.log(jnp.float32(130000.0)) * jnp.arange(half, dtype=jnp.float32) * (2.0 / HEAD_SIZE)
    )
    angle = new_pos.astype(jnp.float32)[:, None] * inverse[None, :]
    angle = jnp.concatenate([angle, angle], axis=-1)[:, None, :]
    cosine = jnp.cos(angle)
    sine = jnp.sin(angle)
    queries_all = rotary(projected[:, 0], cosine, sine).astype(jnp.bfloat16)
    keys_all = rotary(projected[:, 1], cosine, sine).astype(jnp.bfloat16)
    values_all = projected[:, 2].astype(jnp.bfloat16)
    stacked = jnp.stack([queries_all, keys_all, values_all], axis=1)
    mine = exchange(stacked.reshape(tn, rows, 3, heads_here, HEAD_SIZE), "tensor", tn, 1)
    mine = jnp.transpose(mine, (1, 2, 0, 3, 4)).reshape(rows, 3, tn * heads_here, HEAD_SIZE)
    queries = mine[:, 0]
    keys_new = mine[:, 1]
    values_new = mine[:, 2]
    all_heads = queries.shape[1]
    own_len = lax.dynamic_slice_in_dim(cache_len, row_start, rows, 0)
    own_pos = lax.dynamic_slice_in_dim(new_pos, row_start, rows, 0)
    window_here = key_cache.shape[2]
    seq_index = lax.axis_index("seq")
    slots = seq_index * window_here + jnp.arange(window_here, dtype=jnp.int32)
    live = (slots[None, :] < own_len[:, None]) & (slot_mask == 1)
    live = live & (slot_pos < own_pos[:, None]) & (own_pos[:, None] - slot_pos < WINDOW)
    live = live[:, None, :]
    first_shard = seq_index == 0
    kwin = key_cache.reshape(rows, all_heads, HEAD_SIZE, window_here)
    vwin = value_cache.reshape(rows, all_heads, HEAD_SIZE, window_here)
    sink_key_rows = sink_keys.reshape(rows, all_heads, HEAD_SIZE, sink_keys.shape[2])
    vsink = sink_values.reshape(rows, all_heads, HEAD_SIZE, sink_values.shape[2])
    score_win = (
        jnp.einsum("bhd,bhds->bhs", queries, kwin, preferred_element_type=jnp.float32) * 0.125
    )
    score_win = jnp.where(live, score_win, NEG)
    score_sink = (
        jnp.einsum("bhd,bhds->bhs", queries, sink_key_rows, preferred_element_type=jnp.float32)
        * 0.125
    )
    score_sink = jnp.where(first_shard, score_sink, NEG)
    score_new = jnp.sum(queries.astype(jnp.float32) * keys_new.astype(jnp.float32), axis=-1) * 0.125
    score_new = jnp.where(first_shard, score_new, NEG)
    local_top = jnp.maximum(
        jnp.maximum(jnp.max(score_win, axis=-1), jnp.max(score_sink, axis=-1)), score_new
    )
    weight_win = jnp.where(live, jnp.exp(score_win - local_top[..., None]), 0.0)
    weight_sink = jnp.where(first_shard, jnp.exp(score_sink - local_top[..., None]), 0.0)
    weight_new = jnp.where(first_shard, jnp.exp(score_new - local_top), 0.0)
    total = jnp.sum(weight_win, axis=-1) + jnp.sum(weight_sink, axis=-1) + weight_new
    mixture = jnp.einsum(
        "bhs,bhds->bhd", weight_win.astype(jnp.bfloat16), vwin, preferred_element_type=jnp.float32
    )
    mixture = mixture + jnp.einsum(
        "bhs,bhds->bhd", weight_sink.astype(jnp.bfloat16), vsink, preferred_element_type=jnp.float32
    )
    mixture = mixture + undo_round(weight_new)[..., None] * values_new.astype(jnp.float32)
    packed = jnp.concatenate([mixture, total[..., None], local_top[..., None]], axis=-1)
    parts = exchange(packed, "seq", sn, 2, gather=True)
    part_top = parts[..., HEAD_SIZE + 1]
    top = jnp.max(part_top, axis=0)
    scale = jnp.exp(part_top - top[None])
    total = jnp.sum(parts[..., HEAD_SIZE] * scale, axis=0)
    mixture = jnp.sum(parts[..., :HEAD_SIZE] * scale[..., None], axis=0)
    attended_own = (mixture / total[..., None]).astype(jnp.bfloat16)
    to_send = jnp.transpose(attended_own.reshape(rows, tn, lanes), (1, 0, 2))
    attended = exchange(to_send, "tensor", tn, 3).reshape(batch, lanes)
    units = w_gate_up.shape[2]
    gate_matrix = w_gate_up.reshape(width, 2 * units)
    partial_out = jnp.dot(attended, w_out, preferred_element_type=jnp.float32).astype(jnp.bfloat16)
    pieces = exchange(partial_out.reshape(tn, rows, width), "tensor", tn, 4)
    projected_out = jnp.sum(pieces.astype(jnp.float32), axis=0)
    resid_part = (floats + projected_out).astype(jnp.bfloat16)
    normed2 = rms_norm(resid_part.astype(jnp.float32), mlp_gain)
    normed2_all = exchange(normed2, "tensor", tn, 5, gather=True).reshape(tn * rows, width)
    gate_up = jnp.dot(normed2_all, gate_matrix, preferred_element_type=jnp.float32)
    hidden = (jax.nn.silu(gate_up[:, :units]) * gate_up[:, units:]).astype(jnp.bfloat16)
    partial_down = jnp.dot(hidden, w_down, preferred_element_type=jnp.float32).astype(jnp.bfloat16)
    pieces = exchange(partial_down.reshape(tn, rows, width), "tensor", tn, 6)
    mlp_out = jnp.sum(pieces.astype(jnp.float32), axis=0)
    out_states = (resid_part.astype(jnp.float32) + mlp_out).astype(jnp.bfloat16)
    return (out_states, keys_all.reshape(batch, lanes), values_all.reshape(batch, lanes))


def solution(mesh):
    in_specs = (
        P("tensor", None),
        P(),
        P(None, None, "tensor"),
        P("tensor", None),
        P(),
        P(None, None, "tensor"),
        P("tensor", None),
        P("tensor", None, "seq"),
        P("tensor", None, "seq"),
        P("tensor", None, None),
        P("tensor", None, None),
        P(),
        P("tensor", "seq"),
        P("tensor", "seq"),
        P(),
    )
    out_specs = (P("tensor", None), P(None, "tensor"), P(None, "tensor"))
    body = functools.partial(per_device, tn=mesh.shape["tensor"], sn=mesh.shape["seq"])
    return jax.shard_map(
        body, mesh=mesh, in_specs=in_specs, out_specs=out_specs, check_vma=False
    )
```

```python
import functools

import jax
import jax.numpy as jnp
from jax import lax
from jax.experimental import pallas as pl
from jax.experimental.pallas import tpu as pltpu
from jax.sharding import PartitionSpec as P

HEAD_SIZE = 64
WINDOW = 4096


NEG = -1e30
MESH_ID = pl.DeviceIdType.MESH


def rms_norm(values, gain):
    meansq = jnp.mean(values * values, axis=-1, keepdims=True)
    return (values * lax.rsqrt(meansq + 1e-05) * gain.astype(jnp.float32)).astype(jnp.bfloat16)


def rotary(tensor, cosine, sine):
    half = tensor.shape[-1] // 2
    turned = jnp.concatenate([-tensor[..., half:], tensor[..., :half]], axis=-1)
    return tensor * cosine + turned * sine


def undo_round(weights):
    rounded = lax.optimization_barrier(weights.astype(jnp.bfloat16))
    return rounded.astype(jnp.float32)


def _exchange_kernel(n, axis, gather, x_ref, y_ref, send_sem, recv_sem, local_sem):
    me = lax.axis_index(axis)
    barrier = pltpu.get_barrier_semaphore()

    def greet(d, carry):
        peer = lax.rem(me + d, n)
        pl.semaphore_signal(barrier, 1, device_id={axis: peer}, device_id_type=MESH_ID)
        return carry

    lax.fori_loop(1, n, greet, 0)
    pl.semaphore_wait(barrier, n - 1)

    def source(j):
        return x_ref if gather else x_ref.at[j]

    def outgoing(d):
        j = lax.rem(me + d, n)
        return pltpu.make_async_remote_copy(
            src_ref=source(j),
            dst_ref=y_ref.at[me],
            send_sem=send_sem.at[j],
            recv_sem=recv_sem.at[me],
            device_id={axis: j},
            device_id_type=MESH_ID,
        )

    def incoming(d):
        k = lax.rem(me + n - d, n)
        return pltpu.make_async_remote_copy(
            src_ref=source(k),
            dst_ref=y_ref.at[k],
            send_sem=send_sem.at[k],
            recv_sem=recv_sem.at[k],
            device_id={axis: k},
            device_id_type=MESH_ID,
        )

    local = pltpu.make_async_copy(source(me), y_ref.at[me], local_sem)
    local.start()

    def start(d, carry):
        outgoing(d).start()
        return carry

    lax.fori_loop(1, n, start, 0)

    def finish(d, carry):
        outgoing(d).wait_send()
        incoming(d).wait_recv()
        return carry

    lax.fori_loop(1, n, finish, 0)
    local.wait()


def exchange(x, axis, n, cid, gather=False):
    piece = x.shape if gather else x.shape[1:]
    return pl.pallas_call(
        functools.partial(_exchange_kernel, n, axis, gather),
        out_shape=jax.ShapeDtypeStruct((n,) + tuple(piece), x.dtype),
        in_specs=[pl.BlockSpec(memory_space=pl.ANY)],
        out_specs=pl.BlockSpec(memory_space=pl.ANY),
        scratch_shapes=[
            pltpu.SemaphoreType.DMA((n,)),
            pltpu.SemaphoreType.DMA((n,)),
            pltpu.SemaphoreType.DMA(()),
        ],
        compiler_params=pltpu.CompilerParams(collective_id=cid, has_side_effects=True),
    )(x)


def _tail_kernel(
    n,
    att_ref,
    w_out_ref,
    states_ref,
    gain_ref,
    gate_ref,
    down_ref,
    out_ref,
    abuf,
    pbuf,
    rbuf,
    sbuf,
    nbuf,
    gbuf,
    qbuf,
    rbuf2,
    send_sem,
    recv_sem,
    local_sem,
):
    axis = "tensor"
    me = lax.axis_index(axis)
    rows = states_ref.shape[0]
    units = down_ref.shape[0]
    barrier = pltpu.get_barrier_semaphore()

    def greet(d, carry):
        pl.semaphore_signal(
            barrier, 1, device_id={axis: lax.rem(me + d, n)}, device_id_type=MESH_ID
        )
        return carry

    lax.fori_loop(1, n, greet, 0)
    pl.semaphore_wait(barrier, n - 1)

    def phase(p, src_of, dst_of):
        def outgoing(d):
            j = lax.rem(me + d, n)
            return pltpu.make_async_remote_copy(
                src_ref=src_of(j),
                dst_ref=dst_of(me),
                send_sem=send_sem.at[p, j],
                recv_sem=recv_sem.at[p, me],
                device_id={axis: j},
                device_id_type=MESH_ID,
            )

        def incoming(d):
            k = lax.rem(me + n - d, n)
            return pltpu.make_async_remote_copy(
                src_ref=src_of(k),
                dst_ref=dst_of(k),
                send_sem=send_sem.at[p, k],
                recv_sem=recv_sem.at[p, k],
                device_id={axis: k},
                device_id_type=MESH_ID,
            )

        local = pltpu.make_async_copy(src_of(me), dst_of(me), local_sem)
        local.start()

        def start(d, carry):
            outgoing(d).start()
            return carry

        lax.fori_loop(1, n, start, 0)

        def finish(d, carry):
            outgoing(d).wait_send()
            incoming(d).wait_recv()
            return carry

        lax.fori_loop(1, n, finish, 0)
        local.wait()

    def row_block(ref):
        return lambda i: ref.at[pl.ds(i * rows, rows)]

    phase(0, lambda j: att_ref.at[j], row_block(abuf))
    partial = jnp.dot(abuf[...], w_out_ref[...], preferred_element_type=jnp.float32)
    pbuf[...] = partial.astype(jnp.bfloat16)
    phase(1, row_block(pbuf), lambda k: rbuf.at[k])
    summed = jnp.sum(rbuf[...].astype(jnp.float32), axis=0)
    resid = (states_ref[...].astype(jnp.float32) + summed).astype(jnp.bfloat16)
    sbuf[...] = resid
    nbuf[...] = rms_norm(resid.astype(jnp.float32), gain_ref[...])
    phase(2, lambda j: nbuf, row_block(gbuf))
    gate_up = jnp.dot(gbuf[...], gate_ref[...], preferred_element_type=jnp.float32)
    hidden = (jax.nn.silu(gate_up[:, :units]) * gate_up[:, units:]).astype(jnp.bfloat16)
    down = jnp.dot(hidden, down_ref[...], preferred_element_type=jnp.float32)
    qbuf[...] = down.astype(jnp.bfloat16)
    phase(3, row_block(qbuf), lambda k: rbuf2.at[k])
    summed2 = jnp.sum(rbuf2[...].astype(jnp.float32), axis=0)
    out_ref[...] = (sbuf[...].astype(jnp.float32) + summed2).astype(out_ref.dtype)


def tail(att, w_out, states, gain, gate_matrix, w_down, n, cid):
    rows, width = states.shape
    lanes = att.shape[2]
    vmem = pl.BlockSpec(memory_space=pltpu.VMEM)
    return pl.pallas_call(
        functools.partial(_tail_kernel, n),
        out_shape=jax.ShapeDtypeStruct((rows, width), states.dtype),
        in_specs=[vmem] * 6,
        out_specs=vmem,
        scratch_shapes=[
            pltpu.VMEM((n * rows, lanes), jnp.bfloat16),
            pltpu.VMEM((n * rows, width), jnp.bfloat16),
            pltpu.VMEM((n, rows, width), jnp.bfloat16),
            pltpu.VMEM((rows, width), jnp.bfloat16),
            pltpu.VMEM((rows, width), jnp.bfloat16),
            pltpu.VMEM((n * rows, width), jnp.bfloat16),
            pltpu.VMEM((n * rows, width), jnp.bfloat16),
            pltpu.VMEM((n, rows, width), jnp.bfloat16),
            pltpu.SemaphoreType.DMA((4, n)),
            pltpu.SemaphoreType.DMA((4, n)),
            pltpu.SemaphoreType.DMA(()),
        ],
        compiler_params=pltpu.CompilerParams(collective_id=cid, has_side_effects=True),
    )(att, w_out, states, gain.reshape(1, width), gate_matrix, w_down)


def per_device(
    states,
    attn_gain,
    w_qkv,
    w_out,
    mlp_gain,
    w_gate_up,
    w_down,
    key_cache,
    value_cache,
    sink_keys,
    sink_values,
    cache_len,
    slot_mask,
    slot_pos,
    new_pos,
    tn,
    sn,
):
    rows = states.shape[0]
    width = states.shape[1]
    row_start = lax.axis_index("tensor") * rows
    floats = states.astype(jnp.float32)
    normed = rms_norm(floats, attn_gain)
    lanes = w_qkv.shape[2]
    heads_here = lanes // HEAD_SIZE
    qkv_matrix = w_qkv.reshape(width, 3 * lanes)
    normed_all = exchange(normed, "tensor", tn, 0, gather=True).reshape(tn * rows, width)
    projected = jnp.dot(normed_all, qkv_matrix, preferred_element_type=jnp.float32)
    batch = projected.shape[0]
    projected = projected.reshape(batch, 3, heads_here, HEAD_SIZE)
    half = HEAD_SIZE // 2
    inverse = jnp.exp(
        -jnp.log(jnp.float32(130000.0)) * jnp.arange(half, dtype=jnp.float32) * (2.0 / HEAD_SIZE)
    )
    angle = new_pos.astype(jnp.float32)[:, None] * inverse[None, :]
    angle = jnp.concatenate([angle, angle], axis=-1)[:, None, :]
    cosine = jnp.cos(angle)
    sine = jnp.sin(angle)
    queries_all = rotary(projected[:, 0], cosine, sine).astype(jnp.bfloat16)
    keys_all = rotary(projected[:, 1], cosine, sine).astype(jnp.bfloat16)
    values_all = projected[:, 2].astype(jnp.bfloat16)
    stacked = jnp.stack([queries_all, keys_all, values_all], axis=1)
    mine = exchange(stacked.reshape(tn, rows, 3, heads_here, HEAD_SIZE), "tensor", tn, 1)
    mine = jnp.transpose(mine, (1, 2, 0, 3, 4)).reshape(rows, 3, tn * heads_here, HEAD_SIZE)
    queries = mine[:, 0]
    keys_new = mine[:, 1]
    values_new = mine[:, 2]
    all_heads = queries.shape[1]
    own_len = lax.dynamic_slice_in_dim(cache_len, row_start, rows, 0)
    own_pos = lax.dynamic_slice_in_dim(new_pos, row_start, rows, 0)
    window_here = key_cache.shape[2]
    seq_index = lax.axis_index("seq")
    slots = seq_index * window_here + jnp.arange(window_here, dtype=jnp.int32)
    live = (slots[None, :] < own_len[:, None]) & (slot_mask == 1)
    live = live & (slot_pos < own_pos[:, None]) & (own_pos[:, None] - slot_pos < WINDOW)
    live = live[:, None, :]
    first_shard = seq_index == 0
    kwin = key_cache.reshape(rows, all_heads, HEAD_SIZE, window_here)
    vwin = value_cache.reshape(rows, all_heads, HEAD_SIZE, window_here)
    sink_key_rows = sink_keys.reshape(rows, all_heads, HEAD_SIZE, sink_keys.shape[2])
    vsink = sink_values.reshape(rows, all_heads, HEAD_SIZE, sink_values.shape[2])
    score_win = (
        jnp.einsum("bhd,bhds->bhs", queries, kwin, preferred_element_type=jnp.float32) * 0.125
    )
    score_win = jnp.where(live, score_win, NEG)
    score_sink = (
        jnp.einsum("bhd,bhds->bhs", queries, sink_key_rows, preferred_element_type=jnp.float32)
        * 0.125
    )
    score_sink = jnp.where(first_shard, score_sink, NEG)
    score_new = jnp.sum(queries.astype(jnp.float32) * keys_new.astype(jnp.float32), axis=-1) * 0.125
    score_new = jnp.where(first_shard, score_new, NEG)
    local_top = jnp.maximum(
        jnp.maximum(jnp.max(score_win, axis=-1), jnp.max(score_sink, axis=-1)), score_new
    )
    weight_win = jnp.where(live, jnp.exp(score_win - local_top[..., None]), 0.0)
    weight_sink = jnp.where(first_shard, jnp.exp(score_sink - local_top[..., None]), 0.0)
    weight_new = jnp.where(first_shard, jnp.exp(score_new - local_top), 0.0)
    total = jnp.sum(weight_win, axis=-1) + jnp.sum(weight_sink, axis=-1) + weight_new
    mixture = jnp.einsum(
        "bhs,bhds->bhd", weight_win.astype(jnp.bfloat16), vwin, preferred_element_type=jnp.float32
    )
    mixture = mixture + jnp.einsum(
        "bhs,bhds->bhd", weight_sink.astype(jnp.bfloat16), vsink, preferred_element_type=jnp.float32
    )
    mixture = mixture + undo_round(weight_new)[..., None] * values_new.astype(jnp.float32)
    packed = jnp.concatenate([mixture, total[..., None], local_top[..., None]], axis=-1)
    parts = exchange(packed, "seq", sn, 2, gather=True)
    part_top = parts[..., HEAD_SIZE + 1]
    top = jnp.max(part_top, axis=0)
    scale = jnp.exp(part_top - top[None])
    total = jnp.sum(parts[..., HEAD_SIZE] * scale, axis=0)
    mixture = jnp.sum(parts[..., :HEAD_SIZE] * scale[..., None], axis=0)
    attended_own = (mixture / total[..., None]).astype(jnp.bfloat16)
    to_send = jnp.transpose(attended_own.reshape(rows, tn, lanes), (1, 0, 2))
    units = w_gate_up.shape[2]
    gate_matrix = w_gate_up.reshape(width, 2 * units)
    out_states = tail(to_send, w_out, states, mlp_gain, gate_matrix, w_down, tn, 3)
    return (out_states, keys_all.reshape(batch, lanes), values_all.reshape(batch, lanes))


def solution(mesh):
    in_specs = (
        P("tensor", None),
        P(),
        P(None, None, "tensor"),
        P("tensor", None),
        P(),
        P(None, None, "tensor"),
        P("tensor", None),
        P("tensor", None, "seq"),
        P("tensor", None, "seq"),
        P("tensor", None, None),
        P("tensor", None, None),
        P(),
        P("tensor", "seq"),
        P("tensor", "seq"),
        P(),
    )
    out_specs = (P("tensor", None), P(None, "tensor"), P(None, "tensor"))
    body = functools.partial(per_device, tn=mesh.shape["tensor"], sn=mesh.shape["seq"])
    return jax.shard_map(
        body, mesh=mesh, in_specs=in_specs, out_specs=out_specs, check_vma=False
    )
```

```python
import functools

import jax
import jax.numpy as jnp
from jax import lax
from jax.experimental import pallas as pl
from jax.experimental.pallas import tpu as pltpu
from jax.sharding import PartitionSpec as P

HEAD_SIZE = 64
WINDOW = 4096


NEG = -1e30
MESH_ID = pl.DeviceIdType.MESH


def rms_norm(values, gain):
    meansq = jnp.mean(values * values, axis=-1, keepdims=True)
    return (values * lax.rsqrt(meansq + 1e-05) * gain.astype(jnp.float32)).astype(jnp.bfloat16)


def rotary(tensor, cosine, sine):
    half = tensor.shape[-1] // 2
    turned = jnp.concatenate([-tensor[..., half:], tensor[..., :half]], axis=-1)
    return tensor * cosine + turned * sine


def undo_round(weights):
    rounded = lax.optimization_barrier(weights.astype(jnp.bfloat16))
    return rounded.astype(jnp.float32)


def _exchange_kernel(n, axis, gather, x_ref, y_ref, send_sem, recv_sem, local_sem):
    me = lax.axis_index(axis)
    barrier = pltpu.get_barrier_semaphore()

    def greet(d, carry):
        peer = lax.rem(me + d, n)
        pl.semaphore_signal(barrier, 1, device_id={axis: peer}, device_id_type=MESH_ID)
        return carry

    lax.fori_loop(1, n, greet, 0)
    pl.semaphore_wait(barrier, n - 1)

    def source(j):
        return x_ref if gather else x_ref.at[j]

    def outgoing(d):
        j = lax.rem(me + d, n)
        return pltpu.make_async_remote_copy(
            src_ref=source(j),
            dst_ref=y_ref.at[me],
            send_sem=send_sem.at[j],
            recv_sem=recv_sem.at[me],
            device_id={axis: j},
            device_id_type=MESH_ID,
        )

    def incoming(d):
        k = lax.rem(me + n - d, n)
        return pltpu.make_async_remote_copy(
            src_ref=source(k),
            dst_ref=y_ref.at[k],
            send_sem=send_sem.at[k],
            recv_sem=recv_sem.at[k],
            device_id={axis: k},
            device_id_type=MESH_ID,
        )

    local = pltpu.make_async_copy(source(me), y_ref.at[me], local_sem)
    local.start()

    def start(d, carry):
        outgoing(d).start()
        return carry

    lax.fori_loop(1, n, start, 0)

    def finish(d, carry):
        outgoing(d).wait_send()
        incoming(d).wait_recv()
        return carry

    lax.fori_loop(1, n, finish, 0)
    local.wait()


def exchange(x, axis, n, cid, gather=False):
    piece = x.shape if gather else x.shape[1:]
    return pl.pallas_call(
        functools.partial(_exchange_kernel, n, axis, gather),
        out_shape=jax.ShapeDtypeStruct((n,) + tuple(piece), x.dtype),
        in_specs=[pl.BlockSpec(memory_space=pl.ANY)],
        out_specs=pl.BlockSpec(memory_space=pl.ANY),
        scratch_shapes=[
            pltpu.SemaphoreType.DMA((n,)),
            pltpu.SemaphoreType.DMA((n,)),
            pltpu.SemaphoreType.DMA(()),
        ],
        compiler_params=pltpu.CompilerParams(collective_id=cid, has_side_effects=True),
    )(x)


def _tail_kernel(
    n,
    sn,
    part_ref,
    w_out_ref,
    states_ref,
    gain_ref,
    gate_ref,
    down_ref,
    out_ref,
    seq_buf,
    att_buf,
    seq_send,
    seq_recv,
    abuf,
    pbuf,
    rbuf,
    sbuf,
    nbuf,
    gbuf,
    qbuf,
    rbuf2,
    send_sem,
    recv_sem,
    local_sem,
):
    axis = "tensor"
    me = lax.axis_index(axis)
    seq_me = lax.axis_index("seq")
    rows = states_ref.shape[0]
    barrier = pltpu.get_barrier_semaphore()

    def greet(d, carry):
        pl.semaphore_signal(
            barrier, 1, device_id={axis: lax.rem(me + d, n)}, device_id_type=MESH_ID
        )
        return carry

    lax.fori_loop(1, n, greet, 0)

    def greet_seq(d, carry):
        pl.semaphore_signal(
            barrier, 1, device_id={"seq": lax.rem(seq_me + d, sn)}, device_id_type=MESH_ID
        )
        return carry

    lax.fori_loop(1, sn, greet_seq, 0)
    pl.semaphore_wait(barrier, n - 1 + sn - 1)

    def seq_out(d):
        j = lax.rem(seq_me + d, sn)
        return pltpu.make_async_remote_copy(
            src_ref=part_ref,
            dst_ref=seq_buf.at[seq_me],
            send_sem=seq_send.at[j],
            recv_sem=seq_recv.at[seq_me],
            device_id={"seq": j},
            device_id_type=MESH_ID,
        )

    def seq_in(d):
        k = lax.rem(seq_me + sn - d, sn)
        return pltpu.make_async_remote_copy(
            src_ref=part_ref,
            dst_ref=seq_buf.at[k],
            send_sem=seq_send.at[k],
            recv_sem=seq_recv.at[k],
            device_id={"seq": k},
            device_id_type=MESH_ID,
        )

    seq_local = pltpu.make_async_copy(part_ref, seq_buf.at[seq_me], local_sem)
    seq_local.start()

    def seq_start(d, carry):
        seq_out(d).start()
        return carry

    lax.fori_loop(1, sn, seq_start, 0)

    def seq_finish(d, carry):
        seq_out(d).wait_send()
        seq_in(d).wait_recv()
        return carry

    lax.fori_loop(1, sn, seq_finish, 0)
    seq_local.wait()
    parts = seq_buf[...]
    lanes = att_buf.shape[2]
    part_top = parts[..., lanes + 1 : lanes + 2]
    top = jnp.max(part_top, axis=0)
    scale = jnp.exp(part_top - top[None])
    total = jnp.sum(parts[..., lanes : lanes + 1] * scale, axis=0)
    mixture = jnp.sum(parts[..., :lanes] * scale, axis=0)
    att_buf[...] = (mixture / total).astype(att_buf.dtype)
    units = down_ref.shape[0]

    def phase(p, src_of, dst_of):
        def outgoing(d):
            j = lax.rem(me + d, n)
            return pltpu.make_async_remote_copy(
                src_ref=src_of(j),
                dst_ref=dst_of(me),
                send_sem=send_sem.at[p, j],
                recv_sem=recv_sem.at[p, me],
                device_id={axis: j},
                device_id_type=MESH_ID,
            )

        def incoming(d):
            k = lax.rem(me + n - d, n)
            return pltpu.make_async_remote_copy(
                src_ref=src_of(k),
                dst_ref=dst_of(k),
                send_sem=send_sem.at[p, k],
                recv_sem=recv_sem.at[p, k],
                device_id={axis: k},
                device_id_type=MESH_ID,
            )

        local = pltpu.make_async_copy(src_of(me), dst_of(me), local_sem)
        local.start()

        def start(d, carry):
            outgoing(d).start()
            return carry

        lax.fori_loop(1, n, start, 0)

        def finish(d, carry):
            outgoing(d).wait_send()
            incoming(d).wait_recv()
            return carry

        lax.fori_loop(1, n, finish, 0)
        local.wait()

    def row_block(ref):
        return lambda i: ref.at[pl.ds(i * rows, rows)]

    phase(0, lambda j: att_buf.at[j], row_block(abuf))
    partial = jnp.dot(abuf[...], w_out_ref[...], preferred_element_type=jnp.float32)
    pbuf[...] = partial.astype(jnp.bfloat16)
    phase(1, row_block(pbuf), lambda k: rbuf.at[k])
    summed = jnp.sum(rbuf[...].astype(jnp.float32), axis=0)
    resid = (states_ref[...].astype(jnp.float32) + summed).astype(jnp.bfloat16)
    sbuf[...] = resid
    nbuf[...] = rms_norm(resid.astype(jnp.float32), gain_ref[...])
    phase(2, lambda j: nbuf, row_block(gbuf))
    gate_up = jnp.dot(gbuf[...], gate_ref[...], preferred_element_type=jnp.float32)
    hidden = (jax.nn.silu(gate_up[:, :units]) * gate_up[:, units:]).astype(jnp.bfloat16)
    down = jnp.dot(hidden, down_ref[...], preferred_element_type=jnp.float32)
    qbuf[...] = down.astype(jnp.bfloat16)
    phase(3, row_block(qbuf), lambda k: rbuf2.at[k])
    summed2 = jnp.sum(rbuf2[...].astype(jnp.float32), axis=0)
    out_ref[...] = (sbuf[...].astype(jnp.float32) + summed2).astype(out_ref.dtype)


def tail(part, w_out, states, gain, w_gate_up, w_down, n, sn, cid):
    rows, width = states.shape
    lanes = part.shape[2] - 2
    units = w_gate_up.shape[2]
    vmem = pl.BlockSpec(memory_space=pltpu.VMEM)
    return pl.pallas_call(
        functools.partial(_tail_kernel, n, sn),
        out_shape=jax.ShapeDtypeStruct((rows, width), states.dtype),
        in_specs=[vmem] * 6,
        out_specs=vmem,
        scratch_shapes=[
            pltpu.VMEM((sn,) + part.shape, jnp.float32),
            pltpu.VMEM((n, rows, lanes), jnp.bfloat16),
            pltpu.SemaphoreType.DMA((sn,)),
            pltpu.SemaphoreType.DMA((sn,)),
            pltpu.VMEM((n * rows, lanes), jnp.bfloat16),
            pltpu.VMEM((n * rows, width), jnp.bfloat16),
            pltpu.VMEM((n, rows, width), jnp.bfloat16),
            pltpu.VMEM((rows, width), jnp.bfloat16),
            pltpu.VMEM((rows, width), jnp.bfloat16),
            pltpu.VMEM((n * rows, width), jnp.bfloat16),
            pltpu.VMEM((n * rows, width), jnp.bfloat16),
            pltpu.VMEM((n, rows, width), jnp.bfloat16),
            pltpu.SemaphoreType.DMA((4, n)),
            pltpu.SemaphoreType.DMA((4, n)),
            pltpu.SemaphoreType.DMA(()),
        ],
        compiler_params=pltpu.CompilerParams(collective_id=cid, has_side_effects=True),
    )(part, w_out, states, gain.reshape(1, width), w_gate_up.reshape(width, 2 * units), w_down)


def per_device(
    states,
    attn_gain,
    w_qkv,
    w_out,
    mlp_gain,
    w_gate_up,
    w_down,
    key_cache,
    value_cache,
    sink_keys,
    sink_values,
    cache_len,
    slot_mask,
    slot_pos,
    new_pos,
    tn,
    sn,
):
    rows = states.shape[0]
    width = states.shape[1]
    row_start = lax.axis_index("tensor") * rows
    floats = states.astype(jnp.float32)
    normed = rms_norm(floats, attn_gain)
    lanes = w_qkv.shape[2]
    heads_here = lanes // HEAD_SIZE
    qkv_matrix = w_qkv.reshape(width, 3 * lanes)
    normed_all = exchange(normed, "tensor", tn, 0, gather=True).reshape(tn * rows, width)
    projected = jnp.dot(normed_all, qkv_matrix, preferred_element_type=jnp.float32)
    batch = projected.shape[0]
    projected = projected.reshape(batch, 3, heads_here, HEAD_SIZE)
    half = HEAD_SIZE // 2
    inverse = jnp.exp(
        -jnp.log(jnp.float32(130000.0)) * jnp.arange(half, dtype=jnp.float32) * (2.0 / HEAD_SIZE)
    )
    angle = new_pos.astype(jnp.float32)[:, None] * inverse[None, :]
    angle = jnp.concatenate([angle, angle], axis=-1)[:, None, :]
    cosine = jnp.cos(angle)
    sine = jnp.sin(angle)
    queries_all = rotary(projected[:, 0], cosine, sine).astype(jnp.bfloat16)
    keys_all = rotary(projected[:, 1], cosine, sine).astype(jnp.bfloat16)
    values_all = projected[:, 2].astype(jnp.bfloat16)
    stacked = jnp.stack([queries_all, keys_all, values_all], axis=1)
    mine = exchange(stacked.reshape(tn, rows, 3, heads_here, HEAD_SIZE), "tensor", tn, 1)
    mine = jnp.transpose(mine, (1, 2, 0, 3, 4)).reshape(rows, 3, tn * heads_here, HEAD_SIZE)
    queries = mine[:, 0]
    keys_new = mine[:, 1]
    values_new = mine[:, 2]
    all_heads = queries.shape[1]
    own_len = lax.dynamic_slice_in_dim(cache_len, row_start, rows, 0)
    own_pos = lax.dynamic_slice_in_dim(new_pos, row_start, rows, 0)
    window_here = key_cache.shape[2]
    seq_index = lax.axis_index("seq")
    slots = seq_index * window_here + jnp.arange(window_here, dtype=jnp.int32)
    live = (slots[None, :] < own_len[:, None]) & (slot_mask == 1)
    live = live & (slot_pos < own_pos[:, None]) & (own_pos[:, None] - slot_pos < WINDOW)
    live = live[:, None, :]
    first_shard = seq_index == 0
    kwin = key_cache.reshape(rows, all_heads, HEAD_SIZE, window_here)
    vwin = value_cache.reshape(rows, all_heads, HEAD_SIZE, window_here)
    sink_key_rows = sink_keys.reshape(rows, all_heads, HEAD_SIZE, sink_keys.shape[2])
    vsink = sink_values.reshape(rows, all_heads, HEAD_SIZE, sink_values.shape[2])
    score_win = (
        jnp.einsum("bhd,bhds->bhs", queries, kwin, preferred_element_type=jnp.float32) * 0.125
    )
    score_win = jnp.where(live, score_win, NEG)
    score_sink = (
        jnp.einsum("bhd,bhds->bhs", queries, sink_key_rows, preferred_element_type=jnp.float32)
        * 0.125
    )
    score_sink = jnp.where(first_shard, score_sink, NEG)
    score_new = jnp.sum(queries.astype(jnp.float32) * keys_new.astype(jnp.float32), axis=-1) * 0.125
    score_new = jnp.where(first_shard, score_new, NEG)
    local_top = jnp.maximum(
        jnp.maximum(jnp.max(score_win, axis=-1), jnp.max(score_sink, axis=-1)), score_new
    )
    weight_win = jnp.where(live, jnp.exp(score_win - local_top[..., None]), 0.0)
    weight_sink = jnp.where(first_shard, jnp.exp(score_sink - local_top[..., None]), 0.0)
    weight_new = jnp.where(first_shard, jnp.exp(score_new - local_top), 0.0)
    total = jnp.sum(weight_win, axis=-1) + jnp.sum(weight_sink, axis=-1) + weight_new
    mixture = jnp.einsum(
        "bhs,bhds->bhd", weight_win.astype(jnp.bfloat16), vwin, preferred_element_type=jnp.float32
    )
    mixture = mixture + jnp.einsum(
        "bhs,bhds->bhd", weight_sink.astype(jnp.bfloat16), vsink, preferred_element_type=jnp.float32
    )
    mixture = mixture + undo_round(weight_new)[..., None] * values_new.astype(jnp.float32)
    packed = jnp.concatenate([mixture, total[..., None], local_top[..., None]], axis=-1)
    packed = jnp.transpose(packed, (1, 0, 2))
    out_states = tail(packed, w_out, states, mlp_gain, w_gate_up, w_down, tn, sn, 3)
    return (out_states, keys_all.reshape(batch, lanes), values_all.reshape(batch, lanes))


def solution(mesh):
    in_specs = (
        P("tensor", None),
        P(),
        P(None, None, "tensor"),
        P("tensor", None),
        P(),
        P(None, None, "tensor"),
        P("tensor", None),
        P("tensor", None, "seq"),
        P("tensor", None, "seq"),
        P("tensor", None, None),
        P("tensor", None, None),
        P(),
        P("tensor", "seq"),
        P("tensor", "seq"),
        P(),
    )
    out_specs = (P("tensor", None), P(None, "tensor"), P(None, "tensor"))
    body = functools.partial(per_device, tn=mesh.shape["tensor"], sn=mesh.shape["seq"])
    return jax.shard_map(
        body, mesh=mesh, in_specs=in_specs, out_specs=out_specs, check_vma=False
    )
```

```python
import functools

import jax
import jax.numpy as jnp
from jax import lax
from jax.experimental import pallas as pl
from jax.experimental.pallas import tpu as pltpu
from jax.sharding import PartitionSpec as P

HEAD_SIZE = 64
WINDOW = 4096


NEG = -1e30
MESH_ID = pl.DeviceIdType.MESH


def rms_norm(values, gain):
    meansq = jnp.mean(values * values, axis=-1, keepdims=True)
    return (values * lax.rsqrt(meansq + 1e-05) * gain.astype(jnp.float32)).astype(jnp.bfloat16)


def rotary(tensor, cosine, sine):
    half = tensor.shape[-1] // 2
    turned = jnp.concatenate([-tensor[..., half:], tensor[..., :half]], axis=-1)
    return tensor * cosine + turned * sine


def undo_round(weights):
    rounded = lax.optimization_barrier(weights.astype(jnp.bfloat16))
    return rounded.astype(jnp.float32)


def _exchange_kernel(n, axis, gather, x_ref, y_ref, send_sem, recv_sem, local_sem):
    me = lax.axis_index(axis)
    barrier = pltpu.get_barrier_semaphore()

    def greet(d, carry):
        peer = lax.rem(me + d, n)
        pl.semaphore_signal(barrier, 1, device_id={axis: peer}, device_id_type=MESH_ID)
        return carry

    lax.fori_loop(1, n, greet, 0)
    pl.semaphore_wait(barrier, n - 1)

    def source(j):
        return x_ref if gather else x_ref.at[j]

    def outgoing(d):
        j = lax.rem(me + d, n)
        return pltpu.make_async_remote_copy(
            src_ref=source(j),
            dst_ref=y_ref.at[me],
            send_sem=send_sem.at[j],
            recv_sem=recv_sem.at[me],
            device_id={axis: j},
            device_id_type=MESH_ID,
        )

    def incoming(d):
        k = lax.rem(me + n - d, n)
        return pltpu.make_async_remote_copy(
            src_ref=source(k),
            dst_ref=y_ref.at[k],
            send_sem=send_sem.at[k],
            recv_sem=recv_sem.at[k],
            device_id={axis: k},
            device_id_type=MESH_ID,
        )

    local = pltpu.make_async_copy(source(me), y_ref.at[me], local_sem)
    local.start()

    def start(d, carry):
        outgoing(d).start()
        return carry

    lax.fori_loop(1, n, start, 0)

    def finish(d, carry):
        outgoing(d).wait_send()
        incoming(d).wait_recv()
        return carry

    lax.fori_loop(1, n, finish, 0)
    local.wait()


def exchange(x, axis, n, cid, gather=False):
    piece = x.shape if gather else x.shape[1:]
    return pl.pallas_call(
        functools.partial(_exchange_kernel, n, axis, gather),
        out_shape=jax.ShapeDtypeStruct((n,) + tuple(piece), x.dtype),
        in_specs=[pl.BlockSpec(memory_space=pl.ANY)],
        out_specs=pl.BlockSpec(memory_space=pl.ANY),
        scratch_shapes=[
            pltpu.SemaphoreType.DMA((n,)),
            pltpu.SemaphoreType.DMA((n,)),
            pltpu.SemaphoreType.DMA(()),
        ],
        compiler_params=pltpu.CompilerParams(collective_id=cid, has_side_effects=True),
    )(x)


def _tail_kernel(
    n,
    sn,
    part_ref,
    w_out_ref,
    states_ref,
    gain_ref,
    gate_ref,
    down_ref,
    out_ref,
    seq_buf,
    att_buf,
    seq_send,
    seq_recv,
    abuf,
    pbuf,
    rbuf,
    sbuf,
    nbuf,
    gbuf,
    qbuf,
    rbuf2,
    send_sem,
    recv_sem,
    local_sem,
):
    axis = "tensor"
    me = lax.axis_index(axis)
    seq_me = lax.axis_index("seq")
    rows = states_ref.shape[0]
    barrier = pltpu.get_barrier_semaphore()

    def greet(d, carry):
        pl.semaphore_signal(
            barrier, 1, device_id={axis: lax.rem(me + d, n)}, device_id_type=MESH_ID
        )
        return carry

    lax.fori_loop(1, n, greet, 0)

    def greet_seq(d, carry):
        pl.semaphore_signal(
            barrier, 1, device_id={"seq": lax.rem(seq_me + d, sn)}, device_id_type=MESH_ID
        )
        return carry

    lax.fori_loop(1, sn, greet_seq, 0)
    pl.semaphore_wait(barrier, n - 1 + sn - 1)

    def seq_out(d):
        j = lax.rem(seq_me + d, sn)
        return pltpu.make_async_remote_copy(
            src_ref=part_ref,
            dst_ref=seq_buf.at[seq_me],
            send_sem=seq_send.at[j],
            recv_sem=seq_recv.at[seq_me],
            device_id={"seq": j},
            device_id_type=MESH_ID,
        )

    def seq_in(d):
        k = lax.rem(seq_me + sn - d, sn)
        return pltpu.make_async_remote_copy(
            src_ref=part_ref,
            dst_ref=seq_buf.at[k],
            send_sem=seq_send.at[k],
            recv_sem=seq_recv.at[k],
            device_id={"seq": k},
            device_id_type=MESH_ID,
        )

    seq_local = pltpu.make_async_copy(part_ref, seq_buf.at[seq_me], local_sem)
    seq_local.start()

    def seq_start(d, carry):
        seq_out(d).start()
        return carry

    lax.fori_loop(1, sn, seq_start, 0)

    def seq_finish(d, carry):
        seq_out(d).wait_send()
        seq_in(d).wait_recv()
        return carry

    lax.fori_loop(1, sn, seq_finish, 0)
    seq_local.wait()
    parts = seq_buf[...]
    lanes = att_buf.shape[2]
    part_top = parts[..., lanes + 1 : lanes + 2]
    top = jnp.max(part_top, axis=0)
    scale = jnp.exp(part_top - top[None])
    total = jnp.sum(parts[..., lanes : lanes + 1] * scale, axis=0)
    mixture = jnp.sum(parts[..., :lanes] * scale, axis=0)
    att_buf[...] = (mixture / total).astype(att_buf.dtype)
    units = down_ref.shape[0]

    def phase(p, src_of, dst_of):
        def outgoing(d):
            j = lax.rem(me + d, n)
            return pltpu.make_async_remote_copy(
                src_ref=src_of(j),
                dst_ref=dst_of(me),
                send_sem=send_sem.at[p, j],
                recv_sem=recv_sem.at[p, me],
                device_id={axis: j},
                device_id_type=MESH_ID,
            )

        def incoming(d):
            k = lax.rem(me + n - d, n)
            return pltpu.make_async_remote_copy(
                src_ref=src_of(k),
                dst_ref=dst_of(k),
                send_sem=send_sem.at[p, k],
                recv_sem=recv_sem.at[p, k],
                device_id={axis: k},
                device_id_type=MESH_ID,
            )

        local = pltpu.make_async_copy(src_of(me), dst_of(me), local_sem)
        local.start()

        def start(d, carry):
            outgoing(d).start()
            return carry

        lax.fori_loop(1, n, start, 0)

        def finish(d, carry):
            outgoing(d).wait_send()
            incoming(d).wait_recv()
            return carry

        lax.fori_loop(1, n, finish, 0)
        local.wait()

    def row_block(ref):
        return lambda i: ref.at[pl.ds(i * rows, rows)]

    phase(0, lambda j: att_buf.at[j], row_block(abuf))
    partial = jnp.dot(abuf[...], w_out_ref[...], preferred_element_type=jnp.float32)
    pbuf[...] = partial.astype(jnp.bfloat16)
    phase(1, row_block(pbuf), lambda k: rbuf.at[k])
    summed = jnp.sum(rbuf[...].astype(jnp.float32), axis=0)
    resid = (states_ref[...].astype(jnp.float32) + summed).astype(jnp.bfloat16)
    sbuf[...] = resid
    nbuf[...] = rms_norm(resid.astype(jnp.float32), gain_ref[...])
    phase(2, lambda j: nbuf, row_block(gbuf))
    gate_up = jnp.dot(gbuf[...], gate_ref[...], preferred_element_type=jnp.float32)
    hidden = (jax.nn.silu(gate_up[:, :units]) * gate_up[:, units:]).astype(jnp.bfloat16)
    down = jnp.dot(hidden, down_ref[...], preferred_element_type=jnp.float32)
    qbuf[...] = down.astype(jnp.bfloat16)
    phase(3, row_block(qbuf), lambda k: rbuf2.at[k])
    summed2 = jnp.sum(rbuf2[...].astype(jnp.float32), axis=0)
    out_ref[...] = (sbuf[...].astype(jnp.float32) + summed2).astype(out_ref.dtype)


def tail(part, w_out, states, gain, w_gate_up, w_down, n, sn, cid):
    rows, width = states.shape
    lanes = part.shape[2] - 2
    units = w_gate_up.shape[2]
    vmem = pl.BlockSpec(memory_space=pltpu.VMEM)
    return pl.pallas_call(
        functools.partial(_tail_kernel, n, sn),
        out_shape=jax.ShapeDtypeStruct((rows, width), states.dtype),
        in_specs=[vmem] * 6,
        out_specs=vmem,
        scratch_shapes=[
            pltpu.VMEM((sn,) + part.shape, jnp.float32),
            pltpu.VMEM((n, rows, lanes), jnp.bfloat16),
            pltpu.SemaphoreType.DMA((sn,)),
            pltpu.SemaphoreType.DMA((sn,)),
            pltpu.VMEM((n * rows, lanes), jnp.bfloat16),
            pltpu.VMEM((n * rows, width), jnp.bfloat16),
            pltpu.VMEM((n, rows, width), jnp.bfloat16),
            pltpu.VMEM((rows, width), jnp.bfloat16),
            pltpu.VMEM((rows, width), jnp.bfloat16),
            pltpu.VMEM((n * rows, width), jnp.bfloat16),
            pltpu.VMEM((n * rows, width), jnp.bfloat16),
            pltpu.VMEM((n, rows, width), jnp.bfloat16),
            pltpu.SemaphoreType.DMA((4, n)),
            pltpu.SemaphoreType.DMA((4, n)),
            pltpu.SemaphoreType.DMA(()),
        ],
        compiler_params=pltpu.CompilerParams(collective_id=cid, has_side_effects=True),
    )(part, w_out, states, gain.reshape(1, width), w_gate_up.reshape(width, 2 * units), w_down)


def _head_kernel(n, x_ref, w_ref, trig_ref, qkv_ref, recv_ref, gbuf, send_sem, recv_sem, local_sem):
    axis = "tensor"
    me = lax.axis_index(axis)
    rows = x_ref.shape[0]
    block = qkv_ref.shape[1] // 2
    barrier = pltpu.get_barrier_semaphore()

    def greet(d, carry):
        pl.semaphore_signal(
            barrier, 1, device_id={axis: lax.rem(me + d, n)}, device_id_type=MESH_ID
        )
        return carry

    lax.fori_loop(1, n, greet, 0)
    pl.semaphore_wait(barrier, n - 1)

    def phase(p, src_of, dst_of):
        def outgoing(d):
            j = lax.rem(me + d, n)
            return pltpu.make_async_remote_copy(
                src_ref=src_of(j),
                dst_ref=dst_of(me),
                send_sem=send_sem.at[p, j],
                recv_sem=recv_sem.at[p, me],
                device_id={axis: j},
                device_id_type=MESH_ID,
            )

        def incoming(d):
            k = lax.rem(me + n - d, n)
            return pltpu.make_async_remote_copy(
                src_ref=src_of(k),
                dst_ref=dst_of(k),
                send_sem=send_sem.at[p, k],
                recv_sem=recv_sem.at[p, k],
                device_id={axis: k},
                device_id_type=MESH_ID,
            )

        local = pltpu.make_async_copy(src_of(me), dst_of(me), local_sem)
        local.start()

        def start(d, carry):
            outgoing(d).start()
            return carry

        lax.fori_loop(1, n, start, 0)

        def finish(d, carry):
            outgoing(d).wait_send()
            incoming(d).wait_recv()
            return carry

        lax.fori_loop(1, n, finish, 0)
        local.wait()

    phase(0, lambda j: x_ref, lambda k: gbuf.at[pl.ds(k * rows, rows)])
    proj = jnp.dot(gbuf[...], w_ref[...], preferred_element_type=jnp.float32)
    trig = trig_ref[...]
    turned = proj[:, :block] * trig[:, :block] + proj[:, block : 2 * block] * trig[:, block:]
    qkv_ref[:, :block] = turned.astype(qkv_ref.dtype)
    qkv_ref[:, block:] = proj[:, 2 * block :].astype(qkv_ref.dtype)
    phase(1, lambda j: qkv_ref.at[pl.ds(j * rows, rows)], lambda k: recv_ref.at[k])


def head(normed, w_ext, trig, n, cid):
    rows, width = normed.shape
    cols = w_ext.shape[1] // 3 * 2
    vmem = pl.BlockSpec(memory_space=pltpu.VMEM)
    return pl.pallas_call(
        functools.partial(_head_kernel, n),
        out_shape=(
            jax.ShapeDtypeStruct((n * rows, cols), jnp.bfloat16),
            jax.ShapeDtypeStruct((n, rows, cols), jnp.bfloat16),
        ),
        in_specs=[vmem] * 3,
        out_specs=(vmem, vmem),
        scratch_shapes=[
            pltpu.VMEM((n * rows, width), jnp.bfloat16),
            pltpu.SemaphoreType.DMA((2, n)),
            pltpu.SemaphoreType.DMA((2, n)),
            pltpu.SemaphoreType.DMA(()),
        ],
        compiler_params=pltpu.CompilerParams(collective_id=cid, has_side_effects=True),
    )(normed, w_ext, trig)


def per_device(
    states,
    attn_gain,
    w_qkv,
    w_out,
    mlp_gain,
    w_gate_up,
    w_down,
    key_cache,
    value_cache,
    sink_keys,
    sink_values,
    cache_len,
    slot_mask,
    slot_pos,
    new_pos,
    tn,
    sn,
):
    rows = states.shape[0]
    width = states.shape[1]
    row_start = lax.axis_index("tensor") * rows
    floats = states.astype(jnp.float32)
    normed = rms_norm(floats, attn_gain)
    lanes = w_qkv.shape[2]
    heads_here = lanes // HEAD_SIZE
    qkv_matrix = w_qkv.reshape(width, 3 * lanes)
    half = HEAD_SIZE // 2
    inverse = jnp.exp(
        -jnp.log(jnp.float32(130000.0)) * jnp.arange(half, dtype=jnp.float32) * (2.0 / HEAD_SIZE)
    )
    angle = new_pos.astype(jnp.float32)[:, None] * inverse[None, :]
    angle = jnp.concatenate([angle] * (4 * heads_here), axis=-1)
    trig = jnp.concatenate([jnp.cos(angle), jnp.sin(angle)], axis=-1)
    w_heads = w_qkv.reshape(width, 3, heads_here, HEAD_SIZE)
    w_turned = jnp.concatenate([-w_heads[..., half:], w_heads[..., :half]], axis=-1)
    w_ext = jnp.concatenate(
        [
            w_heads[:, 0:2].reshape(width, 2 * lanes),
            w_turned[:, 0:2].reshape(width, 2 * lanes),
            w_heads[:, 2].reshape(width, lanes),
            jnp.zeros((width, lanes), w_qkv.dtype),
        ],
        axis=-1,
    )
    qkv_all, mine = head(normed, w_ext, trig, tn, 0)
    batch = qkv_all.shape[0]
    keys_all = qkv_all[:, lanes : 2 * lanes]
    values_all = qkv_all[:, 2 * lanes : 3 * lanes]
    mine = mine.reshape(tn, rows, 4, heads_here, HEAD_SIZE)
    mine = jnp.transpose(mine, (1, 2, 0, 3, 4)).reshape(rows, 4, tn * heads_here, HEAD_SIZE)
    queries = mine[:, 0]
    keys_new = mine[:, 1]
    values_new = mine[:, 2]
    all_heads = queries.shape[1]
    own_len = lax.dynamic_slice_in_dim(cache_len, row_start, rows, 0)
    own_pos = lax.dynamic_slice_in_dim(new_pos, row_start, rows, 0)
    window_here = key_cache.shape[2]
    seq_index = lax.axis_index("seq")
    slots = seq_index * window_here + jnp.arange(window_here, dtype=jnp.int32)
    live = (slots[None, :] < own_len[:, None]) & (slot_mask == 1)
    live = live & (slot_pos < own_pos[:, None]) & (own_pos[:, None] - slot_pos < WINDOW)
    live = live[:, None, :]
    first_shard = seq_index == 0
    kwin = key_cache.reshape(rows, all_heads, HEAD_SIZE, window_here)
    vwin = value_cache.reshape(rows, all_heads, HEAD_SIZE, window_here)
    sink_key_rows = sink_keys.reshape(rows, all_heads, HEAD_SIZE, sink_keys.shape[2])
    vsink = sink_values.reshape(rows, all_heads, HEAD_SIZE, sink_values.shape[2])
    score_win = (
        jnp.einsum("bhd,bhds->bhs", queries, kwin, preferred_element_type=jnp.float32) * 0.125
    )
    score_win = jnp.where(live, score_win, NEG)
    score_sink = (
        jnp.einsum("bhd,bhds->bhs", queries, sink_key_rows, preferred_element_type=jnp.float32)
        * 0.125
    )
    score_sink = jnp.where(first_shard, score_sink, NEG)
    score_new = jnp.sum(queries.astype(jnp.float32) * keys_new.astype(jnp.float32), axis=-1) * 0.125
    score_new = jnp.where(first_shard, score_new, NEG)
    local_top = jnp.maximum(
        jnp.maximum(jnp.max(score_win, axis=-1), jnp.max(score_sink, axis=-1)), score_new
    )
    weight_win = jnp.where(live, jnp.exp(score_win - local_top[..., None]), 0.0)
    weight_sink = jnp.where(first_shard, jnp.exp(score_sink - local_top[..., None]), 0.0)
    weight_new = jnp.where(first_shard, jnp.exp(score_new - local_top), 0.0)
    total = jnp.sum(weight_win, axis=-1) + jnp.sum(weight_sink, axis=-1) + weight_new
    mixture = jnp.einsum(
        "bhs,bhds->bhd", weight_win.astype(jnp.bfloat16), vwin, preferred_element_type=jnp.float32
    )
    mixture = mixture + jnp.einsum(
        "bhs,bhds->bhd", weight_sink.astype(jnp.bfloat16), vsink, preferred_element_type=jnp.float32
    )
    mixture = mixture + undo_round(weight_new)[..., None] * values_new.astype(jnp.float32)
    packed = jnp.concatenate([mixture, total[..., None], local_top[..., None]], axis=-1)
    packed = jnp.transpose(packed, (1, 0, 2))
    out_states = tail(packed, w_out, states, mlp_gain, w_gate_up, w_down, tn, sn, 3)
    return (out_states, keys_all, values_all)


def solution(mesh):
    in_specs = (
        P("tensor", None),
        P(),
        P(None, None, "tensor"),
        P("tensor", None),
        P(),
        P(None, None, "tensor"),
        P("tensor", None),
        P("tensor", None, "seq"),
        P("tensor", None, "seq"),
        P("tensor", None, None),
        P("tensor", None, None),
        P(),
        P("tensor", "seq"),
        P("tensor", "seq"),
        P(),
    )
    out_specs = (P("tensor", None), P(None, "tensor"), P(None, "tensor"))
    body = functools.partial(per_device, tn=mesh.shape["tensor"], sn=mesh.shape["seq"])
    return jax.shard_map(
        body, mesh=mesh, in_specs=in_specs, out_specs=out_specs, check_vma=False
    )
```

```python
import functools

import jax
import jax.numpy as jnp
from jax import lax
from jax.experimental import pallas as pl
from jax.experimental.pallas import tpu as pltpu
from jax.sharding import PartitionSpec as P

HEAD_SIZE = 64
WINDOW = 4096


NEG = -1e30
MESH_ID = pl.DeviceIdType.MESH


def rms_norm(values, gain):
    meansq = jnp.mean(values * values, axis=-1, keepdims=True)
    return (values * lax.rsqrt(meansq + 1e-05) * gain.astype(jnp.float32)).astype(jnp.bfloat16)


def rotary(tensor, cosine, sine):
    half = tensor.shape[-1] // 2
    turned = jnp.concatenate([-tensor[..., half:], tensor[..., :half]], axis=-1)
    return tensor * cosine + turned * sine


def undo_round(weights):
    rounded = lax.optimization_barrier(weights.astype(jnp.bfloat16))
    return rounded.astype(jnp.float32)


def _exchange_kernel(n, axis, gather, x_ref, y_ref, send_sem, recv_sem, local_sem):
    me = lax.axis_index(axis)
    barrier = pltpu.get_barrier_semaphore()

    def greet(d, carry):
        peer = lax.rem(me + d, n)
        pl.semaphore_signal(barrier, 1, device_id={axis: peer}, device_id_type=MESH_ID)
        return carry

    lax.fori_loop(1, n, greet, 0)
    pl.semaphore_wait(barrier, n - 1)

    def source(j):
        return x_ref if gather else x_ref.at[j]

    def outgoing(d):
        j = lax.rem(me + d, n)
        return pltpu.make_async_remote_copy(
            src_ref=source(j),
            dst_ref=y_ref.at[me],
            send_sem=send_sem.at[j],
            recv_sem=recv_sem.at[me],
            device_id={axis: j},
            device_id_type=MESH_ID,
        )

    def incoming(d):
        k = lax.rem(me + n - d, n)
        return pltpu.make_async_remote_copy(
            src_ref=source(k),
            dst_ref=y_ref.at[k],
            send_sem=send_sem.at[k],
            recv_sem=recv_sem.at[k],
            device_id={axis: k},
            device_id_type=MESH_ID,
        )

    local = pltpu.make_async_copy(source(me), y_ref.at[me], local_sem)
    local.start()

    def start(d, carry):
        outgoing(d).start()
        return carry

    lax.fori_loop(1, n, start, 0)

    def finish(d, carry):
        outgoing(d).wait_send()
        incoming(d).wait_recv()
        return carry

    lax.fori_loop(1, n, finish, 0)
    local.wait()


def exchange(x, axis, n, cid, gather=False):
    piece = x.shape if gather else x.shape[1:]
    return pl.pallas_call(
        functools.partial(_exchange_kernel, n, axis, gather),
        out_shape=jax.ShapeDtypeStruct((n,) + tuple(piece), x.dtype),
        in_specs=[pl.BlockSpec(memory_space=pl.ANY)],
        out_specs=pl.BlockSpec(memory_space=pl.ANY),
        scratch_shapes=[
            pltpu.SemaphoreType.DMA((n,)),
            pltpu.SemaphoreType.DMA((n,)),
            pltpu.SemaphoreType.DMA(()),
        ],
        compiler_params=pltpu.CompilerParams(collective_id=cid, has_side_effects=True),
    )(x)


def _tail_kernel(
    n,
    sn,
    part_ref,
    w_out_ref,
    states_ref,
    gain_ref,
    gate_ref,
    down_ref,
    out_ref,
    seq_buf,
    att_buf,
    seq_send,
    seq_recv,
    abuf,
    pbuf,
    rbuf,
    sbuf,
    nbuf,
    gbuf,
    qbuf,
    rbuf2,
    send_sem,
    recv_sem,
    local_sem,
):
    axis = "tensor"
    me = lax.axis_index(axis)
    seq_me = lax.axis_index("seq")
    rows = states_ref.shape[0]
    barrier = pltpu.get_barrier_semaphore()

    def greet(d, carry):
        pl.semaphore_signal(
            barrier, 1, device_id={axis: lax.rem(me + d, n)}, device_id_type=MESH_ID
        )
        return carry

    lax.fori_loop(1, n, greet, 0)

    def greet_seq(d, carry):
        pl.semaphore_signal(
            barrier, 1, device_id={"seq": lax.rem(seq_me + d, sn)}, device_id_type=MESH_ID
        )
        return carry

    lax.fori_loop(1, sn, greet_seq, 0)
    pl.semaphore_wait(barrier, n - 1 + sn - 1)

    def seq_out(d):
        j = lax.rem(seq_me + d, sn)
        return pltpu.make_async_remote_copy(
            src_ref=part_ref,
            dst_ref=seq_buf.at[seq_me],
            send_sem=seq_send.at[j],
            recv_sem=seq_recv.at[seq_me],
            device_id={"seq": j},
            device_id_type=MESH_ID,
        )

    def seq_in(d):
        k = lax.rem(seq_me + sn - d, sn)
        return pltpu.make_async_remote_copy(
            src_ref=part_ref,
            dst_ref=seq_buf.at[k],
            send_sem=seq_send.at[k],
            recv_sem=seq_recv.at[k],
            device_id={"seq": k},
            device_id_type=MESH_ID,
        )

    seq_local = pltpu.make_async_copy(part_ref, seq_buf.at[seq_me], local_sem)
    seq_local.start()

    def seq_start(d, carry):
        seq_out(d).start()
        return carry

    lax.fori_loop(1, sn, seq_start, 0)

    def seq_finish(d, carry):
        seq_out(d).wait_send()
        seq_in(d).wait_recv()
        return carry

    lax.fori_loop(1, sn, seq_finish, 0)
    seq_local.wait()
    parts = seq_buf[...]
    lanes = att_buf.shape[2]
    part_top = parts[..., lanes + 1 : lanes + 2]
    top = jnp.max(part_top, axis=0)
    scale = jnp.exp(part_top - top[None])
    total = jnp.sum(parts[..., lanes : lanes + 1] * scale, axis=0)
    mixture = jnp.sum(parts[..., :lanes] * scale, axis=0)
    att_buf[...] = (mixture / total).astype(att_buf.dtype)
    units = down_ref.shape[0]

    def phase(p, src_of, dst_of):
        def outgoing(d):
            j = lax.rem(me + d, n)
            return pltpu.make_async_remote_copy(
                src_ref=src_of(j),
                dst_ref=dst_of(me),
                send_sem=send_sem.at[p, j],
                recv_sem=recv_sem.at[p, me],
                device_id={axis: j},
                device_id_type=MESH_ID,
            )

        def incoming(d):
            k = lax.rem(me + n - d, n)
            return pltpu.make_async_remote_copy(
                src_ref=src_of(k),
                dst_ref=dst_of(k),
                send_sem=send_sem.at[p, k],
                recv_sem=recv_sem.at[p, k],
                device_id={axis: k},
                device_id_type=MESH_ID,
            )

        local = pltpu.make_async_copy(src_of(me), dst_of(me), local_sem)
        local.start()

        def start(d, carry):
            outgoing(d).start()
            return carry

        lax.fori_loop(1, n, start, 0)

        def finish(d, carry):
            outgoing(d).wait_send()
            incoming(d).wait_recv()
            return carry

        lax.fori_loop(1, n, finish, 0)
        local.wait()

    def row_block(ref):
        return lambda i: ref.at[pl.ds(i * rows, rows)]

    phase(0, lambda j: att_buf.at[j], row_block(abuf))
    partial = jnp.dot(abuf[...], w_out_ref[...], preferred_element_type=jnp.float32)
    pbuf[...] = partial.astype(jnp.bfloat16)
    phase(1, row_block(pbuf), lambda k: rbuf.at[k])
    summed = jnp.sum(rbuf[...].astype(jnp.float32), axis=0)
    resid = (states_ref[...].astype(jnp.float32) + summed).astype(jnp.bfloat16)
    sbuf[...] = resid
    nbuf[...] = rms_norm(resid.astype(jnp.float32), gain_ref[...])
    phase(2, lambda j: nbuf, row_block(gbuf))
    gate_up = jnp.dot(gbuf[...], gate_ref[...], preferred_element_type=jnp.float32)
    hidden = (jax.nn.silu(gate_up[:, :units]) * gate_up[:, units:]).astype(jnp.bfloat16)
    down = jnp.dot(hidden, down_ref[...], preferred_element_type=jnp.float32)
    qbuf[...] = down.astype(jnp.bfloat16)
    phase(3, row_block(qbuf), lambda k: rbuf2.at[k])
    summed2 = jnp.sum(rbuf2[...].astype(jnp.float32), axis=0)
    out_ref[...] = (sbuf[...].astype(jnp.float32) + summed2).astype(out_ref.dtype)


def tail(part, w_out, states, gain, w_gate_up, w_down, n, sn, cid):
    rows, width = states.shape
    lanes = part.shape[2] - 2
    units = w_gate_up.shape[2]
    vmem = pl.BlockSpec(memory_space=pltpu.VMEM)
    return pl.pallas_call(
        functools.partial(_tail_kernel, n, sn),
        out_shape=jax.ShapeDtypeStruct((rows, width), states.dtype),
        in_specs=[vmem] * 6,
        out_specs=vmem,
        scratch_shapes=[
            pltpu.VMEM((sn,) + part.shape, jnp.float32),
            pltpu.VMEM((n, rows, lanes), jnp.bfloat16),
            pltpu.SemaphoreType.DMA((sn,)),
            pltpu.SemaphoreType.DMA((sn,)),
            pltpu.VMEM((n * rows, lanes), jnp.bfloat16),
            pltpu.VMEM((n * rows, width), jnp.bfloat16),
            pltpu.VMEM((n, rows, width), jnp.bfloat16),
            pltpu.VMEM((rows, width), jnp.bfloat16),
            pltpu.VMEM((rows, width), jnp.bfloat16),
            pltpu.VMEM((n * rows, width), jnp.bfloat16),
            pltpu.VMEM((n * rows, width), jnp.bfloat16),
            pltpu.VMEM((n, rows, width), jnp.bfloat16),
            pltpu.SemaphoreType.DMA((4, n)),
            pltpu.SemaphoreType.DMA((4, n)),
            pltpu.SemaphoreType.DMA(()),
        ],
        compiler_params=pltpu.CompilerParams(collective_id=cid, has_side_effects=True),
    )(part, w_out, states, gain.reshape(1, width), w_gate_up.reshape(width, 2 * units), w_down)


def _head_kernel(n, x_ref, w_ref, trig_ref, qkv_ref, recv_ref, gbuf, send_sem, recv_sem, local_sem):
    axis = "tensor"
    me = lax.axis_index(axis)
    rows = x_ref.shape[0]
    block = qkv_ref.shape[1] // 2
    barrier = pltpu.get_barrier_semaphore()

    def greet(d, carry):
        pl.semaphore_signal(
            barrier, 1, device_id={axis: lax.rem(me + d, n)}, device_id_type=MESH_ID
        )
        return carry

    lax.fori_loop(1, n, greet, 0)
    pl.semaphore_wait(barrier, n - 1)

    def phase(p, src_of, dst_of):
        def outgoing(d):
            j = lax.rem(me + d, n)
            return pltpu.make_async_remote_copy(
                src_ref=src_of(j),
                dst_ref=dst_of(me),
                send_sem=send_sem.at[p, j],
                recv_sem=recv_sem.at[p, me],
                device_id={axis: j},
                device_id_type=MESH_ID,
            )

        def incoming(d):
            k = lax.rem(me + n - d, n)
            return pltpu.make_async_remote_copy(
                src_ref=src_of(k),
                dst_ref=dst_of(k),
                send_sem=send_sem.at[p, k],
                recv_sem=recv_sem.at[p, k],
                device_id={axis: k},
                device_id_type=MESH_ID,
            )

        local = pltpu.make_async_copy(src_of(me), dst_of(me), local_sem)
        local.start()

        def start(d, carry):
            outgoing(d).start()
            return carry

        lax.fori_loop(1, n, start, 0)

        def finish(d, carry):
            outgoing(d).wait_send()
            incoming(d).wait_recv()
            return carry

        lax.fori_loop(1, n, finish, 0)
        local.wait()

    phase(0, lambda j: x_ref, lambda k: gbuf.at[pl.ds(k * rows, rows)])
    proj = jnp.dot(gbuf[...], w_ref[...], preferred_element_type=jnp.float32)
    trig = trig_ref[...]
    pair = proj[:, :block]
    half = HEAD_SIZE // 2
    lane = lax.broadcasted_iota(jnp.int32, pair.shape, 1)
    turned = jnp.where(
        lane % HEAD_SIZE < half,
        -pltpu.roll(pair, block - half, 1),
        pltpu.roll(pair, half, 1),
    )
    rotated = pair * trig[:, :block] + turned * trig[:, block:]
    qkv_ref[:, :block] = rotated.astype(qkv_ref.dtype)
    qkv_ref[:, block : block + block // 2] = proj[:, block:].astype(qkv_ref.dtype)
    qkv_ref[:, block + block // 2 :] = jnp.zeros((pair.shape[0], block // 2), qkv_ref.dtype)
    phase(1, lambda j: qkv_ref.at[pl.ds(j * rows, rows)], lambda k: recv_ref.at[k])


def head(normed, w_ext, trig, n, cid):
    rows, width = normed.shape
    cols = w_ext.shape[1] // 3 * 4
    vmem = pl.BlockSpec(memory_space=pltpu.VMEM)
    return pl.pallas_call(
        functools.partial(_head_kernel, n),
        out_shape=(
            jax.ShapeDtypeStruct((n * rows, cols), jnp.bfloat16),
            jax.ShapeDtypeStruct((n, rows, cols), jnp.bfloat16),
        ),
        in_specs=[vmem] * 3,
        out_specs=(vmem, vmem),
        scratch_shapes=[
            pltpu.VMEM((n * rows, width), jnp.bfloat16),
            pltpu.SemaphoreType.DMA((2, n)),
            pltpu.SemaphoreType.DMA((2, n)),
            pltpu.SemaphoreType.DMA(()),
        ],
        compiler_params=pltpu.CompilerParams(collective_id=cid, has_side_effects=True),
    )(normed, w_ext, trig)


def per_device(
    states,
    attn_gain,
    w_qkv,
    w_out,
    mlp_gain,
    w_gate_up,
    w_down,
    key_cache,
    value_cache,
    sink_keys,
    sink_values,
    cache_len,
    slot_mask,
    slot_pos,
    new_pos,
    tn,
    sn,
):
    rows = states.shape[0]
    width = states.shape[1]
    row_start = lax.axis_index("tensor") * rows
    floats = states.astype(jnp.float32)
    normed = rms_norm(floats, attn_gain)
    lanes = w_qkv.shape[2]
    heads_here = lanes // HEAD_SIZE
    qkv_matrix = w_qkv.reshape(width, 3 * lanes)
    half = HEAD_SIZE // 2
    inverse = jnp.exp(
        -jnp.log(jnp.float32(130000.0)) * jnp.arange(half, dtype=jnp.float32) * (2.0 / HEAD_SIZE)
    )
    angle = new_pos.astype(jnp.float32)[:, None] * inverse[None, :]
    angle = jnp.concatenate([angle] * (4 * heads_here), axis=-1)
    trig = jnp.concatenate([jnp.cos(angle), jnp.sin(angle)], axis=-1)
    qkv_all, mine = head(normed, qkv_matrix, trig, tn, 0)
    batch = qkv_all.shape[0]
    keys_all = qkv_all[:, lanes : 2 * lanes]
    values_all = qkv_all[:, 2 * lanes : 3 * lanes]
    mine = mine.reshape(tn, rows, 4, heads_here, HEAD_SIZE)
    mine = jnp.transpose(mine, (1, 2, 0, 3, 4)).reshape(rows, 4, tn * heads_here, HEAD_SIZE)
    queries = mine[:, 0]
    keys_new = mine[:, 1]
    values_new = mine[:, 2]
    all_heads = queries.shape[1]
    own_len = lax.dynamic_slice_in_dim(cache_len, row_start, rows, 0)
    own_pos = lax.dynamic_slice_in_dim(new_pos, row_start, rows, 0)
    window_here = key_cache.shape[2]
    seq_index = lax.axis_index("seq")
    slots = seq_index * window_here + jnp.arange(window_here, dtype=jnp.int32)
    live = (slots[None, :] < own_len[:, None]) & (slot_mask == 1)
    live = live & (slot_pos < own_pos[:, None]) & (own_pos[:, None] - slot_pos < WINDOW)
    live = live[:, None, :]
    first_shard = seq_index == 0
    kwin = key_cache.reshape(rows, all_heads, HEAD_SIZE, window_here)
    vwin = value_cache.reshape(rows, all_heads, HEAD_SIZE, window_here)
    sink_key_rows = sink_keys.reshape(rows, all_heads, HEAD_SIZE, sink_keys.shape[2])
    vsink = sink_values.reshape(rows, all_heads, HEAD_SIZE, sink_values.shape[2])
    score_win = (
        jnp.einsum("bhd,bhds->bhs", queries, kwin, preferred_element_type=jnp.float32) * 0.125
    )
    score_win = jnp.where(live, score_win, NEG)
    score_sink = (
        jnp.einsum("bhd,bhds->bhs", queries, sink_key_rows, preferred_element_type=jnp.float32)
        * 0.125
    )
    score_sink = jnp.where(first_shard, score_sink, NEG)
    score_new = jnp.sum(queries.astype(jnp.float32) * keys_new.astype(jnp.float32), axis=-1) * 0.125
    score_new = jnp.where(first_shard, score_new, NEG)
    local_top = jnp.maximum(
        jnp.maximum(jnp.max(score_win, axis=-1), jnp.max(score_sink, axis=-1)), score_new
    )
    weight_win = jnp.where(live, jnp.exp(score_win - local_top[..., None]), 0.0)
    weight_sink = jnp.where(first_shard, jnp.exp(score_sink - local_top[..., None]), 0.0)
    weight_new = jnp.where(first_shard, jnp.exp(score_new - local_top), 0.0)
    total = jnp.sum(weight_win, axis=-1) + jnp.sum(weight_sink, axis=-1) + weight_new
    mixture = jnp.einsum(
        "bhs,bhds->bhd", weight_win.astype(jnp.bfloat16), vwin, preferred_element_type=jnp.float32
    )
    mixture = mixture + jnp.einsum(
        "bhs,bhds->bhd", weight_sink.astype(jnp.bfloat16), vsink, preferred_element_type=jnp.float32
    )
    mixture = mixture + undo_round(weight_new)[..., None] * values_new.astype(jnp.float32)
    packed = jnp.concatenate([mixture, total[..., None], local_top[..., None]], axis=-1)
    packed = jnp.transpose(packed, (1, 0, 2))
    out_states = tail(packed, w_out, states, mlp_gain, w_gate_up, w_down, tn, sn, 3)
    return (out_states, keys_all, values_all)


def solution(mesh):
    in_specs = (
        P("tensor", None),
        P(),
        P(None, None, "tensor"),
        P("tensor", None),
        P(),
        P(None, None, "tensor"),
        P("tensor", None),
        P("tensor", None, "seq"),
        P("tensor", None, "seq"),
        P("tensor", None, None),
        P("tensor", None, None),
        P(),
        P("tensor", "seq"),
        P("tensor", "seq"),
        P(),
    )
    out_specs = (P("tensor", None), P(None, "tensor"), P(None, "tensor"))
    body = functools.partial(per_device, tn=mesh.shape["tensor"], sn=mesh.shape["seq"])
    return jax.shard_map(
        body, mesh=mesh, in_specs=in_specs, out_specs=out_specs, check_vma=False
    )
```

```python
import functools

import jax
import jax.numpy as jnp
from jax import lax
from jax.experimental import pallas as pl
from jax.experimental.pallas import tpu as pltpu
from jax.sharding import PartitionSpec as P

HEAD_SIZE = 64
WINDOW = 4096


NEG = -1e30
MESH_ID = pl.DeviceIdType.MESH


def rms_norm(values, gain):
    meansq = jnp.mean(values * values, axis=-1, keepdims=True)
    return (values * lax.rsqrt(meansq + 1e-05) * gain.astype(jnp.float32)).astype(jnp.bfloat16)


def rotary(tensor, cosine, sine):
    half = tensor.shape[-1] // 2
    turned = jnp.concatenate([-tensor[..., half:], tensor[..., :half]], axis=-1)
    return tensor * cosine + turned * sine


def undo_round(weights):
    rounded = lax.optimization_barrier(weights.astype(jnp.bfloat16))
    return rounded.astype(jnp.float32)


def _exchange_kernel(n, axis, gather, x_ref, y_ref, send_sem, recv_sem, local_sem):
    me = lax.axis_index(axis)
    barrier = pltpu.get_barrier_semaphore()

    def greet(d, carry):
        peer = lax.rem(me + d, n)
        pl.semaphore_signal(barrier, 1, device_id={axis: peer}, device_id_type=MESH_ID)
        return carry

    lax.fori_loop(1, n, greet, 0)
    pl.semaphore_wait(barrier, n - 1)

    def source(j):
        return x_ref if gather else x_ref.at[j]

    def outgoing(d):
        j = lax.rem(me + d, n)
        return pltpu.make_async_remote_copy(
            src_ref=source(j),
            dst_ref=y_ref.at[me],
            send_sem=send_sem.at[j],
            recv_sem=recv_sem.at[me],
            device_id={axis: j},
            device_id_type=MESH_ID,
        )

    def incoming(d):
        k = lax.rem(me + n - d, n)
        return pltpu.make_async_remote_copy(
            src_ref=source(k),
            dst_ref=y_ref.at[k],
            send_sem=send_sem.at[k],
            recv_sem=recv_sem.at[k],
            device_id={axis: k},
            device_id_type=MESH_ID,
        )

    local = pltpu.make_async_copy(source(me), y_ref.at[me], local_sem)
    local.start()

    def start(d, carry):
        outgoing(d).start()
        return carry

    lax.fori_loop(1, n, start, 0)

    def finish(d, carry):
        outgoing(d).wait_send()
        incoming(d).wait_recv()
        return carry

    lax.fori_loop(1, n, finish, 0)
    local.wait()


def exchange(x, axis, n, cid, gather=False):
    piece = x.shape if gather else x.shape[1:]
    return pl.pallas_call(
        functools.partial(_exchange_kernel, n, axis, gather),
        out_shape=jax.ShapeDtypeStruct((n,) + tuple(piece), x.dtype),
        in_specs=[pl.BlockSpec(memory_space=pl.ANY)],
        out_specs=pl.BlockSpec(memory_space=pl.ANY),
        scratch_shapes=[
            pltpu.SemaphoreType.DMA((n,)),
            pltpu.SemaphoreType.DMA((n,)),
            pltpu.SemaphoreType.DMA(()),
        ],
        compiler_params=pltpu.CompilerParams(collective_id=cid, has_side_effects=True),
    )(x)


def _tail_kernel(
    n,
    sn,
    part_ref,
    w_out_ref,
    states_ref,
    gain_ref,
    gate_ref,
    down_ref,
    out_ref,
    seq_buf,
    att_buf,
    seq_send,
    seq_recv,
    abuf,
    pbuf,
    rbuf,
    sbuf,
    nbuf,
    gbuf,
    qbuf,
    rbuf2,
    send_sem,
    recv_sem,
    local_sem,
):
    axis = "tensor"
    me = lax.axis_index(axis)
    seq_me = lax.axis_index("seq")
    rows = states_ref.shape[0]
    barrier = pltpu.get_barrier_semaphore()

    def greet(d, carry):
        pl.semaphore_signal(
            barrier, 1, device_id={axis: lax.rem(me + d, n)}, device_id_type=MESH_ID
        )
        return carry

    lax.fori_loop(1, n, greet, 0)

    def greet_seq(d, carry):
        pl.semaphore_signal(
            barrier, 1, device_id={"seq": lax.rem(seq_me + d, sn)}, device_id_type=MESH_ID
        )
        return carry

    lax.fori_loop(1, sn, greet_seq, 0)
    pl.semaphore_wait(barrier, n - 1 + sn - 1)

    def seq_out(d):
        j = lax.rem(seq_me + d, sn)
        return pltpu.make_async_remote_copy(
            src_ref=part_ref,
            dst_ref=seq_buf.at[seq_me],
            send_sem=seq_send.at[j],
            recv_sem=seq_recv.at[seq_me],
            device_id={"seq": j},
            device_id_type=MESH_ID,
        )

    def seq_in(d):
        k = lax.rem(seq_me + sn - d, sn)
        return pltpu.make_async_remote_copy(
            src_ref=part_ref,
            dst_ref=seq_buf.at[k],
            send_sem=seq_send.at[k],
            recv_sem=seq_recv.at[k],
            device_id={"seq": k},
            device_id_type=MESH_ID,
        )

    seq_local = pltpu.make_async_copy(part_ref, seq_buf.at[seq_me], local_sem)
    seq_local.start()

    def seq_start(d, carry):
        seq_out(d).start()
        return carry

    lax.fori_loop(1, sn, seq_start, 0)

    def seq_finish(d, carry):
        seq_out(d).wait_send()
        seq_in(d).wait_recv()
        return carry

    lax.fori_loop(1, sn, seq_finish, 0)
    seq_local.wait()
    parts = seq_buf[...]
    lanes = att_buf.shape[2]
    part_top = parts[..., lanes + 1 : lanes + 2]
    top = jnp.max(part_top, axis=0)
    scale = jnp.exp(part_top - top[None])
    total = jnp.sum(parts[..., lanes : lanes + 1] * scale, axis=0)
    mixture = jnp.sum(parts[..., :lanes] * scale, axis=0)
    att_buf[...] = (mixture / total).astype(att_buf.dtype)
    units = down_ref.shape[0]

    def phase(p, src_of, dst_of):
        def outgoing(d):
            j = lax.rem(me + d, n)
            return pltpu.make_async_remote_copy(
                src_ref=src_of(j),
                dst_ref=dst_of(me),
                send_sem=send_sem.at[p, j],
                recv_sem=recv_sem.at[p, me],
                device_id={axis: j},
                device_id_type=MESH_ID,
            )

        def incoming(d):
            k = lax.rem(me + n - d, n)
            return pltpu.make_async_remote_copy(
                src_ref=src_of(k),
                dst_ref=dst_of(k),
                send_sem=send_sem.at[p, k],
                recv_sem=recv_sem.at[p, k],
                device_id={axis: k},
                device_id_type=MESH_ID,
            )

        local = pltpu.make_async_copy(src_of(me), dst_of(me), local_sem)
        local.start()

        def start(d, carry):
            outgoing(d).start()
            return carry

        lax.fori_loop(1, n, start, 0)

        def finish(d, carry):
            outgoing(d).wait_send()
            incoming(d).wait_recv()
            return carry

        lax.fori_loop(1, n, finish, 0)
        local.wait()

    def row_block(ref):
        return lambda i: ref.at[pl.ds(i * rows, rows)]

    phase(0, lambda j: att_buf.at[j], row_block(abuf))
    partial = jnp.dot(abuf[...], w_out_ref[...], preferred_element_type=jnp.float32)
    pbuf[...] = partial.astype(jnp.bfloat16)
    phase(1, row_block(pbuf), lambda k: rbuf.at[k])
    summed = jnp.sum(rbuf[...].astype(jnp.float32), axis=0)
    resid = (states_ref[...].astype(jnp.float32) + summed).astype(jnp.bfloat16)
    sbuf[...] = resid
    nbuf[...] = rms_norm(resid.astype(jnp.float32), gain_ref[1:2, :])
    phase(2, lambda j: nbuf, row_block(gbuf))
    gate_up = jnp.dot(gbuf[...], gate_ref[...], preferred_element_type=jnp.float32)
    hidden = (jax.nn.silu(gate_up[:, :units]) * gate_up[:, units:]).astype(jnp.bfloat16)
    down = jnp.dot(hidden, down_ref[...], preferred_element_type=jnp.float32)
    qbuf[...] = down.astype(jnp.bfloat16)
    phase(3, row_block(qbuf), lambda k: rbuf2.at[k])
    summed2 = jnp.sum(rbuf2[...].astype(jnp.float32), axis=0)
    out_ref[...] = (sbuf[...].astype(jnp.float32) + summed2).astype(out_ref.dtype)


def tail(part, w_out, states, gain, w_gate_up, w_down, n, sn, cid):
    rows, width = states.shape
    lanes = part.shape[2] - 2
    units = w_gate_up.shape[2]
    vmem = pl.BlockSpec(memory_space=pltpu.VMEM)
    return pl.pallas_call(
        functools.partial(_tail_kernel, n, sn),
        out_shape=jax.ShapeDtypeStruct((rows, width), states.dtype),
        in_specs=[vmem] * 6,
        out_specs=vmem,
        scratch_shapes=[
            pltpu.VMEM((sn,) + part.shape, jnp.float32),
            pltpu.VMEM((n, rows, lanes), jnp.bfloat16),
            pltpu.SemaphoreType.DMA((sn,)),
            pltpu.SemaphoreType.DMA((sn,)),
            pltpu.VMEM((n * rows, lanes), jnp.bfloat16),
            pltpu.VMEM((n * rows, width), jnp.bfloat16),
            pltpu.VMEM((n, rows, width), jnp.bfloat16),
            pltpu.VMEM((rows, width), jnp.bfloat16),
            pltpu.VMEM((rows, width), jnp.bfloat16),
            pltpu.VMEM((n * rows, width), jnp.bfloat16),
            pltpu.VMEM((n * rows, width), jnp.bfloat16),
            pltpu.VMEM((n, rows, width), jnp.bfloat16),
            pltpu.SemaphoreType.DMA((4, n)),
            pltpu.SemaphoreType.DMA((4, n)),
            pltpu.SemaphoreType.DMA(()),
        ],
        compiler_params=pltpu.CompilerParams(collective_id=cid, has_side_effects=True),
    )(part, w_out, states, gain, w_gate_up.reshape(width, 2 * units), w_down)


def _head_kernel(
    n, states_ref, gains_ref, w_ref, trig_ref, qkv_ref, recv_ref, x_ref, gbuf, send_sem, recv_sem, local_sem
):
    axis = "tensor"
    me = lax.axis_index(axis)
    rows = x_ref.shape[0]
    block = qkv_ref.shape[1] // 2
    x_ref[...] = rms_norm(states_ref[...].astype(jnp.float32), gains_ref[0:1, :])
    barrier = pltpu.get_barrier_semaphore()

    def greet(d, carry):
        pl.semaphore_signal(
            barrier, 1, device_id={axis: lax.rem(me + d, n)}, device_id_type=MESH_ID
        )
        return carry

    lax.fori_loop(1, n, greet, 0)
    pl.semaphore_wait(barrier, n - 1)

    def phase(p, src_of, dst_of):
        def outgoing(d):
            j = lax.rem(me + d, n)
            return pltpu.make_async_remote_copy(
                src_ref=src_of(j),
                dst_ref=dst_of(me),
                send_sem=send_sem.at[p, j],
                recv_sem=recv_sem.at[p, me],
                device_id={axis: j},
                device_id_type=MESH_ID,
            )

        def incoming(d):
            k = lax.rem(me + n - d, n)
            return pltpu.make_async_remote_copy(
                src_ref=src_of(k),
                dst_ref=dst_of(k),
                send_sem=send_sem.at[p, k],
                recv_sem=recv_sem.at[p, k],
                device_id={axis: k},
                device_id_type=MESH_ID,
            )

        local = pltpu.make_async_copy(src_of(me), dst_of(me), local_sem)
        local.start()

        def start(d, carry):
            outgoing(d).start()
            return carry

        lax.fori_loop(1, n, start, 0)

        def finish(d, carry):
            outgoing(d).wait_send()
            incoming(d).wait_recv()
            return carry

        lax.fori_loop(1, n, finish, 0)
        local.wait()

    phase(0, lambda j: x_ref, lambda k: gbuf.at[pl.ds(k * rows, rows)])
    proj = jnp.dot(gbuf[...], w_ref[...], preferred_element_type=jnp.float32)
    trig = trig_ref[...]
    pair = proj[:, :block]
    half = HEAD_SIZE // 2
    lane = lax.broadcasted_iota(jnp.int32, pair.shape, 1)
    turned = jnp.where(
        lane % HEAD_SIZE < half,
        -pltpu.roll(pair, block - half, 1),
        pltpu.roll(pair, half, 1),
    )
    rotated = pair * trig[:, :block] + turned * trig[:, block:]
    qkv_ref[:, :block] = rotated.astype(qkv_ref.dtype)
    qkv_ref[:, block : block + block // 2] = proj[:, block:].astype(qkv_ref.dtype)
    qkv_ref[:, block + block // 2 :] = jnp.zeros((pair.shape[0], block // 2), qkv_ref.dtype)
    phase(1, lambda j: qkv_ref.at[pl.ds(j * rows, rows)], lambda k: recv_ref.at[k])


def head(states, gains, w_ext, trig, n, cid):
    rows, width = states.shape
    cols = w_ext.shape[1] // 3 * 4
    vmem = pl.BlockSpec(memory_space=pltpu.VMEM)
    return pl.pallas_call(
        functools.partial(_head_kernel, n),
        out_shape=(
            jax.ShapeDtypeStruct((n * rows, cols), jnp.bfloat16),
            jax.ShapeDtypeStruct((n, rows, cols), jnp.bfloat16),
        ),
        in_specs=[vmem] * 4,
        out_specs=(vmem, vmem),
        scratch_shapes=[
            pltpu.VMEM((rows, width), jnp.bfloat16),
            pltpu.VMEM((n * rows, width), jnp.bfloat16),
            pltpu.SemaphoreType.DMA((2, n)),
            pltpu.SemaphoreType.DMA((2, n)),
            pltpu.SemaphoreType.DMA(()),
        ],
        compiler_params=pltpu.CompilerParams(collective_id=cid, has_side_effects=True),
    )(states, gains, w_ext, trig)


def per_device(
    states,
    attn_gain,
    w_qkv,
    w_out,
    mlp_gain,
    w_gate_up,
    w_down,
    key_cache,
    value_cache,
    sink_keys,
    sink_values,
    cache_len,
    slot_mask,
    slot_pos,
    new_pos,
    tn,
    sn,
):
    rows = states.shape[0]
    width = states.shape[1]
    row_start = lax.axis_index("tensor") * rows
    floats = states.astype(jnp.float32)
    lanes = w_qkv.shape[2]
    heads_here = lanes // HEAD_SIZE
    qkv_matrix = w_qkv.reshape(width, 3 * lanes)
    half = HEAD_SIZE // 2
    inverse = jnp.exp(
        -jnp.log(jnp.float32(130000.0)) * jnp.arange(half, dtype=jnp.float32) * (2.0 / HEAD_SIZE)
    )
    angle = new_pos.astype(jnp.float32)[:, None] * inverse[None, :]
    angle = jnp.concatenate([angle] * (4 * heads_here), axis=-1)
    trig = jnp.concatenate([jnp.cos(angle), jnp.sin(angle)], axis=-1)
    gains = jnp.stack([attn_gain, mlp_gain])
    qkv_all, mine = head(states, gains, qkv_matrix, trig, tn, 0)
    batch = qkv_all.shape[0]
    keys_all = qkv_all[:, lanes : 2 * lanes]
    values_all = qkv_all[:, 2 * lanes : 3 * lanes]
    mine = mine.reshape(tn, rows, 4, heads_here, HEAD_SIZE)
    mine = jnp.transpose(mine, (1, 2, 0, 3, 4)).reshape(rows, 4, tn * heads_here, HEAD_SIZE)
    queries = mine[:, 0]
    keys_new = mine[:, 1]
    values_new = mine[:, 2]
    all_heads = queries.shape[1]
    own_len = lax.dynamic_slice_in_dim(cache_len, row_start, rows, 0)
    own_pos = lax.dynamic_slice_in_dim(new_pos, row_start, rows, 0)
    window_here = key_cache.shape[2]
    seq_index = lax.axis_index("seq")
    slots = seq_index * window_here + jnp.arange(window_here, dtype=jnp.int32)
    live = (slots[None, :] < own_len[:, None]) & (slot_mask == 1)
    live = live & (slot_pos < own_pos[:, None]) & (own_pos[:, None] - slot_pos < WINDOW)
    live = live[:, None, :]
    first_shard = seq_index == 0
    kwin = key_cache.reshape(rows, all_heads, HEAD_SIZE, window_here)
    vwin = value_cache.reshape(rows, all_heads, HEAD_SIZE, window_here)
    sink_key_rows = sink_keys.reshape(rows, all_heads, HEAD_SIZE, sink_keys.shape[2])
    vsink = sink_values.reshape(rows, all_heads, HEAD_SIZE, sink_values.shape[2])
    score_win = (
        jnp.einsum("bhd,bhds->bhs", queries, kwin, preferred_element_type=jnp.float32) * 0.125
    )
    score_win = jnp.where(live, score_win, NEG)
    score_sink = (
        jnp.einsum("bhd,bhds->bhs", queries, sink_key_rows, preferred_element_type=jnp.float32)
        * 0.125
    )
    score_sink = jnp.where(first_shard, score_sink, NEG)
    score_new = jnp.sum(queries.astype(jnp.float32) * keys_new.astype(jnp.float32), axis=-1) * 0.125
    score_new = jnp.where(first_shard, score_new, NEG)
    local_top = jnp.maximum(
        jnp.maximum(jnp.max(score_win, axis=-1), jnp.max(score_sink, axis=-1)), score_new
    )
    weight_win = jnp.where(live, jnp.exp(score_win - local_top[..., None]), 0.0)
    weight_sink = jnp.where(first_shard, jnp.exp(score_sink - local_top[..., None]), 0.0)
    weight_new = jnp.where(first_shard, jnp.exp(score_new - local_top), 0.0)
    total = jnp.sum(weight_win, axis=-1) + jnp.sum(weight_sink, axis=-1) + weight_new
    mixture = jnp.einsum(
        "bhs,bhds->bhd", weight_win.astype(jnp.bfloat16), vwin, preferred_element_type=jnp.float32
    )
    mixture = mixture + jnp.einsum(
        "bhs,bhds->bhd", weight_sink.astype(jnp.bfloat16), vsink, preferred_element_type=jnp.float32
    )
    mixture = mixture + undo_round(weight_new)[..., None] * values_new.astype(jnp.float32)
    packed = jnp.concatenate([mixture, total[..., None], local_top[..., None]], axis=-1)
    packed = jnp.transpose(packed, (1, 0, 2))
    out_states = tail(packed, w_out, states, gains, w_gate_up, w_down, tn, sn, 3)
    return (out_states, keys_all, values_all)


def solution(mesh):
    in_specs = (
        P("tensor", None),
        P(),
        P(None, None, "tensor"),
        P("tensor", None),
        P(),
        P(None, None, "tensor"),
        P("tensor", None),
        P("tensor", None, "seq"),
        P("tensor", None, "seq"),
        P("tensor", None, None),
        P("tensor", None, None),
        P(),
        P("tensor", "seq"),
        P("tensor", "seq"),
        P(),
    )
    out_specs = (P("tensor", None), P(None, "tensor"), P(None, "tensor"))
    body = functools.partial(per_device, tn=mesh.shape["tensor"], sn=mesh.shape["seq"])
    return jax.shard_map(
        body, mesh=mesh, in_specs=in_specs, out_specs=out_specs, check_vma=False
    )
```

```python
import functools

import jax
import jax.numpy as jnp
from jax import lax
from jax.experimental import pallas as pl
from jax.experimental.pallas import tpu as pltpu
from jax.sharding import PartitionSpec as P

HEAD_SIZE = 64
WINDOW = 4096


NEG = -1e30
MESH_ID = pl.DeviceIdType.MESH


def rms_norm(values, gain):
    meansq = jnp.mean(values * values, axis=-1, keepdims=True)
    return (values * lax.rsqrt(meansq + 1e-05) * gain.astype(jnp.float32)).astype(jnp.bfloat16)


def rotary(tensor, cosine, sine):
    half = tensor.shape[-1] // 2
    turned = jnp.concatenate([-tensor[..., half:], tensor[..., :half]], axis=-1)
    return tensor * cosine + turned * sine


def undo_round(weights):
    rounded = lax.optimization_barrier(weights.astype(jnp.bfloat16))
    return rounded.astype(jnp.float32)


def _exchange_kernel(n, axis, gather, x_ref, y_ref, send_sem, recv_sem, local_sem):
    me = lax.axis_index(axis)
    barrier = pltpu.get_barrier_semaphore()

    def greet(d, carry):
        peer = lax.rem(me + d, n)
        pl.semaphore_signal(barrier, 1, device_id={axis: peer}, device_id_type=MESH_ID)
        return carry

    lax.fori_loop(1, n, greet, 0)
    pl.semaphore_wait(barrier, n - 1)

    def source(j):
        return x_ref if gather else x_ref.at[j]

    def outgoing(d):
        j = lax.rem(me + d, n)
        return pltpu.make_async_remote_copy(
            src_ref=source(j),
            dst_ref=y_ref.at[me],
            send_sem=send_sem.at[j],
            recv_sem=recv_sem.at[me],
            device_id={axis: j},
            device_id_type=MESH_ID,
        )

    def incoming(d):
        k = lax.rem(me + n - d, n)
        return pltpu.make_async_remote_copy(
            src_ref=source(k),
            dst_ref=y_ref.at[k],
            send_sem=send_sem.at[k],
            recv_sem=recv_sem.at[k],
            device_id={axis: k},
            device_id_type=MESH_ID,
        )

    local = pltpu.make_async_copy(source(me), y_ref.at[me], local_sem)
    local.start()

    def start(d, carry):
        outgoing(d).start()
        return carry

    lax.fori_loop(1, n, start, 0)

    def finish(d, carry):
        outgoing(d).wait_send()
        incoming(d).wait_recv()
        return carry

    lax.fori_loop(1, n, finish, 0)
    local.wait()


def exchange(x, axis, n, cid, gather=False):
    piece = x.shape if gather else x.shape[1:]
    return pl.pallas_call(
        functools.partial(_exchange_kernel, n, axis, gather),
        out_shape=jax.ShapeDtypeStruct((n,) + tuple(piece), x.dtype),
        in_specs=[pl.BlockSpec(memory_space=pl.ANY)],
        out_specs=pl.BlockSpec(memory_space=pl.ANY),
        scratch_shapes=[
            pltpu.SemaphoreType.DMA((n,)),
            pltpu.SemaphoreType.DMA((n,)),
            pltpu.SemaphoreType.DMA(()),
        ],
        compiler_params=pltpu.CompilerParams(collective_id=cid, has_side_effects=True),
    )(x)


def _tail_kernel(
    n,
    sn,
    part_ref,
    w_out_ref,
    states_ref,
    gain_ref,
    gate_ref,
    down_ref,
    out_ref,
    seq_buf,
    att_buf,
    seq_send,
    seq_recv,
    abuf,
    pbuf,
    rbuf,
    sbuf,
    nbuf,
    gbuf,
    qbuf,
    rbuf2,
    send_sem,
    recv_sem,
    local_sem,
):
    axis = "tensor"
    me = lax.axis_index(axis)
    seq_me = lax.axis_index("seq")
    rows = states_ref.shape[0]
    barrier = pltpu.get_barrier_semaphore()

    def greet(d, carry):
        pl.semaphore_signal(
            barrier, 1, device_id={axis: lax.rem(me + d, n)}, device_id_type=MESH_ID
        )
        return carry

    lax.fori_loop(1, n, greet, 0)

    def greet_seq(d, carry):
        pl.semaphore_signal(
            barrier, 1, device_id={"seq": lax.rem(seq_me + d, sn)}, device_id_type=MESH_ID
        )
        return carry

    lax.fori_loop(1, sn, greet_seq, 0)
    pl.semaphore_wait(barrier, n - 1 + sn - 1)

    def seq_out(d):
        j = lax.rem(seq_me + d, sn)
        return pltpu.make_async_remote_copy(
            src_ref=part_ref,
            dst_ref=seq_buf.at[seq_me],
            send_sem=seq_send.at[j],
            recv_sem=seq_recv.at[seq_me],
            device_id={"seq": j},
            device_id_type=MESH_ID,
        )

    def seq_in(d):
        k = lax.rem(seq_me + sn - d, sn)
        return pltpu.make_async_remote_copy(
            src_ref=part_ref,
            dst_ref=seq_buf.at[k],
            send_sem=seq_send.at[k],
            recv_sem=seq_recv.at[k],
            device_id={"seq": k},
            device_id_type=MESH_ID,
        )

    seq_local = pltpu.make_async_copy(part_ref, seq_buf.at[seq_me], local_sem)
    seq_local.start()

    def seq_start(d, carry):
        seq_out(d).start()
        return carry

    lax.fori_loop(1, sn, seq_start, 0)

    def seq_finish(d, carry):
        seq_out(d).wait_send()
        seq_in(d).wait_recv()
        return carry

    lax.fori_loop(1, sn, seq_finish, 0)
    seq_local.wait()
    parts = seq_buf[...]
    lanes = att_buf.shape[2]
    part_top = parts[..., lanes + 1 : lanes + 2]
    top = jnp.max(part_top, axis=0)
    scale = jnp.exp(part_top - top[None])
    total = jnp.sum(parts[..., lanes : lanes + 1] * scale, axis=0)
    mixture = jnp.sum(parts[..., :lanes] * scale, axis=0)
    att_buf[...] = (mixture / total).astype(att_buf.dtype)
    units = down_ref.shape[0]

    def phase(p, src_of, dst_of):
        def outgoing(d):
            j = lax.rem(me + d, n)
            return pltpu.make_async_remote_copy(
                src_ref=src_of(j),
                dst_ref=dst_of(me),
                send_sem=send_sem.at[p, j],
                recv_sem=recv_sem.at[p, me],
                device_id={axis: j},
                device_id_type=MESH_ID,
            )

        def incoming(d):
            k = lax.rem(me + n - d, n)
            return pltpu.make_async_remote_copy(
                src_ref=src_of(k),
                dst_ref=dst_of(k),
                send_sem=send_sem.at[p, k],
                recv_sem=recv_sem.at[p, k],
                device_id={axis: k},
                device_id_type=MESH_ID,
            )

        local = pltpu.make_async_copy(src_of(me), dst_of(me), local_sem)
        local.start()

        def start(d, carry):
            outgoing(d).start()
            return carry

        lax.fori_loop(1, n, start, 0)

        def finish(d, carry):
            outgoing(d).wait_send()
            incoming(d).wait_recv()
            return carry

        lax.fori_loop(1, n, finish, 0)
        local.wait()

    def row_block(ref):
        return lambda i: ref.at[pl.ds(i * rows, rows)]

    phase(0, lambda j: att_buf.at[j], row_block(abuf))
    partial = jnp.dot(abuf[...], w_out_ref[...], preferred_element_type=jnp.float32)
    pbuf[...] = partial.astype(jnp.bfloat16)
    phase(1, row_block(pbuf), lambda k: rbuf.at[k])
    summed = jnp.sum(rbuf[...].astype(jnp.float32), axis=0)
    resid = (states_ref[...].astype(jnp.float32) + summed).astype(jnp.bfloat16)
    sbuf[...] = resid
    nbuf[...] = rms_norm(resid.astype(jnp.float32), gain_ref[1:2, :])
    phase(2, lambda j: nbuf, row_block(gbuf))
    gate_up = jnp.dot(gbuf[...], gate_ref[...], preferred_element_type=jnp.float32)
    hidden = (jax.nn.silu(gate_up[:, :units]) * gate_up[:, units:]).astype(jnp.bfloat16)
    down = jnp.dot(hidden, down_ref[...], preferred_element_type=jnp.float32)
    qbuf[...] = down.astype(jnp.bfloat16)
    phase(3, row_block(qbuf), lambda k: rbuf2.at[k])
    summed2 = jnp.sum(rbuf2[...].astype(jnp.float32), axis=0)
    out_ref[...] = (sbuf[...].astype(jnp.float32) + summed2).astype(out_ref.dtype)


def tail(part, w_out, states, gain, w_gate_up, w_down, n, sn, cid):
    rows, width = states.shape
    lanes = part.shape[2] - 2
    units = w_gate_up.shape[2]
    vmem = pl.BlockSpec(memory_space=pltpu.VMEM)
    return pl.pallas_call(
        functools.partial(_tail_kernel, n, sn),
        out_shape=jax.ShapeDtypeStruct((rows, width), states.dtype),
        in_specs=[vmem] * 6,
        out_specs=vmem,
        scratch_shapes=[
            pltpu.VMEM((sn,) + part.shape, jnp.float32),
            pltpu.VMEM((n, rows, lanes), jnp.bfloat16),
            pltpu.SemaphoreType.DMA((sn,)),
            pltpu.SemaphoreType.DMA((sn,)),
            pltpu.VMEM((n * rows, lanes), jnp.bfloat16),
            pltpu.VMEM((n * rows, width), jnp.bfloat16),
            pltpu.VMEM((n, rows, width), jnp.bfloat16),
            pltpu.VMEM((rows, width), jnp.bfloat16),
            pltpu.VMEM((rows, width), jnp.bfloat16),
            pltpu.VMEM((n * rows, width), jnp.bfloat16),
            pltpu.VMEM((n * rows, width), jnp.bfloat16),
            pltpu.VMEM((n, rows, width), jnp.bfloat16),
            pltpu.SemaphoreType.DMA((4, n)),
            pltpu.SemaphoreType.DMA((4, n)),
            pltpu.SemaphoreType.DMA(()),
        ],
        compiler_params=pltpu.CompilerParams(collective_id=cid, has_side_effects=True),
    )(part, w_out, states, gain, w_gate_up.reshape(width, 2 * units), w_down)


def _head_kernel(
    n, states_ref, gains_ref, w_ref, trig_ref, qkv_ref, recv_ref, x_ref, gbuf, send_sem, recv_sem, local_sem
):
    axis = "tensor"
    me = lax.axis_index(axis)
    rows = x_ref.shape[0]
    block = qkv_ref.shape[1] // 2
    x_ref[...] = rms_norm(states_ref[...].astype(jnp.float32), gains_ref[0:1, :])
    barrier = pltpu.get_barrier_semaphore()

    def greet(d, carry):
        pl.semaphore_signal(
            barrier, 1, device_id={axis: lax.rem(me + d, n)}, device_id_type=MESH_ID
        )
        return carry

    lax.fori_loop(1, n, greet, 0)
    pl.semaphore_wait(barrier, n - 1)

    def phase(p, src_of, dst_of):
        def outgoing(d):
            j = lax.rem(me + d, n)
            return pltpu.make_async_remote_copy(
                src_ref=src_of(j),
                dst_ref=dst_of(me),
                send_sem=send_sem.at[p, j],
                recv_sem=recv_sem.at[p, me],
                device_id={axis: j},
                device_id_type=MESH_ID,
            )

        def incoming(d):
            k = lax.rem(me + n - d, n)
            return pltpu.make_async_remote_copy(
                src_ref=src_of(k),
                dst_ref=dst_of(k),
                send_sem=send_sem.at[p, k],
                recv_sem=recv_sem.at[p, k],
                device_id={axis: k},
                device_id_type=MESH_ID,
            )

        local = pltpu.make_async_copy(src_of(me), dst_of(me), local_sem)
        local.start()

        def start(d, carry):
            outgoing(d).start()
            return carry

        lax.fori_loop(1, n, start, 0)

        def finish(d, carry):
            outgoing(d).wait_send()
            incoming(d).wait_recv()
            return carry

        lax.fori_loop(1, n, finish, 0)
        local.wait()

    phase(0, lambda j: x_ref, lambda k: gbuf.at[pl.ds(k * rows, rows)])
    proj = jnp.dot(gbuf[...], w_ref[...], preferred_element_type=jnp.float32)
    trig = trig_ref[...]
    pair = proj[:, :block]
    half = HEAD_SIZE // 2
    lane = lax.broadcasted_iota(jnp.int32, pair.shape, 1)
    turned = jnp.where(
        lane % HEAD_SIZE < half,
        -pltpu.roll(pair, block - half, 1),
        pltpu.roll(pair, half, 1),
    )
    rotated = pair * trig[:, :block] + turned * trig[:, block:]
    qkv_ref[:, :block] = rotated.astype(qkv_ref.dtype)
    qkv_ref[:, block : block + block // 2] = proj[:, block:].astype(qkv_ref.dtype)
    qkv_ref[:, block + block // 2 :] = jnp.zeros((pair.shape[0], block // 2), qkv_ref.dtype)
    phase(1, lambda j: qkv_ref.at[pl.ds(j * rows, rows)], lambda k: recv_ref.at[k])


def head(states, gains, w_ext, trig, n, cid):
    rows, width = states.shape
    cols = w_ext.shape[1] // 3 * 4
    vmem = pl.BlockSpec(memory_space=pltpu.VMEM)
    return pl.pallas_call(
        functools.partial(_head_kernel, n),
        out_shape=(
            jax.ShapeDtypeStruct((n * rows, cols), jnp.bfloat16),
            jax.ShapeDtypeStruct((n, rows, cols), jnp.bfloat16),
        ),
        in_specs=[vmem] * 4,
        out_specs=(vmem, vmem),
        scratch_shapes=[
            pltpu.VMEM((rows, width), jnp.bfloat16),
            pltpu.VMEM((n * rows, width), jnp.bfloat16),
            pltpu.SemaphoreType.DMA((2, n)),
            pltpu.SemaphoreType.DMA((2, n)),
            pltpu.SemaphoreType.DMA(()),
        ],
        compiler_params=pltpu.CompilerParams(collective_id=cid, has_side_effects=True),
    )(states, gains, w_ext, trig)


def per_device(
    states,
    attn_gain,
    w_qkv,
    w_out,
    mlp_gain,
    w_gate_up,
    w_down,
    key_cache,
    value_cache,
    sink_keys,
    sink_values,
    cache_len,
    slot_mask,
    slot_pos,
    new_pos,
    tn,
    sn,
):
    rows = states.shape[0]
    width = states.shape[1]
    row_start = lax.axis_index("tensor") * rows
    floats = states.astype(jnp.float32)
    lanes = w_qkv.shape[2]
    heads_here = lanes // HEAD_SIZE
    qkv_matrix = w_qkv.reshape(width, 3 * lanes)
    half = HEAD_SIZE // 2
    inverse = jnp.exp(
        -jnp.log(jnp.float32(130000.0)) * jnp.arange(half, dtype=jnp.float32) * (2.0 / HEAD_SIZE)
    )
    angle = new_pos.astype(jnp.float32)[:, None] * inverse[None, :]
    angle = jnp.concatenate([angle] * (4 * heads_here), axis=-1)
    trig = jnp.concatenate([jnp.cos(angle), jnp.sin(angle)], axis=-1)
    gains = jnp.stack([attn_gain, mlp_gain])
    qkv_all, mine = head(states, gains, qkv_matrix, trig, tn, 0)
    batch = qkv_all.shape[0]
    keys_all = qkv_all[:, lanes : 2 * lanes]
    values_all = qkv_all[:, 2 * lanes : 3 * lanes]
    mine = mine.reshape(tn, rows, 4, heads_here, HEAD_SIZE)
    mine = jnp.transpose(mine, (1, 2, 0, 3, 4)).reshape(rows, 4, tn * heads_here, HEAD_SIZE)
    queries = mine[:, 0]
    keys_new = mine[:, 1]
    values_new = mine[:, 2]
    all_heads = queries.shape[1]
    own_len = lax.dynamic_slice_in_dim(cache_len, row_start, rows, 0)
    own_pos = lax.dynamic_slice_in_dim(new_pos, row_start, rows, 0)
    window_here = key_cache.shape[2]
    seq_index = lax.axis_index("seq")
    slots = seq_index * window_here + jnp.arange(window_here, dtype=jnp.int32)
    live = (slots[None, :] < own_len[:, None]) & (slot_mask == 1)
    live = live & (slot_pos < own_pos[:, None]) & (own_pos[:, None] - slot_pos < WINDOW)
    live = live[:, None, :]
    first_shard = seq_index == 0
    kwin = key_cache.reshape(rows, all_heads, HEAD_SIZE, window_here)
    vwin = value_cache.reshape(rows, all_heads, HEAD_SIZE, window_here)
    sink_key_rows = sink_keys.reshape(rows, all_heads, HEAD_SIZE, sink_keys.shape[2])
    vsink = sink_values.reshape(rows, all_heads, HEAD_SIZE, sink_values.shape[2])
    score_win = (
        jnp.einsum("bhd,bhds->bhs", queries, kwin, preferred_element_type=jnp.float32) * 0.125
    )
    score_win = jnp.where(live, score_win, NEG)
    score_sink = (
        jnp.sum(
            queries.astype(jnp.float32)[..., None] * sink_key_rows.astype(jnp.float32), axis=2
        )
        * 0.125
    )
    score_sink = jnp.where(first_shard, score_sink, NEG)
    score_new = jnp.sum(queries.astype(jnp.float32) * keys_new.astype(jnp.float32), axis=-1) * 0.125
    score_new = jnp.where(first_shard, score_new, NEG)
    local_top = jnp.maximum(
        jnp.maximum(jnp.max(score_win, axis=-1), jnp.max(score_sink, axis=-1)), score_new
    )
    weight_win = jnp.where(live, jnp.exp(score_win - local_top[..., None]), 0.0)
    weight_sink = jnp.where(first_shard, jnp.exp(score_sink - local_top[..., None]), 0.0)
    weight_new = jnp.where(first_shard, jnp.exp(score_new - local_top), 0.0)
    total = jnp.sum(weight_win, axis=-1) + jnp.sum(weight_sink, axis=-1) + weight_new
    mixture = jnp.einsum(
        "bhs,bhds->bhd", weight_win.astype(jnp.bfloat16), vwin, preferred_element_type=jnp.float32
    )
    mixture = mixture + jnp.sum(
        undo_round(weight_sink)[:, :, None, :] * vsink.astype(jnp.float32), axis=-1
    )
    mixture = mixture + undo_round(weight_new)[..., None] * values_new.astype(jnp.float32)
    packed = jnp.concatenate([mixture, total[..., None], local_top[..., None]], axis=-1)
    packed = jnp.transpose(packed, (1, 0, 2))
    out_states = tail(packed, w_out, states, gains, w_gate_up, w_down, tn, sn, 3)
    return (out_states, keys_all, values_all)


def solution(mesh):
    in_specs = (
        P("tensor", None),
        P(),
        P(None, None, "tensor"),
        P("tensor", None),
        P(),
        P(None, None, "tensor"),
        P("tensor", None),
        P("tensor", None, "seq"),
        P("tensor", None, "seq"),
        P("tensor", None, None),
        P("tensor", None, None),
        P(),
        P("tensor", "seq"),
        P("tensor", "seq"),
        P(),
    )
    out_specs = (P("tensor", None), P(None, "tensor"), P(None, "tensor"))
    body = functools.partial(per_device, tn=mesh.shape["tensor"], sn=mesh.shape["seq"])
    return jax.shard_map(
        body, mesh=mesh, in_specs=in_specs, out_specs=out_specs, check_vma=False
    )
```

```python
import functools

import jax
import jax.numpy as jnp
from jax import lax
from jax.experimental import pallas as pl
from jax.experimental.pallas import tpu as pltpu
from jax.sharding import PartitionSpec as P

HEAD_SIZE = 64
WINDOW = 4096


NEG = -1e30
MESH_ID = pl.DeviceIdType.MESH


def rms_norm(values, gain):
    meansq = jnp.mean(values * values, axis=-1, keepdims=True)
    return (values * lax.rsqrt(meansq + 1e-05) * gain.astype(jnp.float32)).astype(jnp.bfloat16)


def rotary(tensor, cosine, sine):
    half = tensor.shape[-1] // 2
    turned = jnp.concatenate([-tensor[..., half:], tensor[..., :half]], axis=-1)
    return tensor * cosine + turned * sine


def undo_round(weights):
    rounded = lax.optimization_barrier(weights.astype(jnp.bfloat16))
    return rounded.astype(jnp.float32)


def _exchange_kernel(n, axis, gather, x_ref, y_ref, send_sem, recv_sem, local_sem):
    me = lax.axis_index(axis)
    barrier = pltpu.get_barrier_semaphore()

    def greet(d, carry):
        peer = lax.rem(me + d, n)
        pl.semaphore_signal(barrier, 1, device_id={axis: peer}, device_id_type=MESH_ID)
        return carry

    lax.fori_loop(1, n, greet, 0)
    pl.semaphore_wait(barrier, n - 1)

    def source(j):
        return x_ref if gather else x_ref.at[j]

    def outgoing(d):
        j = lax.rem(me + d, n)
        return pltpu.make_async_remote_copy(
            src_ref=source(j),
            dst_ref=y_ref.at[me],
            send_sem=send_sem.at[j],
            recv_sem=recv_sem.at[me],
            device_id={axis: j},
            device_id_type=MESH_ID,
        )

    def incoming(d):
        k = lax.rem(me + n - d, n)
        return pltpu.make_async_remote_copy(
            src_ref=source(k),
            dst_ref=y_ref.at[k],
            send_sem=send_sem.at[k],
            recv_sem=recv_sem.at[k],
            device_id={axis: k},
            device_id_type=MESH_ID,
        )

    local = pltpu.make_async_copy(source(me), y_ref.at[me], local_sem)
    local.start()

    def start(d, carry):
        outgoing(d).start()
        return carry

    lax.fori_loop(1, n, start, 0)

    def finish(d, carry):
        outgoing(d).wait_send()
        incoming(d).wait_recv()
        return carry

    lax.fori_loop(1, n, finish, 0)
    local.wait()


def exchange(x, axis, n, cid, gather=False):
    piece = x.shape if gather else x.shape[1:]
    return pl.pallas_call(
        functools.partial(_exchange_kernel, n, axis, gather),
        out_shape=jax.ShapeDtypeStruct((n,) + tuple(piece), x.dtype),
        in_specs=[pl.BlockSpec(memory_space=pl.ANY)],
        out_specs=pl.BlockSpec(memory_space=pl.ANY),
        scratch_shapes=[
            pltpu.SemaphoreType.DMA((n,)),
            pltpu.SemaphoreType.DMA((n,)),
            pltpu.SemaphoreType.DMA(()),
        ],
        compiler_params=pltpu.CompilerParams(collective_id=cid, has_side_effects=True),
    )(x)


def _tail_kernel(
    n,
    sn,
    part_ref,
    w_out_ref,
    states_ref,
    gain_ref,
    gate_ref,
    down_ref,
    out_ref,
    seq_buf,
    att_buf,
    seq_send,
    seq_recv,
    abuf,
    pbuf,
    rbuf,
    sbuf,
    nbuf,
    gbuf,
    qbuf,
    rbuf2,
    send_sem,
    recv_sem,
    local_sem,
):
    axis = "tensor"
    me = lax.axis_index(axis)
    seq_me = lax.axis_index("seq")
    rows = states_ref.shape[0]
    barrier = pltpu.get_barrier_semaphore()

    def greet(d, carry):
        pl.semaphore_signal(
            barrier, 1, device_id={axis: lax.rem(me + d, n)}, device_id_type=MESH_ID
        )
        return carry

    lax.fori_loop(1, n, greet, 0)

    def greet_seq(d, carry):
        pl.semaphore_signal(
            barrier, 1, device_id={"seq": lax.rem(seq_me + d, sn)}, device_id_type=MESH_ID
        )
        return carry

    lax.fori_loop(1, sn, greet_seq, 0)
    pl.semaphore_wait(barrier, n - 1 + sn - 1)

    def seq_out(d):
        j = lax.rem(seq_me + d, sn)
        return pltpu.make_async_remote_copy(
            src_ref=part_ref,
            dst_ref=seq_buf.at[seq_me],
            send_sem=seq_send.at[j],
            recv_sem=seq_recv.at[seq_me],
            device_id={"seq": j},
            device_id_type=MESH_ID,
        )

    def seq_in(d):
        k = lax.rem(seq_me + sn - d, sn)
        return pltpu.make_async_remote_copy(
            src_ref=part_ref,
            dst_ref=seq_buf.at[k],
            send_sem=seq_send.at[k],
            recv_sem=seq_recv.at[k],
            device_id={"seq": k},
            device_id_type=MESH_ID,
        )

    seq_local = pltpu.make_async_copy(part_ref, seq_buf.at[seq_me], local_sem)
    seq_local.start()

    def seq_start(d, carry):
        seq_out(d).start()
        return carry

    lax.fori_loop(1, sn, seq_start, 0)

    def seq_finish(d, carry):
        seq_out(d).wait_send()
        seq_in(d).wait_recv()
        return carry

    lax.fori_loop(1, sn, seq_finish, 0)
    seq_local.wait()
    parts = seq_buf[...]
    lanes = att_buf.shape[2]
    part_top = parts[..., lanes + 1 : lanes + 2]
    top = jnp.max(part_top, axis=0)
    scale = jnp.exp(part_top - top[None])
    total = jnp.sum(parts[..., lanes : lanes + 1] * scale, axis=0)
    mixture = jnp.sum(parts[..., :lanes] * scale, axis=0)
    att_buf[...] = (mixture / total).astype(att_buf.dtype)
    units = down_ref.shape[0]

    def phase(p, src_of, dst_of):
        def outgoing(d):
            j = lax.rem(me + d, n)
            return pltpu.make_async_remote_copy(
                src_ref=src_of(j),
                dst_ref=dst_of(me),
                send_sem=send_sem.at[p, j],
                recv_sem=recv_sem.at[p, me],
                device_id={axis: j},
                device_id_type=MESH_ID,
            )

        def incoming(d):
            k = lax.rem(me + n - d, n)
            return pltpu.make_async_remote_copy(
                src_ref=src_of(k),
                dst_ref=dst_of(k),
                send_sem=send_sem.at[p, k],
                recv_sem=recv_sem.at[p, k],
                device_id={axis: k},
                device_id_type=MESH_ID,
            )

        local = pltpu.make_async_copy(src_of(me), dst_of(me), local_sem)
        local.start()

        def start(d, carry):
            outgoing(d).start()
            return carry

        lax.fori_loop(1, n, start, 0)

        def finish(d, carry):
            outgoing(d).wait_send()
            incoming(d).wait_recv()
            return carry

        lax.fori_loop(1, n, finish, 0)
        local.wait()

    def row_block(ref):
        return lambda i: ref.at[pl.ds(i * rows, rows)]

    phase(0, lambda j: att_buf.at[j], row_block(abuf))
    partial = jnp.dot(abuf[...], w_out_ref[...], preferred_element_type=jnp.float32)
    pbuf[...] = partial.astype(jnp.bfloat16)
    phase(1, row_block(pbuf), lambda k: rbuf.at[k])
    summed = jnp.sum(rbuf[...].astype(jnp.float32), axis=0)
    resid = (states_ref[...].astype(jnp.float32) + summed).astype(jnp.bfloat16)
    sbuf[...] = resid
    nbuf[...] = rms_norm(resid.astype(jnp.float32), gain_ref[1:2, :])
    phase(2, lambda j: nbuf, row_block(gbuf))
    gate_up = jnp.dot(gbuf[...], gate_ref[...], preferred_element_type=jnp.float32)
    hidden = (jax.nn.silu(gate_up[:, :units]) * gate_up[:, units:]).astype(jnp.bfloat16)
    down = jnp.dot(hidden, down_ref[...], preferred_element_type=jnp.float32)
    qbuf[...] = down.astype(jnp.bfloat16)
    phase(3, row_block(qbuf), lambda k: rbuf2.at[k])
    summed2 = jnp.sum(rbuf2[...].astype(jnp.float32), axis=0)
    out_ref[...] = (sbuf[...].astype(jnp.float32) + summed2).astype(out_ref.dtype)


def tail(part, w_out, states, gain, w_gate_up, w_down, n, sn, cid):
    rows, width = states.shape
    lanes = part.shape[2] - 2
    units = w_gate_up.shape[2]
    vmem = pl.BlockSpec(memory_space=pltpu.VMEM)
    return pl.pallas_call(
        functools.partial(_tail_kernel, n, sn),
        out_shape=jax.ShapeDtypeStruct((rows, width), states.dtype),
        in_specs=[vmem] * 6,
        out_specs=vmem,
        scratch_shapes=[
            pltpu.VMEM((sn,) + part.shape, jnp.float32),
            pltpu.VMEM((n, rows, lanes), jnp.bfloat16),
            pltpu.SemaphoreType.DMA((sn,)),
            pltpu.SemaphoreType.DMA((sn,)),
            pltpu.VMEM((n * rows, lanes), jnp.bfloat16),
            pltpu.VMEM((n * rows, width), jnp.bfloat16),
            pltpu.VMEM((n, rows, width), jnp.bfloat16),
            pltpu.VMEM((rows, width), jnp.bfloat16),
            pltpu.VMEM((rows, width), jnp.bfloat16),
            pltpu.VMEM((n * rows, width), jnp.bfloat16),
            pltpu.VMEM((n * rows, width), jnp.bfloat16),
            pltpu.VMEM((n, rows, width), jnp.bfloat16),
            pltpu.SemaphoreType.DMA((4, n)),
            pltpu.SemaphoreType.DMA((4, n)),
            pltpu.SemaphoreType.DMA(()),
        ],
        compiler_params=pltpu.CompilerParams(collective_id=cid, has_side_effects=True),
    )(part, w_out, states, gain, w_gate_up.reshape(width, 2 * units), w_down)


def _head_kernel(
    n, states_ref, gains_ref, w_ref, trig_ref, qkv_ref, recv_ref, x_ref, gbuf, send_sem, recv_sem, local_sem
):
    axis = "tensor"
    me = lax.axis_index(axis)
    rows = x_ref.shape[0]
    block = qkv_ref.shape[1] // 2
    x_ref[...] = rms_norm(states_ref[...].astype(jnp.float32), gains_ref[0:1, :])
    barrier = pltpu.get_barrier_semaphore()

    def greet(d, carry):
        pl.semaphore_signal(
            barrier, 1, device_id={axis: lax.rem(me + d, n)}, device_id_type=MESH_ID
        )
        return carry

    lax.fori_loop(1, n, greet, 0)
    pl.semaphore_wait(barrier, n - 1)

    def phase(p, src_of, dst_of):
        def outgoing(d):
            j = lax.rem(me + d, n)
            return pltpu.make_async_remote_copy(
                src_ref=src_of(j),
                dst_ref=dst_of(me),
                send_sem=send_sem.at[p, j],
                recv_sem=recv_sem.at[p, me],
                device_id={axis: j},
                device_id_type=MESH_ID,
            )

        def incoming(d):
            k = lax.rem(me + n - d, n)
            return pltpu.make_async_remote_copy(
                src_ref=src_of(k),
                dst_ref=dst_of(k),
                send_sem=send_sem.at[p, k],
                recv_sem=recv_sem.at[p, k],
                device_id={axis: k},
                device_id_type=MESH_ID,
            )

        local = pltpu.make_async_copy(src_of(me), dst_of(me), local_sem)
        local.start()

        def start(d, carry):
            outgoing(d).start()
            return carry

        lax.fori_loop(1, n, start, 0)

        def finish(d, carry):
            outgoing(d).wait_send()
            incoming(d).wait_recv()
            return carry

        lax.fori_loop(1, n, finish, 0)
        local.wait()

    phase(0, lambda j: x_ref, lambda k: gbuf.at[pl.ds(k * rows, rows)])
    proj = jnp.dot(gbuf[...], w_ref[...], preferred_element_type=jnp.float32)
    trig = trig_ref[...]
    pair = proj[:, :block]
    half = HEAD_SIZE // 2
    lane = lax.broadcasted_iota(jnp.int32, pair.shape, 1)
    turned = jnp.where(
        lane % HEAD_SIZE < half,
        -pltpu.roll(pair, block - half, 1),
        pltpu.roll(pair, half, 1),
    )
    rotated = pair * trig[:, :block] + turned * trig[:, block:]
    qkv_ref[:, :block] = rotated.astype(qkv_ref.dtype)
    qkv_ref[:, block : block + block // 2] = proj[:, block:].astype(qkv_ref.dtype)
    qkv_ref[:, block + block // 2 :] = jnp.zeros((pair.shape[0], block // 2), qkv_ref.dtype)
    phase(1, lambda j: qkv_ref.at[pl.ds(j * rows, rows)], lambda k: recv_ref.at[k])


def head(states, gains, w_ext, trig, n, cid):
    rows, width = states.shape
    cols = w_ext.shape[1] // 3 * 4
    vmem = pl.BlockSpec(memory_space=pltpu.VMEM)
    return pl.pallas_call(
        functools.partial(_head_kernel, n),
        out_shape=(
            jax.ShapeDtypeStruct((n * rows, cols), jnp.bfloat16),
            jax.ShapeDtypeStruct((n, rows, cols), jnp.bfloat16),
        ),
        in_specs=[vmem] * 4,
        out_specs=(vmem, vmem),
        scratch_shapes=[
            pltpu.VMEM((rows, width), jnp.bfloat16),
            pltpu.VMEM((n * rows, width), jnp.bfloat16),
            pltpu.SemaphoreType.DMA((2, n)),
            pltpu.SemaphoreType.DMA((2, n)),
            pltpu.SemaphoreType.DMA(()),
        ],
        compiler_params=pltpu.CompilerParams(collective_id=cid, has_side_effects=True),
    )(states, gains, w_ext, trig)


def per_device(
    states,
    attn_gain,
    w_qkv,
    w_out,
    mlp_gain,
    w_gate_up,
    w_down,
    key_cache,
    value_cache,
    sink_keys,
    sink_values,
    cache_len,
    slot_mask,
    slot_pos,
    new_pos,
    tn,
    sn,
):
    rows = states.shape[0]
    width = states.shape[1]
    row_start = lax.axis_index("tensor") * rows
    floats = states.astype(jnp.float32)
    lanes = w_qkv.shape[2]
    heads_here = lanes // HEAD_SIZE
    qkv_matrix = w_qkv.reshape(width, 3 * lanes)
    half = HEAD_SIZE // 2
    inverse = jnp.exp(
        -jnp.log(jnp.float32(130000.0)) * jnp.arange(half, dtype=jnp.float32) * (2.0 / HEAD_SIZE)
    )
    angle = new_pos.astype(jnp.float32)[:, None] * inverse[None, :]
    angle = jnp.concatenate([angle] * (4 * heads_here), axis=-1)
    trig = jnp.concatenate([jnp.cos(angle), jnp.sin(angle)], axis=-1)
    gains = jnp.stack([attn_gain, mlp_gain])
    qkv_all, mine = head(states, gains, qkv_matrix, trig, tn, 0)
    batch = qkv_all.shape[0]
    keys_all = qkv_all[:, lanes : 2 * lanes]
    values_all = qkv_all[:, 2 * lanes : 3 * lanes]
    mine = mine.reshape(tn, rows, 4, heads_here, HEAD_SIZE)
    mine = jnp.transpose(mine, (1, 2, 0, 3, 4)).reshape(rows, 4, tn * heads_here, HEAD_SIZE)
    queries = mine[:, 0]
    keys_new = mine[:, 1]
    values_new = mine[:, 2]
    all_heads = queries.shape[1]
    own_len = lax.dynamic_slice_in_dim(cache_len, row_start, rows, 0)
    own_pos = lax.dynamic_slice_in_dim(new_pos, row_start, rows, 0)
    window_here = key_cache.shape[2]
    seq_index = lax.axis_index("seq")
    slots = seq_index * window_here + jnp.arange(window_here, dtype=jnp.int32)
    live = (slots[None, :] < own_len[:, None]) & (slot_mask == 1)
    live = live & (slot_pos < own_pos[:, None]) & (own_pos[:, None] - slot_pos < WINDOW)
    live = live[:, None, :]
    first_shard = seq_index == 0
    kwin = key_cache.reshape(rows, all_heads, HEAD_SIZE, window_here)
    vwin = value_cache.reshape(rows, all_heads, HEAD_SIZE, window_here)
    sink_key_rows = sink_keys.reshape(rows, all_heads, HEAD_SIZE, sink_keys.shape[2])
    vsink = sink_values.reshape(rows, all_heads, HEAD_SIZE, sink_values.shape[2])
    score_win = (
        jnp.sum(queries.astype(jnp.float32)[..., None] * kwin.astype(jnp.float32), axis=2)
        * 0.125
    )
    score_win = jnp.where(live, score_win, NEG)
    score_sink = (
        jnp.sum(
            queries.astype(jnp.float32)[..., None] * sink_key_rows.astype(jnp.float32), axis=2
        )
        * 0.125
    )
    score_sink = jnp.where(first_shard, score_sink, NEG)
    score_new = jnp.sum(queries.astype(jnp.float32) * keys_new.astype(jnp.float32), axis=-1) * 0.125
    score_new = jnp.where(first_shard, score_new, NEG)
    local_top = jnp.maximum(
        jnp.maximum(jnp.max(score_win, axis=-1), jnp.max(score_sink, axis=-1)), score_new
    )
    weight_win = jnp.where(live, jnp.exp(score_win - local_top[..., None]), 0.0)
    weight_sink = jnp.where(first_shard, jnp.exp(score_sink - local_top[..., None]), 0.0)
    weight_new = jnp.where(first_shard, jnp.exp(score_new - local_top), 0.0)
    total = jnp.sum(weight_win, axis=-1) + jnp.sum(weight_sink, axis=-1) + weight_new
    mixture = jnp.einsum(
        "bhs,bhds->bhd", weight_win.astype(jnp.bfloat16), vwin, preferred_element_type=jnp.float32
    )
    mixture = mixture + jnp.sum(
        undo_round(weight_sink)[:, :, None, :] * vsink.astype(jnp.float32), axis=-1
    )
    mixture = mixture + undo_round(weight_new)[..., None] * values_new.astype(jnp.float32)
    packed = jnp.concatenate([mixture, total[..., None], local_top[..., None]], axis=-1)
    packed = jnp.transpose(packed, (1, 0, 2))
    out_states = tail(packed, w_out, states, gains, w_gate_up, w_down, tn, sn, 3)
    return (out_states, keys_all, values_all)


def solution(mesh):
    in_specs = (
        P("tensor", None),
        P(),
        P(None, None, "tensor"),
        P("tensor", None),
        P(),
        P(None, None, "tensor"),
        P("tensor", None),
        P("tensor", None, "seq"),
        P("tensor", None, "seq"),
        P("tensor", None, None),
        P("tensor", None, None),
        P(),
        P("tensor", "seq"),
        P("tensor", "seq"),
        P(),
    )
    out_specs = (P("tensor", None), P(None, "tensor"), P(None, "tensor"))
    body = functools.partial(per_device, tn=mesh.shape["tensor"], sn=mesh.shape["seq"])
    return jax.shard_map(
        body, mesh=mesh, in_specs=in_specs, out_specs=out_specs, check_vma=False
    )
```

```python
import functools

import jax
import jax.numpy as jnp
from jax import lax
from jax.experimental import pallas as pl
from jax.experimental.pallas import tpu as pltpu
from jax.sharding import PartitionSpec as P

HEAD_SIZE = 64
WINDOW = 4096


NEG = -1e30
MESH_ID = pl.DeviceIdType.MESH


def rms_norm(values, gain):
    meansq = jnp.mean(values * values, axis=-1, keepdims=True)
    return (values * lax.rsqrt(meansq + 1e-05) * gain.astype(jnp.float32)).astype(jnp.bfloat16)


def rotary(tensor, cosine, sine):
    half = tensor.shape[-1] // 2
    turned = jnp.concatenate([-tensor[..., half:], tensor[..., :half]], axis=-1)
    return tensor * cosine + turned * sine


def undo_round(weights):
    rounded = lax.optimization_barrier(weights.astype(jnp.bfloat16))
    return rounded.astype(jnp.float32)


def _exchange_kernel(n, axis, gather, x_ref, y_ref, send_sem, recv_sem, local_sem):
    me = lax.axis_index(axis)
    barrier = pltpu.get_barrier_semaphore()

    def greet(d, carry):
        peer = lax.rem(me + d, n)
        pl.semaphore_signal(barrier, 1, device_id={axis: peer}, device_id_type=MESH_ID)
        return carry

    lax.fori_loop(1, n, greet, 0)
    pl.semaphore_wait(barrier, n - 1)

    def source(j):
        return x_ref if gather else x_ref.at[j]

    def outgoing(d):
        j = lax.rem(me + d, n)
        return pltpu.make_async_remote_copy(
            src_ref=source(j),
            dst_ref=y_ref.at[me],
            send_sem=send_sem.at[j],
            recv_sem=recv_sem.at[me],
            device_id={axis: j},
            device_id_type=MESH_ID,
        )

    def incoming(d):
        k = lax.rem(me + n - d, n)
        return pltpu.make_async_remote_copy(
            src_ref=source(k),
            dst_ref=y_ref.at[k],
            send_sem=send_sem.at[k],
            recv_sem=recv_sem.at[k],
            device_id={axis: k},
            device_id_type=MESH_ID,
        )

    local = pltpu.make_async_copy(source(me), y_ref.at[me], local_sem)
    local.start()

    def start(d, carry):
        outgoing(d).start()
        return carry

    lax.fori_loop(1, n, start, 0)

    def finish(d, carry):
        outgoing(d).wait_send()
        incoming(d).wait_recv()
        return carry

    lax.fori_loop(1, n, finish, 0)
    local.wait()


def exchange(x, axis, n, cid, gather=False):
    piece = x.shape if gather else x.shape[1:]
    return pl.pallas_call(
        functools.partial(_exchange_kernel, n, axis, gather),
        out_shape=jax.ShapeDtypeStruct((n,) + tuple(piece), x.dtype),
        in_specs=[pl.BlockSpec(memory_space=pl.ANY)],
        out_specs=pl.BlockSpec(memory_space=pl.ANY),
        scratch_shapes=[
            pltpu.SemaphoreType.DMA((n,)),
            pltpu.SemaphoreType.DMA((n,)),
            pltpu.SemaphoreType.DMA(()),
        ],
        compiler_params=pltpu.CompilerParams(collective_id=cid, has_side_effects=True),
    )(x)


def _tail_kernel(
    n,
    sn,
    part_ref,
    w_out_ref,
    states_ref,
    gain_ref,
    gate_ref,
    down_ref,
    out_ref,
    seq_buf,
    att_buf,
    seq_send,
    seq_recv,
    abuf,
    pbuf,
    rbuf,
    sbuf,
    nbuf,
    gbuf,
    qbuf,
    rbuf2,
    send_sem,
    recv_sem,
    local_sem,
):
    axis = "tensor"
    me = lax.axis_index(axis)
    seq_me = lax.axis_index("seq")
    rows = states_ref.shape[0]
    barrier = pltpu.get_barrier_semaphore()

    def greet(d, carry):
        pl.semaphore_signal(
            barrier, 1, device_id={axis: lax.rem(me + d, n)}, device_id_type=MESH_ID
        )
        return carry

    lax.fori_loop(1, n, greet, 0)

    def greet_seq(d, carry):
        pl.semaphore_signal(
            barrier, 1, device_id={"seq": lax.rem(seq_me + d, sn)}, device_id_type=MESH_ID
        )
        return carry

    lax.fori_loop(1, sn, greet_seq, 0)
    pl.semaphore_wait(barrier, n - 1 + sn - 1)

    def seq_out(d):
        j = lax.rem(seq_me + d, sn)
        return pltpu.make_async_remote_copy(
            src_ref=part_ref,
            dst_ref=seq_buf.at[seq_me],
            send_sem=seq_send.at[j],
            recv_sem=seq_recv.at[seq_me],
            device_id={"seq": j},
            device_id_type=MESH_ID,
        )

    def seq_in(d):
        k = lax.rem(seq_me + sn - d, sn)
        return pltpu.make_async_remote_copy(
            src_ref=part_ref,
            dst_ref=seq_buf.at[k],
            send_sem=seq_send.at[k],
            recv_sem=seq_recv.at[k],
            device_id={"seq": k},
            device_id_type=MESH_ID,
        )

    seq_local = pltpu.make_async_copy(part_ref, seq_buf.at[seq_me], local_sem)
    seq_local.start()

    def seq_start(d, carry):
        seq_out(d).start()
        return carry

    lax.fori_loop(1, sn, seq_start, 0)

    def seq_finish(d, carry):
        seq_out(d).wait_send()
        seq_in(d).wait_recv()
        return carry

    lax.fori_loop(1, sn, seq_finish, 0)
    seq_local.wait()
    parts = seq_buf[...]
    lanes = att_buf.shape[2]
    part_top = parts[..., lanes + 1 : lanes + 2]
    top = jnp.max(part_top, axis=0)
    scale = jnp.exp(part_top - top[None])
    total = jnp.sum(parts[..., lanes : lanes + 1] * scale, axis=0)
    mixture = jnp.sum(parts[..., :lanes] * scale, axis=0)
    att_buf[...] = (mixture / total).astype(att_buf.dtype)
    units = down_ref.shape[0]

    def phase(p, src_of, dst_of):
        def outgoing(d):
            j = lax.rem(me + d, n)
            return pltpu.make_async_remote_copy(
                src_ref=src_of(j),
                dst_ref=dst_of(me),
                send_sem=send_sem.at[p, j],
                recv_sem=recv_sem.at[p, me],
                device_id={axis: j},
                device_id_type=MESH_ID,
            )

        def incoming(d):
            k = lax.rem(me + n - d, n)
            return pltpu.make_async_remote_copy(
                src_ref=src_of(k),
                dst_ref=dst_of(k),
                send_sem=send_sem.at[p, k],
                recv_sem=recv_sem.at[p, k],
                device_id={axis: k},
                device_id_type=MESH_ID,
            )

        local = pltpu.make_async_copy(src_of(me), dst_of(me), local_sem)
        local.start()

        def start(d, carry):
            outgoing(d).start()
            return carry

        lax.fori_loop(1, n, start, 0)

        def finish(d, carry):
            outgoing(d).wait_send()
            incoming(d).wait_recv()
            return carry

        lax.fori_loop(1, n, finish, 0)
        local.wait()

    def row_block(ref):
        return lambda i: ref.at[pl.ds(i * rows, rows)]

    phase(0, lambda j: att_buf.at[j], row_block(abuf))
    partial = jnp.dot(abuf[...], w_out_ref[...], preferred_element_type=jnp.float32)
    pbuf[...] = partial.astype(jnp.bfloat16)
    phase(1, row_block(pbuf), lambda k: rbuf.at[k])
    summed = jnp.sum(rbuf[...].astype(jnp.float32), axis=0)
    resid = (states_ref[...].astype(jnp.float32) + summed).astype(jnp.bfloat16)
    sbuf[...] = resid
    nbuf[...] = rms_norm(resid.astype(jnp.float32), gain_ref[...].reshape(1, -1))
    phase(2, lambda j: nbuf, row_block(gbuf))
    gate_up = jnp.dot(gbuf[...], gate_ref[...], preferred_element_type=jnp.float32)
    hidden = (jax.nn.silu(gate_up[:, :units]) * gate_up[:, units:]).astype(jnp.bfloat16)
    down = jnp.dot(hidden, down_ref[...], preferred_element_type=jnp.float32)
    qbuf[...] = down.astype(jnp.bfloat16)
    phase(3, row_block(qbuf), lambda k: rbuf2.at[k])
    summed2 = jnp.sum(rbuf2[...].astype(jnp.float32), axis=0)
    out_ref[...] = (sbuf[...].astype(jnp.float32) + summed2).astype(out_ref.dtype)


def tail(part, w_out, states, gain, w_gate_up, w_down, n, sn, cid):
    rows, width = states.shape
    lanes = part.shape[2] - 2
    units = w_gate_up.shape[2]
    vmem = pl.BlockSpec(memory_space=pltpu.VMEM)
    return pl.pallas_call(
        functools.partial(_tail_kernel, n, sn),
        out_shape=jax.ShapeDtypeStruct((rows, width), states.dtype),
        in_specs=[vmem] * 6,
        out_specs=vmem,
        scratch_shapes=[
            pltpu.VMEM((sn,) + part.shape, jnp.float32),
            pltpu.VMEM((n, rows, lanes), jnp.bfloat16),
            pltpu.SemaphoreType.DMA((sn,)),
            pltpu.SemaphoreType.DMA((sn,)),
            pltpu.VMEM((n * rows, lanes), jnp.bfloat16),
            pltpu.VMEM((n * rows, width), jnp.bfloat16),
            pltpu.VMEM((n, rows, width), jnp.bfloat16),
            pltpu.VMEM((rows, width), jnp.bfloat16),
            pltpu.VMEM((rows, width), jnp.bfloat16),
            pltpu.VMEM((n * rows, width), jnp.bfloat16),
            pltpu.VMEM((n * rows, width), jnp.bfloat16),
            pltpu.VMEM((n, rows, width), jnp.bfloat16),
            pltpu.SemaphoreType.DMA((4, n)),
            pltpu.SemaphoreType.DMA((4, n)),
            pltpu.SemaphoreType.DMA(()),
        ],
        compiler_params=pltpu.CompilerParams(collective_id=cid, has_side_effects=True),
    )(part, w_out, states, gain, w_gate_up.reshape(width, 2 * units), w_down)


def _head_kernel(
    n, states_ref, gains_ref, w_ref, trig_ref, qkv_ref, recv_ref, x_ref, gbuf, send_sem, recv_sem, local_sem
):
    axis = "tensor"
    me = lax.axis_index(axis)
    rows = x_ref.shape[0]
    block = qkv_ref.shape[1] // 2
    x_ref[...] = rms_norm(states_ref[...].astype(jnp.float32), gains_ref[...].reshape(1, -1))
    barrier = pltpu.get_barrier_semaphore()

    def greet(d, carry):
        pl.semaphore_signal(
            barrier, 1, device_id={axis: lax.rem(me + d, n)}, device_id_type=MESH_ID
        )
        return carry

    lax.fori_loop(1, n, greet, 0)
    pl.semaphore_wait(barrier, n - 1)

    def phase(p, src_of, dst_of):
        def outgoing(d):
            j = lax.rem(me + d, n)
            return pltpu.make_async_remote_copy(
                src_ref=src_of(j),
                dst_ref=dst_of(me),
                send_sem=send_sem.at[p, j],
                recv_sem=recv_sem.at[p, me],
                device_id={axis: j},
                device_id_type=MESH_ID,
            )

        def incoming(d):
            k = lax.rem(me + n - d, n)
            return pltpu.make_async_remote_copy(
                src_ref=src_of(k),
                dst_ref=dst_of(k),
                send_sem=send_sem.at[p, k],
                recv_sem=recv_sem.at[p, k],
                device_id={axis: k},
                device_id_type=MESH_ID,
            )

        local = pltpu.make_async_copy(src_of(me), dst_of(me), local_sem)
        local.start()

        def start(d, carry):
            outgoing(d).start()
            return carry

        lax.fori_loop(1, n, start, 0)

        def finish(d, carry):
            outgoing(d).wait_send()
            incoming(d).wait_recv()
            return carry

        lax.fori_loop(1, n, finish, 0)
        local.wait()

    phase(0, lambda j: x_ref, lambda k: gbuf.at[pl.ds(k * rows, rows)])
    proj = jnp.dot(gbuf[...], w_ref[...], preferred_element_type=jnp.float32)
    trig = trig_ref[...]
    pair = proj[:, :block]
    half = HEAD_SIZE // 2
    lane = lax.broadcasted_iota(jnp.int32, pair.shape, 1)
    turned = jnp.where(
        lane % HEAD_SIZE < half,
        -pltpu.roll(pair, block - half, 1),
        pltpu.roll(pair, half, 1),
    )
    rotated = pair * trig[:, :block] + turned * trig[:, block:]
    qkv_ref[:, :block] = rotated.astype(qkv_ref.dtype)
    qkv_ref[:, block : block + block // 2] = proj[:, block:].astype(qkv_ref.dtype)
    qkv_ref[:, block + block // 2 :] = jnp.zeros((pair.shape[0], block // 2), qkv_ref.dtype)
    phase(1, lambda j: qkv_ref.at[pl.ds(j * rows, rows)], lambda k: recv_ref.at[k])


def head(states, gains, w_ext, trig, n, cid):
    rows, width = states.shape
    cols = w_ext.shape[1] // 3 * 4
    vmem = pl.BlockSpec(memory_space=pltpu.VMEM)
    return pl.pallas_call(
        functools.partial(_head_kernel, n),
        out_shape=(
            jax.ShapeDtypeStruct((n * rows, cols), jnp.bfloat16),
            jax.ShapeDtypeStruct((n, rows, cols), jnp.bfloat16),
        ),
        in_specs=[vmem] * 4,
        out_specs=(vmem, vmem),
        scratch_shapes=[
            pltpu.VMEM((rows, width), jnp.bfloat16),
            pltpu.VMEM((n * rows, width), jnp.bfloat16),
            pltpu.SemaphoreType.DMA((2, n)),
            pltpu.SemaphoreType.DMA((2, n)),
            pltpu.SemaphoreType.DMA(()),
        ],
        compiler_params=pltpu.CompilerParams(collective_id=cid, has_side_effects=True),
    )(states, gains, w_ext, trig)


def per_device(
    states,
    attn_gain,
    w_qkv,
    w_out,
    mlp_gain,
    w_gate_up,
    w_down,
    key_cache,
    value_cache,
    sink_keys,
    sink_values,
    cache_len,
    slot_mask,
    slot_pos,
    new_pos,
    tn,
    sn,
):
    rows = states.shape[0]
    width = states.shape[1]
    row_start = lax.axis_index("tensor") * rows
    floats = states.astype(jnp.float32)
    lanes = w_qkv.shape[2]
    heads_here = lanes // HEAD_SIZE
    qkv_matrix = w_qkv.reshape(width, 3 * lanes)
    half = HEAD_SIZE // 2
    inverse = jnp.exp(
        -jnp.log(jnp.float32(130000.0)) * jnp.arange(half, dtype=jnp.float32) * (2.0 / HEAD_SIZE)
    )
    angle = new_pos.astype(jnp.float32)[:, None] * inverse[None, :]
    angle = jnp.concatenate([angle] * (4 * heads_here), axis=-1)
    trig = jnp.concatenate([jnp.cos(angle), jnp.sin(angle)], axis=-1)
    qkv_all, mine = head(states, attn_gain, qkv_matrix, trig, tn, 0)
    batch = qkv_all.shape[0]
    keys_all = qkv_all[:, lanes : 2 * lanes]
    values_all = qkv_all[:, 2 * lanes : 3 * lanes]
    mine = mine.reshape(tn, rows, 4, heads_here, HEAD_SIZE)
    mine = jnp.transpose(mine, (1, 2, 0, 3, 4)).reshape(rows, 4, tn * heads_here, HEAD_SIZE)
    queries = mine[:, 0]
    keys_new = mine[:, 1]
    values_new = mine[:, 2]
    all_heads = queries.shape[1]
    own_len = lax.dynamic_slice_in_dim(cache_len, row_start, rows, 0)
    own_pos = lax.dynamic_slice_in_dim(new_pos, row_start, rows, 0)
    window_here = key_cache.shape[2]
    seq_index = lax.axis_index("seq")
    slots = seq_index * window_here + jnp.arange(window_here, dtype=jnp.int32)
    live = (slots[None, :] < own_len[:, None]) & (slot_mask == 1)
    live = live & (slot_pos < own_pos[:, None]) & (own_pos[:, None] - slot_pos < WINDOW)
    live = live[:, None, :]
    first_shard = seq_index == 0
    kwin = key_cache.reshape(rows, all_heads, HEAD_SIZE, window_here)
    vwin = value_cache.reshape(rows, all_heads, HEAD_SIZE, window_here)
    sink_key_rows = sink_keys.reshape(rows, all_heads, HEAD_SIZE, sink_keys.shape[2])
    vsink = sink_values.reshape(rows, all_heads, HEAD_SIZE, sink_values.shape[2])
    score_win = (
        jnp.einsum("bhd,bhds->bhs", queries, kwin, preferred_element_type=jnp.float32) * 0.125
    )
    score_win = jnp.where(live, score_win, NEG)
    score_sink = (
        jnp.sum(
            queries.astype(jnp.float32)[..., None] * sink_key_rows.astype(jnp.float32), axis=2
        )
        * 0.125
    )
    score_sink = jnp.where(first_shard, score_sink, NEG)
    score_new = jnp.sum(queries.astype(jnp.float32) * keys_new.astype(jnp.float32), axis=-1) * 0.125
    score_new = jnp.where(first_shard, score_new, NEG)
    local_top = jnp.maximum(
        jnp.maximum(jnp.max(score_win, axis=-1), jnp.max(score_sink, axis=-1)), score_new
    )
    weight_win = jnp.where(live, jnp.exp(score_win - local_top[..., None]), 0.0)
    weight_sink = jnp.where(first_shard, jnp.exp(score_sink - local_top[..., None]), 0.0)
    weight_new = jnp.where(first_shard, jnp.exp(score_new - local_top), 0.0)
    total = jnp.sum(weight_win, axis=-1) + jnp.sum(weight_sink, axis=-1) + weight_new
    mixture = jnp.einsum(
        "bhs,bhds->bhd", weight_win.astype(jnp.bfloat16), vwin, preferred_element_type=jnp.float32
    )
    mixture = mixture + jnp.sum(
        undo_round(weight_sink)[:, :, None, :] * vsink.astype(jnp.float32), axis=-1
    )
    mixture = mixture + undo_round(weight_new)[..., None] * values_new.astype(jnp.float32)
    packed = jnp.concatenate([mixture, total[..., None], local_top[..., None]], axis=-1)
    packed = jnp.transpose(packed, (1, 0, 2))
    out_states = tail(packed, w_out, states, mlp_gain, w_gate_up, w_down, tn, sn, 3)
    return (out_states, keys_all, values_all)


def solution(mesh):
    in_specs = (
        P("tensor", None),
        P(),
        P(None, None, "tensor"),
        P("tensor", None),
        P(),
        P(None, None, "tensor"),
        P("tensor", None),
        P("tensor", None, "seq"),
        P("tensor", None, "seq"),
        P("tensor", None, None),
        P("tensor", None, None),
        P(),
        P("tensor", "seq"),
        P("tensor", "seq"),
        P(),
    )
    out_specs = (P("tensor", None), P(None, "tensor"), P(None, "tensor"))
    body = functools.partial(per_device, tn=mesh.shape["tensor"], sn=mesh.shape["seq"])
    return jax.shard_map(
        body, mesh=mesh, in_specs=in_specs, out_specs=out_specs, check_vma=False
    )
```

```python
import functools

import jax
import jax.numpy as jnp
from jax import lax
from jax.experimental import pallas as pl
from jax.experimental.pallas import tpu as pltpu
from jax.sharding import PartitionSpec as P

HEAD_SIZE = 64
WINDOW = 4096


NEG = -1e30
MESH_ID = pl.DeviceIdType.MESH


def rms_norm(values, gain):
    meansq = jnp.mean(values * values, axis=-1, keepdims=True)
    return (values * lax.rsqrt(meansq + 1e-05) * gain.astype(jnp.float32)).astype(jnp.bfloat16)


def rotary(tensor, cosine, sine):
    half = tensor.shape[-1] // 2
    turned = jnp.concatenate([-tensor[..., half:], tensor[..., :half]], axis=-1)
    return tensor * cosine + turned * sine


def undo_round(weights):
    rounded = lax.optimization_barrier(weights.astype(jnp.bfloat16))
    return rounded.astype(jnp.float32)


def _exchange_kernel(n, axis, gather, x_ref, y_ref, send_sem, recv_sem, local_sem):
    me = lax.axis_index(axis)
    barrier = pltpu.get_barrier_semaphore()

    def greet(d, carry):
        peer = lax.rem(me + d, n)
        pl.semaphore_signal(barrier, 1, device_id={axis: peer}, device_id_type=MESH_ID)
        return carry

    lax.fori_loop(1, n, greet, 0)
    pl.semaphore_wait(barrier, n - 1)

    def source(j):
        return x_ref if gather else x_ref.at[j]

    def outgoing(d):
        j = lax.rem(me + d, n)
        return pltpu.make_async_remote_copy(
            src_ref=source(j),
            dst_ref=y_ref.at[me],
            send_sem=send_sem.at[j],
            recv_sem=recv_sem.at[me],
            device_id={axis: j},
            device_id_type=MESH_ID,
        )

    def incoming(d):
        k = lax.rem(me + n - d, n)
        return pltpu.make_async_remote_copy(
            src_ref=source(k),
            dst_ref=y_ref.at[k],
            send_sem=send_sem.at[k],
            recv_sem=recv_sem.at[k],
            device_id={axis: k},
            device_id_type=MESH_ID,
        )

    local = pltpu.make_async_copy(source(me), y_ref.at[me], local_sem)
    local.start()

    def start(d, carry):
        outgoing(d).start()
        return carry

    lax.fori_loop(1, n, start, 0)

    def finish(d, carry):
        outgoing(d).wait_send()
        incoming(d).wait_recv()
        return carry

    lax.fori_loop(1, n, finish, 0)
    local.wait()


def exchange(x, axis, n, cid, gather=False):
    piece = x.shape if gather else x.shape[1:]
    return pl.pallas_call(
        functools.partial(_exchange_kernel, n, axis, gather),
        out_shape=jax.ShapeDtypeStruct((n,) + tuple(piece), x.dtype),
        in_specs=[pl.BlockSpec(memory_space=pl.ANY)],
        out_specs=pl.BlockSpec(memory_space=pl.ANY),
        scratch_shapes=[
            pltpu.SemaphoreType.DMA((n,)),
            pltpu.SemaphoreType.DMA((n,)),
            pltpu.SemaphoreType.DMA(()),
        ],
        compiler_params=pltpu.CompilerParams(collective_id=cid, has_side_effects=True),
    )(x)


def _tail_kernel(
    n,
    sn,
    part_ref,
    w_out_ref,
    states_ref,
    gain_ref,
    gate_ref,
    down_ref,
    out_ref,
    seq_buf,
    att_buf,
    seq_send,
    seq_recv,
    abuf,
    pbuf,
    rbuf,
    sbuf,
    nbuf,
    gbuf,
    qbuf,
    rbuf2,
    send_sem,
    recv_sem,
    local_sem,
):
    axis = "tensor"
    me = lax.axis_index(axis)
    seq_me = lax.axis_index("seq")
    rows = states_ref.shape[0]
    barrier = pltpu.get_barrier_semaphore()

    def greet(d, carry):
        pl.semaphore_signal(
            barrier, 1, device_id={axis: lax.rem(me + d, n)}, device_id_type=MESH_ID
        )
        return carry

    lax.fori_loop(1, n, greet, 0)

    def greet_seq(d, carry):
        pl.semaphore_signal(
            barrier, 1, device_id={"seq": lax.rem(seq_me + d, sn)}, device_id_type=MESH_ID
        )
        return carry

    lax.fori_loop(1, sn, greet_seq, 0)
    pl.semaphore_wait(barrier, n - 1 + sn - 1)

    def seq_out(d):
        j = lax.rem(seq_me + d, sn)
        return pltpu.make_async_remote_copy(
            src_ref=part_ref,
            dst_ref=seq_buf.at[seq_me],
            send_sem=seq_send.at[j],
            recv_sem=seq_recv.at[seq_me],
            device_id={"seq": j},
            device_id_type=MESH_ID,
        )

    def seq_in(d):
        k = lax.rem(seq_me + sn - d, sn)
        return pltpu.make_async_remote_copy(
            src_ref=part_ref,
            dst_ref=seq_buf.at[k],
            send_sem=seq_send.at[k],
            recv_sem=seq_recv.at[k],
            device_id={"seq": k},
            device_id_type=MESH_ID,
        )

    seq_local = pltpu.make_async_copy(part_ref, seq_buf.at[seq_me], local_sem)
    seq_local.start()

    def seq_start(d, carry):
        seq_out(d).start()
        return carry

    lax.fori_loop(1, sn, seq_start, 0)

    def seq_finish(d, carry):
        seq_out(d).wait_send()
        seq_in(d).wait_recv()
        return carry

    lax.fori_loop(1, sn, seq_finish, 0)
    seq_local.wait()
    parts = seq_buf[...]
    lanes = att_buf.shape[2]
    part_top = parts[..., lanes + 1 : lanes + 2]
    top = jnp.max(part_top, axis=0)
    scale = jnp.exp(part_top - top[None])
    total = jnp.sum(parts[..., lanes : lanes + 1] * scale, axis=0)
    mixture = jnp.sum(parts[..., :lanes] * scale, axis=0)
    att_buf[...] = (mixture / total).astype(att_buf.dtype)
    units = down_ref.shape[0]

    def phase(p, src_of, dst_of):
        def outgoing(d):
            j = lax.rem(me + d, n)
            return pltpu.make_async_remote_copy(
                src_ref=src_of(j),
                dst_ref=dst_of(me),
                send_sem=send_sem.at[p, j],
                recv_sem=recv_sem.at[p, me],
                device_id={axis: j},
                device_id_type=MESH_ID,
            )

        def incoming(d):
            k = lax.rem(me + n - d, n)
            return pltpu.make_async_remote_copy(
                src_ref=src_of(k),
                dst_ref=dst_of(k),
                send_sem=send_sem.at[p, k],
                recv_sem=recv_sem.at[p, k],
                device_id={axis: k},
                device_id_type=MESH_ID,
            )

        local = pltpu.make_async_copy(src_of(me), dst_of(me), local_sem)
        local.start()

        def start(d, carry):
            outgoing(d).start()
            return carry

        lax.fori_loop(1, n, start, 0)

        def finish(d, carry):
            outgoing(d).wait_send()
            incoming(d).wait_recv()
            return carry

        lax.fori_loop(1, n, finish, 0)
        local.wait()

    def row_block(ref):
        return lambda i: ref.at[pl.ds(i * rows, rows)]

    phase(0, lambda j: att_buf.at[j], row_block(abuf))
    partial = jnp.dot(abuf[...], w_out_ref[...], preferred_element_type=jnp.float32)
    pbuf[...] = partial.astype(jnp.bfloat16)
    phase(1, row_block(pbuf), lambda k: rbuf.at[k])
    summed = jnp.sum(rbuf[...].astype(jnp.float32), axis=0)
    resid = (states_ref[...].astype(jnp.float32) + summed).astype(jnp.bfloat16)
    sbuf[...] = resid
    nbuf[...] = rms_norm(resid.astype(jnp.float32), gain_ref[...].reshape(1, -1))
    phase(2, lambda j: nbuf, row_block(gbuf))
    gate_up = jnp.dot(gbuf[...], gate_ref[...], preferred_element_type=jnp.float32)
    hidden = (jax.nn.silu(gate_up[:, :units]) * gate_up[:, units:]).astype(jnp.bfloat16)
    down = jnp.dot(hidden, down_ref[...], preferred_element_type=jnp.float32)
    qbuf[...] = down.astype(jnp.bfloat16)
    phase(3, row_block(qbuf), lambda k: rbuf2.at[k])
    summed2 = jnp.sum(rbuf2[...].astype(jnp.float32), axis=0)
    out_ref[...] = (sbuf[...].astype(jnp.float32) + summed2).astype(out_ref.dtype)


def tail(part, w_out, states, gain, w_gate_up, w_down, n, sn, cid):
    rows, width = states.shape
    lanes = part.shape[2] - 2
    units = w_gate_up.shape[2]
    vmem = pl.BlockSpec(memory_space=pltpu.VMEM)
    return pl.pallas_call(
        functools.partial(_tail_kernel, n, sn),
        out_shape=jax.ShapeDtypeStruct((rows, width), states.dtype),
        in_specs=[vmem] * 6,
        out_specs=vmem,
        scratch_shapes=[
            pltpu.VMEM((sn,) + part.shape, jnp.float32),
            pltpu.VMEM((n, rows, lanes), jnp.bfloat16),
            pltpu.SemaphoreType.DMA((sn,)),
            pltpu.SemaphoreType.DMA((sn,)),
            pltpu.VMEM((n * rows, lanes), jnp.bfloat16),
            pltpu.VMEM((n * rows, width), jnp.bfloat16),
            pltpu.VMEM((n, rows, width), jnp.bfloat16),
            pltpu.VMEM((rows, width), jnp.bfloat16),
            pltpu.VMEM((rows, width), jnp.bfloat16),
            pltpu.VMEM((n * rows, width), jnp.bfloat16),
            pltpu.VMEM((n * rows, width), jnp.bfloat16),
            pltpu.VMEM((n, rows, width), jnp.bfloat16),
            pltpu.SemaphoreType.DMA((4, n)),
            pltpu.SemaphoreType.DMA((4, n)),
            pltpu.SemaphoreType.DMA(()),
        ],
        compiler_params=pltpu.CompilerParams(collective_id=cid, has_side_effects=True),
    )(part, w_out, states, gain, w_gate_up.reshape(width, 2 * units), w_down)


def _head_kernel(
    n, states_ref, gains_ref, w_ref, trig_ref, qkv_ref, recv_ref, x_ref, gbuf, send_sem, recv_sem, local_sem
):
    axis = "tensor"
    me = lax.axis_index(axis)
    rows = x_ref.shape[0]
    block = qkv_ref.shape[1] // 2
    x_ref[...] = rms_norm(states_ref[...].astype(jnp.float32), gains_ref[...].reshape(1, -1))
    barrier = pltpu.get_barrier_semaphore()

    def greet(d, carry):
        pl.semaphore_signal(
            barrier, 1, device_id={axis: lax.rem(me + d, n)}, device_id_type=MESH_ID
        )
        return carry

    lax.fori_loop(1, n, greet, 0)
    pl.semaphore_wait(barrier, n - 1)

    def phase(p, src_of, dst_of):
        def outgoing(d):
            j = lax.rem(me + d, n)
            return pltpu.make_async_remote_copy(
                src_ref=src_of(j),
                dst_ref=dst_of(me),
                send_sem=send_sem.at[p, j],
                recv_sem=recv_sem.at[p, me],
                device_id={axis: j},
                device_id_type=MESH_ID,
            )

        def incoming(d):
            k = lax.rem(me + n - d, n)
            return pltpu.make_async_remote_copy(
                src_ref=src_of(k),
                dst_ref=dst_of(k),
                send_sem=send_sem.at[p, k],
                recv_sem=recv_sem.at[p, k],
                device_id={axis: k},
                device_id_type=MESH_ID,
            )

        local = pltpu.make_async_copy(src_of(me), dst_of(me), local_sem)
        local.start()

        def start(d, carry):
            outgoing(d).start()
            return carry

        lax.fori_loop(1, n, start, 0)

        def finish(d, carry):
            outgoing(d).wait_send()
            incoming(d).wait_recv()
            return carry

        lax.fori_loop(1, n, finish, 0)
        local.wait()

    phase(0, lambda j: x_ref, lambda k: gbuf.at[pl.ds(k * rows, rows)])
    lanes = w_ref.shape[1]
    gathered = gbuf[...]
    contract_last = (((1,), (1,)), ((), ()))
    pair = lax.dot_general(
        gathered,
        w_ref[0:2].reshape(2 * lanes, w_ref.shape[2]),
        contract_last,
        preferred_element_type=jnp.float32,
    )
    value_proj = lax.dot_general(
        gathered, w_ref[2], contract_last, preferred_element_type=jnp.float32
    )
    trig = trig_ref[...]
    half = HEAD_SIZE // 2
    lane = lax.broadcasted_iota(jnp.int32, pair.shape, 1)
    turned = jnp.where(
        lane % HEAD_SIZE < half,
        -pltpu.roll(pair, block - half, 1),
        pltpu.roll(pair, half, 1),
    )
    rotated = pair * trig[:, :block] + turned * trig[:, block:]
    qkv_ref[:, :block] = rotated.astype(qkv_ref.dtype)
    qkv_ref[:, block : block + block // 2] = value_proj.astype(qkv_ref.dtype)
    qkv_ref[:, block + block // 2 :] = jnp.zeros((pair.shape[0], block // 2), qkv_ref.dtype)
    phase(1, lambda j: qkv_ref.at[pl.ds(j * rows, rows)], lambda k: recv_ref.at[k])


def head(states, gains, w_ext, trig, n, cid):
    rows, width = states.shape
    cols = w_ext.shape[1] * 4
    vmem = pl.BlockSpec(memory_space=pltpu.VMEM)
    return pl.pallas_call(
        functools.partial(_head_kernel, n),
        out_shape=(
            jax.ShapeDtypeStruct((n * rows, cols), jnp.bfloat16),
            jax.ShapeDtypeStruct((n, rows, cols), jnp.bfloat16),
        ),
        in_specs=[vmem] * 4,
        out_specs=(vmem, vmem),
        scratch_shapes=[
            pltpu.VMEM((rows, width), jnp.bfloat16),
            pltpu.VMEM((n * rows, width), jnp.bfloat16),
            pltpu.SemaphoreType.DMA((2, n)),
            pltpu.SemaphoreType.DMA((2, n)),
            pltpu.SemaphoreType.DMA(()),
        ],
        compiler_params=pltpu.CompilerParams(collective_id=cid, has_side_effects=True),
    )(states, gains, w_ext, trig)


def per_device(
    states,
    attn_gain,
    w_qkv,
    w_out,
    mlp_gain,
    w_gate_up,
    w_down,
    key_cache,
    value_cache,
    sink_keys,
    sink_values,
    cache_len,
    slot_mask,
    slot_pos,
    new_pos,
    tn,
    sn,
):
    rows = states.shape[0]
    width = states.shape[1]
    row_start = lax.axis_index("tensor") * rows
    floats = states.astype(jnp.float32)
    lanes = w_qkv.shape[2]
    heads_here = lanes // HEAD_SIZE
    half = HEAD_SIZE // 2
    inverse = jnp.exp(
        -jnp.log(jnp.float32(130000.0)) * jnp.arange(half, dtype=jnp.float32) * (2.0 / HEAD_SIZE)
    )
    angle = new_pos.astype(jnp.float32)[:, None] * inverse[None, :]
    angle = jnp.concatenate([angle] * (4 * heads_here), axis=-1)
    trig = jnp.concatenate([jnp.cos(angle), jnp.sin(angle)], axis=-1)
    qkv_all, mine = head(states, attn_gain, jnp.transpose(w_qkv, (1, 2, 0)), trig, tn, 0)
    batch = qkv_all.shape[0]
    keys_all = qkv_all[:, lanes : 2 * lanes]
    values_all = qkv_all[:, 2 * lanes : 3 * lanes]
    mine = mine.reshape(tn, rows, 4, heads_here, HEAD_SIZE)
    mine = jnp.transpose(mine, (1, 2, 0, 3, 4)).reshape(rows, 4, tn * heads_here, HEAD_SIZE)
    queries = mine[:, 0]
    keys_new = mine[:, 1]
    values_new = mine[:, 2]
    all_heads = queries.shape[1]
    own_len = lax.dynamic_slice_in_dim(cache_len, row_start, rows, 0)
    own_pos = lax.dynamic_slice_in_dim(new_pos, row_start, rows, 0)
    window_here = key_cache.shape[2]
    seq_index = lax.axis_index("seq")
    slots = seq_index * window_here + jnp.arange(window_here, dtype=jnp.int32)
    live = (slots[None, :] < own_len[:, None]) & (slot_mask == 1)
    live = live & (slot_pos < own_pos[:, None]) & (own_pos[:, None] - slot_pos < WINDOW)
    live = live[:, None, :]
    first_shard = seq_index == 0
    kwin = key_cache.reshape(rows, all_heads, HEAD_SIZE, window_here)
    vwin = value_cache.reshape(rows, all_heads, HEAD_SIZE, window_here)
    sink_key_rows = sink_keys.reshape(rows, all_heads, HEAD_SIZE, sink_keys.shape[2])
    vsink = sink_values.reshape(rows, all_heads, HEAD_SIZE, sink_values.shape[2])
    score_win = (
        jnp.einsum("bhd,bhds->bhs", queries, kwin, preferred_element_type=jnp.float32) * 0.125
    )
    score_win = jnp.where(live, score_win, NEG)
    score_sink = (
        jnp.sum(
            queries.astype(jnp.float32)[..., None] * sink_key_rows.astype(jnp.float32), axis=2
        )
        * 0.125
    )
    score_sink = jnp.where(first_shard, score_sink, NEG)
    score_new = jnp.sum(queries.astype(jnp.float32) * keys_new.astype(jnp.float32), axis=-1) * 0.125
    score_new = jnp.where(first_shard, score_new, NEG)
    local_top = jnp.maximum(
        jnp.maximum(jnp.max(score_win, axis=-1), jnp.max(score_sink, axis=-1)), score_new
    )
    weight_win = jnp.where(live, jnp.exp(score_win - local_top[..., None]), 0.0)
    weight_sink = jnp.where(first_shard, jnp.exp(score_sink - local_top[..., None]), 0.0)
    weight_new = jnp.where(first_shard, jnp.exp(score_new - local_top), 0.0)
    total = jnp.sum(weight_win, axis=-1) + jnp.sum(weight_sink, axis=-1) + weight_new
    mixture = jnp.einsum(
        "bhs,bhds->bhd", weight_win.astype(jnp.bfloat16), vwin, preferred_element_type=jnp.float32
    )
    mixture = mixture + jnp.sum(
        undo_round(weight_sink)[:, :, None, :] * vsink.astype(jnp.float32), axis=-1
    )
    mixture = mixture + undo_round(weight_new)[..., None] * values_new.astype(jnp.float32)
    packed = jnp.concatenate([mixture, total[..., None], local_top[..., None]], axis=-1)
    packed = jnp.transpose(packed, (1, 0, 2))
    out_states = tail(packed, w_out, states, mlp_gain, w_gate_up, w_down, tn, sn, 3)
    return (out_states, keys_all, values_all)


def solution(mesh):
    in_specs = (
        P("tensor", None),
        P(),
        P(None, None, "tensor"),
        P("tensor", None),
        P(),
        P(None, None, "tensor"),
        P("tensor", None),
        P("tensor", None, "seq"),
        P("tensor", None, "seq"),
        P("tensor", None, None),
        P("tensor", None, None),
        P(),
        P("tensor", "seq"),
        P("tensor", "seq"),
        P(),
    )
    out_specs = (P("tensor", None), P(None, "tensor"), P(None, "tensor"))
    body = functools.partial(per_device, tn=mesh.shape["tensor"], sn=mesh.shape["seq"])
    return jax.shard_map(
        body, mesh=mesh, in_specs=in_specs, out_specs=out_specs, check_vma=False
    )
```

```python
import functools

import jax
import jax.numpy as jnp
from jax import lax
from jax.experimental import pallas as pl
from jax.experimental.pallas import tpu as pltpu
from jax.sharding import PartitionSpec as P

HEAD_SIZE = 64
WINDOW = 4096


NEG = -1e30
MESH_ID = pl.DeviceIdType.MESH


def rms_norm(values, gain):
    meansq = jnp.mean(values * values, axis=-1, keepdims=True)
    return (values * lax.rsqrt(meansq + 1e-05) * gain.astype(jnp.float32)).astype(jnp.bfloat16)


def rotary(tensor, cosine, sine):
    half = tensor.shape[-1] // 2
    turned = jnp.concatenate([-tensor[..., half:], tensor[..., :half]], axis=-1)
    return tensor * cosine + turned * sine


def undo_round(weights):
    rounded = lax.optimization_barrier(weights.astype(jnp.bfloat16))
    return rounded.astype(jnp.float32)


def _exchange_kernel(n, axis, gather, x_ref, y_ref, send_sem, recv_sem, local_sem):
    me = lax.axis_index(axis)
    barrier = pltpu.get_barrier_semaphore()

    def greet(d, carry):
        peer = lax.rem(me + d, n)
        pl.semaphore_signal(barrier, 1, device_id={axis: peer}, device_id_type=MESH_ID)
        return carry

    lax.fori_loop(1, n, greet, 0)
    pl.semaphore_wait(barrier, n - 1)

    def source(j):
        return x_ref if gather else x_ref.at[j]

    def outgoing(d):
        j = lax.rem(me + d, n)
        return pltpu.make_async_remote_copy(
            src_ref=source(j),
            dst_ref=y_ref.at[me],
            send_sem=send_sem.at[j],
            recv_sem=recv_sem.at[me],
            device_id={axis: j},
            device_id_type=MESH_ID,
        )

    def incoming(d):
        k = lax.rem(me + n - d, n)
        return pltpu.make_async_remote_copy(
            src_ref=source(k),
            dst_ref=y_ref.at[k],
            send_sem=send_sem.at[k],
            recv_sem=recv_sem.at[k],
            device_id={axis: k},
            device_id_type=MESH_ID,
        )

    local = pltpu.make_async_copy(source(me), y_ref.at[me], local_sem)
    local.start()

    def start(d, carry):
        outgoing(d).start()
        return carry

    lax.fori_loop(1, n, start, 0)

    def finish(d, carry):
        outgoing(d).wait_send()
        incoming(d).wait_recv()
        return carry

    lax.fori_loop(1, n, finish, 0)
    local.wait()


def exchange(x, axis, n, cid, gather=False):
    piece = x.shape if gather else x.shape[1:]
    return pl.pallas_call(
        functools.partial(_exchange_kernel, n, axis, gather),
        out_shape=jax.ShapeDtypeStruct((n,) + tuple(piece), x.dtype),
        in_specs=[pl.BlockSpec(memory_space=pl.ANY)],
        out_specs=pl.BlockSpec(memory_space=pl.ANY),
        scratch_shapes=[
            pltpu.SemaphoreType.DMA((n,)),
            pltpu.SemaphoreType.DMA((n,)),
            pltpu.SemaphoreType.DMA(()),
        ],
        compiler_params=pltpu.CompilerParams(collective_id=cid, has_side_effects=True),
    )(x)


def _tail_kernel(
    n,
    sn,
    part_ref,
    w_out_ref,
    states_ref,
    gain_ref,
    gate_ref,
    down_ref,
    out_ref,
    seq_buf,
    att_buf,
    seq_send,
    seq_recv,
    abuf,
    pbuf,
    rbuf,
    sbuf,
    nbuf,
    gbuf,
    qbuf,
    rbuf2,
    send_sem,
    recv_sem,
    local_sem,
):
    axis = "tensor"
    me = lax.axis_index(axis)
    seq_me = lax.axis_index("seq")
    rows = states_ref.shape[0]
    barrier = pltpu.get_barrier_semaphore()

    def greet(d, carry):
        pl.semaphore_signal(
            barrier, 1, device_id={axis: lax.rem(me + d, n)}, device_id_type=MESH_ID
        )
        return carry

    lax.fori_loop(1, n, greet, 0)

    def greet_seq(d, carry):
        pl.semaphore_signal(
            barrier, 1, device_id={"seq": lax.rem(seq_me + d, sn)}, device_id_type=MESH_ID
        )
        return carry

    lax.fori_loop(1, sn, greet_seq, 0)
    pl.semaphore_wait(barrier, n - 1 + sn - 1)

    def seq_out(d):
        j = lax.rem(seq_me + d, sn)
        return pltpu.make_async_remote_copy(
            src_ref=part_ref,
            dst_ref=seq_buf.at[seq_me],
            send_sem=seq_send.at[j],
            recv_sem=seq_recv.at[seq_me],
            device_id={"seq": j},
            device_id_type=MESH_ID,
        )

    def seq_in(d):
        k = lax.rem(seq_me + sn - d, sn)
        return pltpu.make_async_remote_copy(
            src_ref=part_ref,
            dst_ref=seq_buf.at[k],
            send_sem=seq_send.at[k],
            recv_sem=seq_recv.at[k],
            device_id={"seq": k},
            device_id_type=MESH_ID,
        )

    seq_local = pltpu.make_async_copy(part_ref, seq_buf.at[seq_me], local_sem)
    seq_local.start()

    def seq_start(d, carry):
        seq_out(d).start()
        return carry

    lax.fori_loop(1, sn, seq_start, 0)

    def seq_finish(d, carry):
        seq_out(d).wait_send()
        seq_in(d).wait_recv()
        return carry

    lax.fori_loop(1, sn, seq_finish, 0)
    seq_local.wait()
    parts = seq_buf[...]
    lanes = att_buf.shape[2]
    part_top = parts[..., lanes + 1 : lanes + 2]
    top = jnp.max(part_top, axis=0)
    scale = jnp.exp(part_top - top[None])
    total = jnp.sum(parts[..., lanes : lanes + 1] * scale, axis=0)
    mixture = jnp.sum(parts[..., :lanes] * scale, axis=0)
    att_buf[...] = (mixture / total).astype(att_buf.dtype)
    units = down_ref.shape[0]

    def phase(p, src_of, dst_of):
        def outgoing(d):
            j = lax.rem(me + d, n)
            return pltpu.make_async_remote_copy(
                src_ref=src_of(j),
                dst_ref=dst_of(me),
                send_sem=send_sem.at[p, j],
                recv_sem=recv_sem.at[p, me],
                device_id={axis: j},
                device_id_type=MESH_ID,
            )

        def incoming(d):
            k = lax.rem(me + n - d, n)
            return pltpu.make_async_remote_copy(
                src_ref=src_of(k),
                dst_ref=dst_of(k),
                send_sem=send_sem.at[p, k],
                recv_sem=recv_sem.at[p, k],
                device_id={axis: k},
                device_id_type=MESH_ID,
            )

        local = pltpu.make_async_copy(src_of(me), dst_of(me), local_sem)
        local.start()

        def start(d, carry):
            outgoing(d).start()
            return carry

        lax.fori_loop(1, n, start, 0)

        def finish(d, carry):
            outgoing(d).wait_send()
            incoming(d).wait_recv()
            return carry

        lax.fori_loop(1, n, finish, 0)
        local.wait()

    def row_block(ref):
        return lambda i: ref.at[pl.ds(i * rows, rows)]

    phase(0, lambda j: att_buf.at[j], row_block(abuf))
    partial = jnp.dot(abuf[...], w_out_ref[...], preferred_element_type=jnp.float32)
    pbuf[...] = partial.astype(jnp.bfloat16)
    phase(1, row_block(pbuf), lambda k: rbuf.at[k])
    summed = jnp.sum(rbuf[...].astype(jnp.float32), axis=0)
    resid = (states_ref[...].astype(jnp.float32) + summed).astype(jnp.bfloat16)
    sbuf[...] = resid
    nbuf[...] = rms_norm(resid.astype(jnp.float32), gain_ref[...].reshape(1, -1))
    phase(2, lambda j: nbuf, row_block(gbuf))
    gate_up = jnp.dot(gbuf[...], gate_ref[...], preferred_element_type=jnp.float32)
    hidden = (jax.nn.silu(gate_up[:, :units]) * gate_up[:, units:]).astype(jnp.bfloat16)
    down = jnp.dot(hidden, down_ref[...], preferred_element_type=jnp.float32)
    qbuf[...] = down.astype(jnp.bfloat16)
    phase(3, row_block(qbuf), lambda k: rbuf2.at[k])
    summed2 = jnp.sum(rbuf2[...].astype(jnp.float32), axis=0)
    out_ref[...] = (sbuf[...].astype(jnp.float32) + summed2).astype(out_ref.dtype)


def tail(part, w_out, states, gain, w_gate_up, w_down, n, sn, cid):
    rows, width = states.shape
    lanes = part.shape[2] - 2
    units = w_gate_up.shape[2]
    vmem = pl.BlockSpec(memory_space=pltpu.VMEM)
    return pl.pallas_call(
        functools.partial(_tail_kernel, n, sn),
        out_shape=jax.ShapeDtypeStruct((rows, width), states.dtype),
        in_specs=[vmem] * 6,
        out_specs=vmem,
        scratch_shapes=[
            pltpu.VMEM((sn,) + part.shape, jnp.float32),
            pltpu.VMEM((n, rows, lanes), jnp.bfloat16),
            pltpu.SemaphoreType.DMA((sn,)),
            pltpu.SemaphoreType.DMA((sn,)),
            pltpu.VMEM((n * rows, lanes), jnp.bfloat16),
            pltpu.VMEM((n * rows, width), jnp.bfloat16),
            pltpu.VMEM((n, rows, width), jnp.bfloat16),
            pltpu.VMEM((rows, width), jnp.bfloat16),
            pltpu.VMEM((rows, width), jnp.bfloat16),
            pltpu.VMEM((n * rows, width), jnp.bfloat16),
            pltpu.VMEM((n * rows, width), jnp.bfloat16),
            pltpu.VMEM((n, rows, width), jnp.bfloat16),
            pltpu.SemaphoreType.DMA((4, n)),
            pltpu.SemaphoreType.DMA((4, n)),
            pltpu.SemaphoreType.DMA(()),
        ],
        compiler_params=pltpu.CompilerParams(collective_id=cid, has_side_effects=True),
    )(part, w_out, states, gain, w_gate_up.reshape(width, 2 * units), w_down)


def _head_kernel(
    n, states_ref, gains_ref, w_ref, trig_ref, qkv_ref, recv_ref, x_ref, gbuf, send_sem, recv_sem, local_sem
):
    axis = "tensor"
    me = lax.axis_index(axis)
    rows = x_ref.shape[0]
    block = qkv_ref.shape[1] // 2
    x_ref[...] = rms_norm(states_ref[...].astype(jnp.float32), gains_ref[...].reshape(1, -1))
    barrier = pltpu.get_barrier_semaphore()

    def greet(d, carry):
        pl.semaphore_signal(
            barrier, 1, device_id={axis: lax.rem(me + d, n)}, device_id_type=MESH_ID
        )
        return carry

    lax.fori_loop(1, n, greet, 0)
    pl.semaphore_wait(barrier, n - 1)

    def phase(p, src_of, dst_of):
        def outgoing(d):
            j = lax.rem(me + d, n)
            return pltpu.make_async_remote_copy(
                src_ref=src_of(j),
                dst_ref=dst_of(me),
                send_sem=send_sem.at[p, j],
                recv_sem=recv_sem.at[p, me],
                device_id={axis: j},
                device_id_type=MESH_ID,
            )

        def incoming(d):
            k = lax.rem(me + n - d, n)
            return pltpu.make_async_remote_copy(
                src_ref=src_of(k),
                dst_ref=dst_of(k),
                send_sem=send_sem.at[p, k],
                recv_sem=recv_sem.at[p, k],
                device_id={axis: k},
                device_id_type=MESH_ID,
            )

        local = pltpu.make_async_copy(src_of(me), dst_of(me), local_sem)
        local.start()

        def start(d, carry):
            outgoing(d).start()
            return carry

        lax.fori_loop(1, n, start, 0)

        def finish(d, carry):
            outgoing(d).wait_send()
            incoming(d).wait_recv()
            return carry

        lax.fori_loop(1, n, finish, 0)
        local.wait()

    phase(0, lambda j: x_ref, lambda k: gbuf.at[pl.ds(k * rows, rows)])
    lanes = w_ref.shape[1]
    gathered = gbuf[...]
    contract_last = (((1,), (1,)), ((), ()))
    pair = lax.dot_general(
        gathered,
        w_ref[0:2].reshape(2 * lanes, w_ref.shape[2]),
        contract_last,
        preferred_element_type=jnp.float32,
    )
    value_proj = lax.dot_general(
        gathered, w_ref[2], contract_last, preferred_element_type=jnp.float32
    )
    trig = trig_ref[...]
    half = HEAD_SIZE // 2
    lane = lax.broadcasted_iota(jnp.int32, pair.shape, 1)
    turned = jnp.where(
        lane % HEAD_SIZE < half,
        -pltpu.roll(pair, block - half, 1),
        pltpu.roll(pair, half, 1),
    )
    rotated = pair * trig[:, :block] + turned * trig[:, block:]
    qkv_ref[:, :block] = rotated.astype(qkv_ref.dtype)
    qkv_ref[:, block : block + block // 2] = value_proj.astype(qkv_ref.dtype)
    qkv_ref[:, block + block // 2 :] = jnp.zeros((pair.shape[0], block // 2), qkv_ref.dtype)
    phase(1, lambda j: qkv_ref.at[pl.ds(j * rows, rows)], lambda k: recv_ref.at[k])


def head(states, gains, w_ext, trig, n, cid):
    rows, width = states.shape
    cols = w_ext.shape[1] * 4
    vmem = pl.BlockSpec(memory_space=pltpu.VMEM)
    return pl.pallas_call(
        functools.partial(_head_kernel, n),
        out_shape=(
            jax.ShapeDtypeStruct((n * rows, cols), jnp.bfloat16),
            jax.ShapeDtypeStruct((n, rows, cols), jnp.bfloat16),
        ),
        in_specs=[vmem] * 4,
        out_specs=(vmem, vmem),
        scratch_shapes=[
            pltpu.VMEM((rows, width), jnp.bfloat16),
            pltpu.VMEM((n * rows, width), jnp.bfloat16),
            pltpu.SemaphoreType.DMA((2, n)),
            pltpu.SemaphoreType.DMA((2, n)),
            pltpu.SemaphoreType.DMA(()),
        ],
        compiler_params=pltpu.CompilerParams(collective_id=cid, has_side_effects=True),
    )(states, gains, w_ext, trig)


def per_device(
    states,
    attn_gain,
    w_qkv,
    w_out,
    mlp_gain,
    w_gate_up,
    w_down,
    key_cache,
    value_cache,
    sink_keys,
    sink_values,
    cache_len,
    slot_mask,
    slot_pos,
    new_pos,
    tn,
    sn,
):
    rows = states.shape[0]
    width = states.shape[1]
    row_start = lax.axis_index("tensor") * rows
    floats = states.astype(jnp.float32)
    lanes = w_qkv.shape[2]
    heads_here = lanes // HEAD_SIZE
    half = HEAD_SIZE // 2
    inverse = jnp.exp(
        -jnp.log(jnp.float32(130000.0)) * jnp.arange(half, dtype=jnp.float32) * (2.0 / HEAD_SIZE)
    )
    angle = new_pos.astype(jnp.float32)[:, None] * inverse[None, :]
    angle = jnp.concatenate([angle] * (4 * heads_here), axis=-1)
    trig = jnp.concatenate([jnp.cos(angle), jnp.sin(angle)], axis=-1)
    sink_rows = sink_keys.astype(jnp.float32).reshape(
        rows, lanes * tn // HEAD_SIZE, HEAD_SIZE, sink_keys.shape[2]
    )
    states, sink_rows = lax.optimization_barrier((states, sink_rows))
    qkv_all, mine = head(states, attn_gain, jnp.transpose(w_qkv, (1, 2, 0)), trig, tn, 0)
    batch = qkv_all.shape[0]
    keys_all = qkv_all[:, lanes : 2 * lanes]
    values_all = qkv_all[:, 2 * lanes : 3 * lanes]
    mine = mine.reshape(tn, rows, 4, heads_here, HEAD_SIZE)
    mine = jnp.transpose(mine, (1, 2, 0, 3, 4)).reshape(rows, 4, tn * heads_here, HEAD_SIZE)
    queries = mine[:, 0]
    keys_new = mine[:, 1]
    values_new = mine[:, 2]
    all_heads = queries.shape[1]
    own_len = lax.dynamic_slice_in_dim(cache_len, row_start, rows, 0)
    own_pos = lax.dynamic_slice_in_dim(new_pos, row_start, rows, 0)
    window_here = key_cache.shape[2]
    seq_index = lax.axis_index("seq")
    slots = seq_index * window_here + jnp.arange(window_here, dtype=jnp.int32)
    live = (slots[None, :] < own_len[:, None]) & (slot_mask == 1)
    live = live & (slot_pos < own_pos[:, None]) & (own_pos[:, None] - slot_pos < WINDOW)
    live = live[:, None, :]
    first_shard = seq_index == 0
    kwin = key_cache.reshape(rows, all_heads, HEAD_SIZE, window_here)
    vwin = value_cache.reshape(rows, all_heads, HEAD_SIZE, window_here)
    sink_key_rows = sink_keys.reshape(rows, all_heads, HEAD_SIZE, sink_keys.shape[2])
    vsink = sink_values.reshape(rows, all_heads, HEAD_SIZE, sink_values.shape[2])
    score_win = (
        jnp.einsum("bhd,bhds->bhs", queries, kwin, preferred_element_type=jnp.float32) * 0.125
    )
    score_win = jnp.where(live, score_win, NEG)
    score_sink = (
        jnp.sum(
            queries.astype(jnp.float32)[..., None] * sink_rows, axis=2
        )
        * 0.125
    )
    score_sink = jnp.where(first_shard, score_sink, NEG)
    score_new = jnp.sum(queries.astype(jnp.float32) * keys_new.astype(jnp.float32), axis=-1) * 0.125
    score_new = jnp.where(first_shard, score_new, NEG)
    local_top = jnp.maximum(
        jnp.maximum(jnp.max(score_win, axis=-1), jnp.max(score_sink, axis=-1)), score_new
    )
    weight_win = jnp.where(live, jnp.exp(score_win - local_top[..., None]), 0.0)
    weight_sink = jnp.where(first_shard, jnp.exp(score_sink - local_top[..., None]), 0.0)
    weight_new = jnp.where(first_shard, jnp.exp(score_new - local_top), 0.0)
    total = jnp.sum(weight_win, axis=-1) + jnp.sum(weight_sink, axis=-1) + weight_new
    mixture = jnp.einsum(
        "bhs,bhds->bhd", weight_win.astype(jnp.bfloat16), vwin, preferred_element_type=jnp.float32
    )
    mixture = mixture + jnp.sum(
        undo_round(weight_sink)[:, :, None, :] * vsink.astype(jnp.float32), axis=-1
    )
    mixture = mixture + undo_round(weight_new)[..., None] * values_new.astype(jnp.float32)
    packed = jnp.concatenate([mixture, total[..., None], local_top[..., None]], axis=-1)
    packed = jnp.transpose(packed, (1, 0, 2))
    out_states = tail(packed, w_out, states, mlp_gain, w_gate_up, w_down, tn, sn, 3)
    return (out_states, keys_all, values_all)


def solution(mesh):
    in_specs = (
        P("tensor", None),
        P(),
        P(None, None, "tensor"),
        P("tensor", None),
        P(),
        P(None, None, "tensor"),
        P("tensor", None),
        P("tensor", None, "seq"),
        P("tensor", None, "seq"),
        P("tensor", None, None),
        P("tensor", None, None),
        P(),
        P("tensor", "seq"),
        P("tensor", "seq"),
        P(),
    )
    out_specs = (P("tensor", None), P(None, "tensor"), P(None, "tensor"))
    body = functools.partial(per_device, tn=mesh.shape["tensor"], sn=mesh.shape["seq"])
    return jax.shard_map(
        body, mesh=mesh, in_specs=in_specs, out_specs=out_specs, check_vma=False
    )
```

```python
import functools

import jax
import jax.numpy as jnp
from jax import lax
from jax.experimental import pallas as pl
from jax.experimental.pallas import tpu as pltpu
from jax.sharding import PartitionSpec as P

HEAD_SIZE = 64
WINDOW = 4096


NEG = -1e30
MESH_ID = pl.DeviceIdType.MESH


def rms_norm(values, gain):
    meansq = jnp.mean(values * values, axis=-1, keepdims=True)
    return (values * lax.rsqrt(meansq + 1e-05) * gain.astype(jnp.float32)).astype(jnp.bfloat16)


def rotary(tensor, cosine, sine):
    half = tensor.shape[-1] // 2
    turned = jnp.concatenate([-tensor[..., half:], tensor[..., :half]], axis=-1)
    return tensor * cosine + turned * sine


def undo_round(weights):
    rounded = lax.optimization_barrier(weights.astype(jnp.bfloat16))
    return rounded.astype(jnp.float32)


def _exchange_kernel(n, axis, gather, x_ref, y_ref, send_sem, recv_sem, local_sem):
    me = lax.axis_index(axis)
    barrier = pltpu.get_barrier_semaphore()

    def greet(d, carry):
        peer = lax.rem(me + d, n)
        pl.semaphore_signal(barrier, 1, device_id={axis: peer}, device_id_type=MESH_ID)
        return carry

    lax.fori_loop(1, n, greet, 0)
    pl.semaphore_wait(barrier, n - 1)

    def source(j):
        return x_ref if gather else x_ref.at[j]

    def outgoing(d):
        j = lax.rem(me + d, n)
        return pltpu.make_async_remote_copy(
            src_ref=source(j),
            dst_ref=y_ref.at[me],
            send_sem=send_sem.at[j],
            recv_sem=recv_sem.at[me],
            device_id={axis: j},
            device_id_type=MESH_ID,
        )

    def incoming(d):
        k = lax.rem(me + n - d, n)
        return pltpu.make_async_remote_copy(
            src_ref=source(k),
            dst_ref=y_ref.at[k],
            send_sem=send_sem.at[k],
            recv_sem=recv_sem.at[k],
            device_id={axis: k},
            device_id_type=MESH_ID,
        )

    local = pltpu.make_async_copy(source(me), y_ref.at[me], local_sem)
    local.start()

    def start(d, carry):
        outgoing(d).start()
        return carry

    lax.fori_loop(1, n, start, 0)

    def finish(d, carry):
        outgoing(d).wait_send()
        incoming(d).wait_recv()
        return carry

    lax.fori_loop(1, n, finish, 0)
    local.wait()


def exchange(x, axis, n, cid, gather=False):
    piece = x.shape if gather else x.shape[1:]
    return pl.pallas_call(
        functools.partial(_exchange_kernel, n, axis, gather),
        out_shape=jax.ShapeDtypeStruct((n,) + tuple(piece), x.dtype),
        in_specs=[pl.BlockSpec(memory_space=pl.ANY)],
        out_specs=pl.BlockSpec(memory_space=pl.ANY),
        scratch_shapes=[
            pltpu.SemaphoreType.DMA((n,)),
            pltpu.SemaphoreType.DMA((n,)),
            pltpu.SemaphoreType.DMA(()),
        ],
        compiler_params=pltpu.CompilerParams(collective_id=cid, has_side_effects=True),
    )(x)


def _tail_kernel(
    n,
    sn,
    part_ref,
    w_out_ref,
    states_ref,
    gain_ref,
    gate_ref,
    down_ref,
    out_ref,
    seq_buf,
    att_buf,
    seq_send,
    seq_recv,
    abuf,
    pbuf,
    rbuf,
    sbuf,
    nbuf,
    gbuf,
    qbuf,
    rbuf2,
    send_sem,
    recv_sem,
    local_sem,
):
    axis = "tensor"
    me = lax.axis_index(axis)
    seq_me = lax.axis_index("seq")
    rows = states_ref.shape[0]
    barrier = pltpu.get_barrier_semaphore()

    def greet(d, carry):
        pl.semaphore_signal(
            barrier, 1, device_id={axis: lax.rem(me + d, n)}, device_id_type=MESH_ID
        )
        return carry

    lax.fori_loop(1, n, greet, 0)

    def greet_seq(d, carry):
        pl.semaphore_signal(
            barrier, 1, device_id={"seq": lax.rem(seq_me + d, sn)}, device_id_type=MESH_ID
        )
        return carry

    lax.fori_loop(1, sn, greet_seq, 0)
    pl.semaphore_wait(barrier, n - 1 + sn - 1)

    def seq_out(d):
        j = lax.rem(seq_me + d, sn)
        return pltpu.make_async_remote_copy(
            src_ref=part_ref,
            dst_ref=seq_buf.at[seq_me],
            send_sem=seq_send.at[j],
            recv_sem=seq_recv.at[seq_me],
            device_id={"seq": j},
            device_id_type=MESH_ID,
        )

    def seq_in(d):
        k = lax.rem(seq_me + sn - d, sn)
        return pltpu.make_async_remote_copy(
            src_ref=part_ref,
            dst_ref=seq_buf.at[k],
            send_sem=seq_send.at[k],
            recv_sem=seq_recv.at[k],
            device_id={"seq": k},
            device_id_type=MESH_ID,
        )

    seq_local = pltpu.make_async_copy(part_ref, seq_buf.at[seq_me], local_sem)
    seq_local.start()

    def seq_start(d, carry):
        seq_out(d).start()
        return carry

    lax.fori_loop(1, sn, seq_start, 0)

    def seq_finish(d, carry):
        seq_out(d).wait_send()
        seq_in(d).wait_recv()
        return carry

    lax.fori_loop(1, sn, seq_finish, 0)
    seq_local.wait()
    parts = seq_buf[...]
    lanes = att_buf.shape[2]
    part_top = parts[..., lanes + 1 : lanes + 2]
    top = jnp.max(part_top, axis=0)
    scale = jnp.exp(part_top - top[None])
    total = jnp.sum(parts[..., lanes : lanes + 1] * scale, axis=0)
    mixture = jnp.sum(parts[..., :lanes] * scale, axis=0)
    att_buf[...] = (mixture / total).astype(att_buf.dtype)
    units = down_ref.shape[0]

    def phase(p, src_of, dst_of):
        def outgoing(d):
            j = lax.rem(me + d, n)
            return pltpu.make_async_remote_copy(
                src_ref=src_of(j),
                dst_ref=dst_of(me),
                send_sem=send_sem.at[p, j],
                recv_sem=recv_sem.at[p, me],
                device_id={axis: j},
                device_id_type=MESH_ID,
            )

        def incoming(d):
            k = lax.rem(me + n - d, n)
            return pltpu.make_async_remote_copy(
                src_ref=src_of(k),
                dst_ref=dst_of(k),
                send_sem=send_sem.at[p, k],
                recv_sem=recv_sem.at[p, k],
                device_id={axis: k},
                device_id_type=MESH_ID,
            )

        local = pltpu.make_async_copy(src_of(me), dst_of(me), local_sem)
        local.start()

        def start(d, carry):
            outgoing(d).start()
            return carry

        lax.fori_loop(1, n, start, 0)

        def finish(d, carry):
            outgoing(d).wait_send()
            incoming(d).wait_recv()
            return carry

        lax.fori_loop(1, n, finish, 0)
        local.wait()

    def row_block(ref):
        return lambda i: ref.at[pl.ds(i * rows, rows)]

    phase(0, lambda j: att_buf.at[j], row_block(abuf))
    partial = jnp.dot(abuf[...], w_out_ref[...], preferred_element_type=jnp.float32)
    pbuf[...] = partial.astype(jnp.bfloat16)
    phase(1, row_block(pbuf), lambda k: rbuf.at[k])
    summed = jnp.sum(rbuf[...].astype(jnp.float32), axis=0)
    resid = (states_ref[...].astype(jnp.float32) + summed).astype(jnp.bfloat16)
    sbuf[...] = resid
    nbuf[...] = rms_norm(resid.astype(jnp.float32), gain_ref[...].reshape(1, -1))
    phase(2, lambda j: nbuf, row_block(gbuf))
    gate_up = jnp.dot(gbuf[...], gate_ref[...], preferred_element_type=jnp.float32)
    hidden = (jax.nn.silu(gate_up[:, :units]) * gate_up[:, units:]).astype(jnp.bfloat16)
    down = jnp.dot(hidden, down_ref[...], preferred_element_type=jnp.float32)
    qbuf[...] = down.astype(jnp.bfloat16)
    phase(3, row_block(qbuf), lambda k: rbuf2.at[k])
    summed2 = jnp.sum(rbuf2[...].astype(jnp.float32), axis=0)
    out_ref[...] = (sbuf[...].astype(jnp.float32) + summed2).astype(out_ref.dtype)


def tail(part, w_out, states, gain, w_gate_up, w_down, n, sn, cid):
    rows, width = states.shape
    lanes = part.shape[2] - 2
    units = w_gate_up.shape[2]
    vmem = pl.BlockSpec(memory_space=pltpu.VMEM)
    return pl.pallas_call(
        functools.partial(_tail_kernel, n, sn),
        out_shape=jax.ShapeDtypeStruct((rows, width), states.dtype),
        in_specs=[vmem] * 6,
        out_specs=vmem,
        scratch_shapes=[
            pltpu.VMEM((sn,) + part.shape, jnp.float32),
            pltpu.VMEM((n, rows, lanes), jnp.bfloat16),
            pltpu.SemaphoreType.DMA((sn,)),
            pltpu.SemaphoreType.DMA((sn,)),
            pltpu.VMEM((n * rows, lanes), jnp.bfloat16),
            pltpu.VMEM((n * rows, width), jnp.bfloat16),
            pltpu.VMEM((n, rows, width), jnp.bfloat16),
            pltpu.VMEM((rows, width), jnp.bfloat16),
            pltpu.VMEM((rows, width), jnp.bfloat16),
            pltpu.VMEM((n * rows, width), jnp.bfloat16),
            pltpu.VMEM((n * rows, width), jnp.bfloat16),
            pltpu.VMEM((n, rows, width), jnp.bfloat16),
            pltpu.SemaphoreType.DMA((4, n)),
            pltpu.SemaphoreType.DMA((4, n)),
            pltpu.SemaphoreType.DMA(()),
        ],
        compiler_params=pltpu.CompilerParams(collective_id=cid, has_side_effects=True),
    )(part, w_out, states, gain, w_gate_up.reshape(width, 2 * units), w_down)


def _head_kernel(
    n, states_ref, gains_ref, w_ref, trig_ref, qkv_ref, recv_ref, x_ref, gbuf, send_sem, recv_sem, local_sem
):
    axis = "tensor"
    me = lax.axis_index(axis)
    rows = x_ref.shape[0]
    block = qkv_ref.shape[1] // 2
    x_ref[...] = rms_norm(states_ref[...].astype(jnp.float32), gains_ref[...].reshape(1, -1))
    barrier = pltpu.get_barrier_semaphore()

    def greet(d, carry):
        pl.semaphore_signal(
            barrier, 1, device_id={axis: lax.rem(me + d, n)}, device_id_type=MESH_ID
        )
        return carry

    lax.fori_loop(1, n, greet, 0)
    pl.semaphore_wait(barrier, n - 1)

    def phase(p, src_of, dst_of):
        def outgoing(d):
            j = lax.rem(me + d, n)
            return pltpu.make_async_remote_copy(
                src_ref=src_of(j),
                dst_ref=dst_of(me),
                send_sem=send_sem.at[p, j],
                recv_sem=recv_sem.at[p, me],
                device_id={axis: j},
                device_id_type=MESH_ID,
            )

        def incoming(d):
            k = lax.rem(me + n - d, n)
            return pltpu.make_async_remote_copy(
                src_ref=src_of(k),
                dst_ref=dst_of(k),
                send_sem=send_sem.at[p, k],
                recv_sem=recv_sem.at[p, k],
                device_id={axis: k},
                device_id_type=MESH_ID,
            )

        local = pltpu.make_async_copy(src_of(me), dst_of(me), local_sem)
        local.start()

        def start(d, carry):
            outgoing(d).start()
            return carry

        lax.fori_loop(1, n, start, 0)

        def finish(d, carry):
            outgoing(d).wait_send()
            incoming(d).wait_recv()
            return carry

        lax.fori_loop(1, n, finish, 0)
        local.wait()

    phase(0, lambda j: x_ref, lambda k: gbuf.at[pl.ds(k * rows, rows)])
    lanes = w_ref.shape[1]
    gathered = gbuf[...]
    contract_last = (((1,), (1,)), ((), ()))
    pair = lax.dot_general(
        gathered,
        w_ref[0:2].reshape(2 * lanes, w_ref.shape[2]),
        contract_last,
        preferred_element_type=jnp.float32,
    )
    value_proj = lax.dot_general(
        gathered, w_ref[2], contract_last, preferred_element_type=jnp.float32
    )
    trig = trig_ref[...]
    half = HEAD_SIZE // 2
    lane = lax.broadcasted_iota(jnp.int32, pair.shape, 1)
    turned = jnp.where(
        lane % HEAD_SIZE < half,
        -pltpu.roll(pair, block - half, 1),
        pltpu.roll(pair, half, 1),
    )
    rotated = pair * trig[:, :block] + turned * trig[:, block:]
    qkv_ref[:, :block] = rotated.astype(qkv_ref.dtype)
    qkv_ref[:, block : block + block // 2] = value_proj.astype(qkv_ref.dtype)
    qkv_ref[:, block + block // 2 :] = jnp.zeros((pair.shape[0], block // 2), qkv_ref.dtype)
    phase(1, lambda j: qkv_ref.at[pl.ds(j * rows, rows)], lambda k: recv_ref.at[k])


def head(states, gains, w_ext, trig, n, cid):
    rows, width = states.shape
    cols = w_ext.shape[1] * 4
    vmem = pl.BlockSpec(memory_space=pltpu.VMEM)
    return pl.pallas_call(
        functools.partial(_head_kernel, n),
        out_shape=(
            jax.ShapeDtypeStruct((n * rows, cols), jnp.bfloat16),
            jax.ShapeDtypeStruct((n, rows, cols), jnp.bfloat16),
        ),
        in_specs=[vmem] * 4,
        out_specs=(vmem, vmem),
        scratch_shapes=[
            pltpu.VMEM((rows, width), jnp.bfloat16),
            pltpu.VMEM((n * rows, width), jnp.bfloat16),
            pltpu.SemaphoreType.DMA((2, n)),
            pltpu.SemaphoreType.DMA((2, n)),
            pltpu.SemaphoreType.DMA(()),
        ],
        compiler_params=pltpu.CompilerParams(
            collective_id=cid, has_side_effects=True, vmem_limit_bytes=8 * 1024 * 1024
        ),
    )(states, gains, w_ext, trig)


def per_device(
    states,
    attn_gain,
    w_qkv,
    w_out,
    mlp_gain,
    w_gate_up,
    w_down,
    key_cache,
    value_cache,
    sink_keys,
    sink_values,
    cache_len,
    slot_mask,
    slot_pos,
    new_pos,
    tn,
    sn,
):
    rows = states.shape[0]
    width = states.shape[1]
    row_start = lax.axis_index("tensor") * rows
    floats = states.astype(jnp.float32)
    lanes = w_qkv.shape[2]
    heads_here = lanes // HEAD_SIZE
    half = HEAD_SIZE // 2
    inverse = jnp.exp(
        -jnp.log(jnp.float32(130000.0)) * jnp.arange(half, dtype=jnp.float32) * (2.0 / HEAD_SIZE)
    )
    angle = new_pos.astype(jnp.float32)[:, None] * inverse[None, :]
    angle = jnp.concatenate([angle] * (4 * heads_here), axis=-1)
    trig = jnp.concatenate([jnp.cos(angle), jnp.sin(angle)], axis=-1)
    sink_rows = sink_keys.astype(jnp.float32).reshape(
        rows, lanes * tn // HEAD_SIZE, HEAD_SIZE, sink_keys.shape[2]
    )
    states, sink_rows = lax.optimization_barrier((states, sink_rows))
    qkv_all, mine = head(states, attn_gain, jnp.transpose(w_qkv, (1, 2, 0)), trig, tn, 0)
    batch = qkv_all.shape[0]
    keys_all = qkv_all[:, lanes : 2 * lanes]
    values_all = qkv_all[:, 2 * lanes : 3 * lanes]
    mine = mine.reshape(tn, rows, 4, heads_here, HEAD_SIZE)
    mine = jnp.transpose(mine, (1, 2, 0, 3, 4)).reshape(rows, 4, tn * heads_here, HEAD_SIZE)
    queries = mine[:, 0]
    keys_new = mine[:, 1]
    values_new = mine[:, 2]
    all_heads = queries.shape[1]
    own_len = lax.dynamic_slice_in_dim(cache_len, row_start, rows, 0)
    own_pos = lax.dynamic_slice_in_dim(new_pos, row_start, rows, 0)
    window_here = key_cache.shape[2]
    seq_index = lax.axis_index("seq")
    slots = seq_index * window_here + jnp.arange(window_here, dtype=jnp.int32)
    live = (slots[None, :] < own_len[:, None]) & (slot_mask == 1)
    live = live & (slot_pos < own_pos[:, None]) & (own_pos[:, None] - slot_pos < WINDOW)
    live = live[:, None, :]
    first_shard = seq_index == 0
    kwin = key_cache.reshape(rows, all_heads, HEAD_SIZE, window_here)
    vwin = value_cache.reshape(rows, all_heads, HEAD_SIZE, window_here)
    sink_key_rows = sink_keys.reshape(rows, all_heads, HEAD_SIZE, sink_keys.shape[2])
    vsink = sink_values.reshape(rows, all_heads, HEAD_SIZE, sink_values.shape[2])
    score_win = (
        jnp.einsum("bhd,bhds->bhs", queries, kwin, preferred_element_type=jnp.float32) * 0.125
    )
    score_win = jnp.where(live, score_win, NEG)
    score_sink = (
        jnp.sum(
            queries.astype(jnp.float32)[..., None] * sink_rows, axis=2
        )
        * 0.125
    )
    score_sink = jnp.where(first_shard, score_sink, NEG)
    score_new = jnp.sum(queries.astype(jnp.float32) * keys_new.astype(jnp.float32), axis=-1) * 0.125
    score_new = jnp.where(first_shard, score_new, NEG)
    local_top = jnp.maximum(
        jnp.maximum(jnp.max(score_win, axis=-1), jnp.max(score_sink, axis=-1)), score_new
    )
    weight_win = jnp.where(live, jnp.exp(score_win - local_top[..., None]), 0.0)
    weight_sink = jnp.where(first_shard, jnp.exp(score_sink - local_top[..., None]), 0.0)
    weight_new = jnp.where(first_shard, jnp.exp(score_new - local_top), 0.0)
    total = jnp.sum(weight_win, axis=-1) + jnp.sum(weight_sink, axis=-1) + weight_new
    mixture = jnp.einsum(
        "bhs,bhds->bhd", weight_win.astype(jnp.bfloat16), vwin, preferred_element_type=jnp.float32
    )
    mixture = mixture + jnp.sum(
        undo_round(weight_sink)[:, :, None, :] * vsink.astype(jnp.float32), axis=-1
    )
    mixture = mixture + undo_round(weight_new)[..., None] * values_new.astype(jnp.float32)
    packed = jnp.concatenate([mixture, total[..., None], local_top[..., None]], axis=-1)
    packed = jnp.transpose(packed, (1, 0, 2))
    out_states = tail(packed, w_out, states, mlp_gain, w_gate_up, w_down, tn, sn, 3)
    return (out_states, keys_all, values_all)


def solution(mesh):
    in_specs = (
        P("tensor", None),
        P(),
        P(None, None, "tensor"),
        P("tensor", None),
        P(),
        P(None, None, "tensor"),
        P("tensor", None),
        P("tensor", None, "seq"),
        P("tensor", None, "seq"),
        P("tensor", None, None),
        P("tensor", None, None),
        P(),
        P("tensor", "seq"),
        P("tensor", "seq"),
        P(),
    )
    out_specs = (P("tensor", None), P(None, "tensor"), P(None, "tensor"))
    body = functools.partial(per_device, tn=mesh.shape["tensor"], sn=mesh.shape["seq"])
    return jax.shard_map(
        body, mesh=mesh, in_specs=in_specs, out_specs=out_specs, check_vma=False
    )
```

```python
import functools

import jax
import jax.numpy as jnp
from jax import lax
from jax.experimental import pallas as pl
from jax.experimental.pallas import tpu as pltpu
from jax.sharding import PartitionSpec as P

HEAD_SIZE = 64
WINDOW = 4096


NEG = -1e30
MESH_ID = pl.DeviceIdType.MESH


def rms_norm(values, gain):
    meansq = jnp.mean(values * values, axis=-1, keepdims=True)
    return (values * lax.rsqrt(meansq + 1e-05) * gain.astype(jnp.float32)).astype(jnp.bfloat16)


def rotary(tensor, cosine, sine):
    half = tensor.shape[-1] // 2
    turned = jnp.concatenate([-tensor[..., half:], tensor[..., :half]], axis=-1)
    return tensor * cosine + turned * sine


def undo_round(weights):
    rounded = lax.optimization_barrier(weights.astype(jnp.bfloat16))
    return rounded.astype(jnp.float32)


def _exchange_kernel(n, axis, gather, x_ref, y_ref, send_sem, recv_sem, local_sem):
    me = lax.axis_index(axis)
    barrier = pltpu.get_barrier_semaphore()

    def greet(d, carry):
        peer = lax.rem(me + d, n)
        pl.semaphore_signal(barrier, 1, device_id={axis: peer}, device_id_type=MESH_ID)
        return carry

    lax.fori_loop(1, n, greet, 0)
    pl.semaphore_wait(barrier, n - 1)

    def source(j):
        return x_ref if gather else x_ref.at[j]

    def outgoing(d):
        j = lax.rem(me + d, n)
        return pltpu.make_async_remote_copy(
            src_ref=source(j),
            dst_ref=y_ref.at[me],
            send_sem=send_sem.at[j],
            recv_sem=recv_sem.at[me],
            device_id={axis: j},
            device_id_type=MESH_ID,
        )

    def incoming(d):
        k = lax.rem(me + n - d, n)
        return pltpu.make_async_remote_copy(
            src_ref=source(k),
            dst_ref=y_ref.at[k],
            send_sem=send_sem.at[k],
            recv_sem=recv_sem.at[k],
            device_id={axis: k},
            device_id_type=MESH_ID,
        )

    local = pltpu.make_async_copy(source(me), y_ref.at[me], local_sem)
    local.start()

    def start(d, carry):
        outgoing(d).start()
        return carry

    lax.fori_loop(1, n, start, 0)

    def finish(d, carry):
        outgoing(d).wait_send()
        incoming(d).wait_recv()
        return carry

    lax.fori_loop(1, n, finish, 0)
    local.wait()


def exchange(x, axis, n, cid, gather=False):
    piece = x.shape if gather else x.shape[1:]
    return pl.pallas_call(
        functools.partial(_exchange_kernel, n, axis, gather),
        out_shape=jax.ShapeDtypeStruct((n,) + tuple(piece), x.dtype),
        in_specs=[pl.BlockSpec(memory_space=pl.ANY)],
        out_specs=pl.BlockSpec(memory_space=pl.ANY),
        scratch_shapes=[
            pltpu.SemaphoreType.DMA((n,)),
            pltpu.SemaphoreType.DMA((n,)),
            pltpu.SemaphoreType.DMA(()),
        ],
        compiler_params=pltpu.CompilerParams(collective_id=cid, has_side_effects=True),
    )(x)


def _tail_kernel(
    n,
    sn,
    part_ref,
    w_out_ref,
    states_ref,
    gain_ref,
    gate_ref,
    down_ref,
    out_ref,
    resid_ref,
    seq_buf,
    att_buf,
    seq_send,
    seq_recv,
    abuf,
    pbuf,
    rbuf,
    sbuf,
    nbuf,
    gbuf,
    qbuf,
    rbuf2,
    send_sem,
    recv_sem,
    local_sem,
):
    axis = "tensor"
    me = lax.axis_index(axis)
    seq_me = lax.axis_index("seq")
    rows = states_ref.shape[0]
    barrier = pltpu.get_barrier_semaphore()

    def greet(d, carry):
        pl.semaphore_signal(
            barrier, 1, device_id={axis: lax.rem(me + d, n)}, device_id_type=MESH_ID
        )
        return carry

    lax.fori_loop(1, n, greet, 0)

    def greet_seq(d, carry):
        pl.semaphore_signal(
            barrier, 1, device_id={"seq": lax.rem(seq_me + d, sn)}, device_id_type=MESH_ID
        )
        return carry

    lax.fori_loop(1, sn, greet_seq, 0)
    pl.semaphore_wait(barrier, n - 1 + sn - 1)

    def seq_out(d):
        j = lax.rem(seq_me + d, sn)
        return pltpu.make_async_remote_copy(
            src_ref=part_ref,
            dst_ref=seq_buf.at[seq_me],
            send_sem=seq_send.at[j],
            recv_sem=seq_recv.at[seq_me],
            device_id={"seq": j},
            device_id_type=MESH_ID,
        )

    def seq_in(d):
        k = lax.rem(seq_me + sn - d, sn)
        return pltpu.make_async_remote_copy(
            src_ref=part_ref,
            dst_ref=seq_buf.at[k],
            send_sem=seq_send.at[k],
            recv_sem=seq_recv.at[k],
            device_id={"seq": k},
            device_id_type=MESH_ID,
        )

    seq_local = pltpu.make_async_copy(part_ref, seq_buf.at[seq_me], local_sem)
    seq_local.start()

    def seq_start(d, carry):
        seq_out(d).start()
        return carry

    lax.fori_loop(1, sn, seq_start, 0)

    def seq_finish(d, carry):
        seq_out(d).wait_send()
        seq_in(d).wait_recv()
        return carry

    lax.fori_loop(1, sn, seq_finish, 0)
    seq_local.wait()
    parts = seq_buf[...]
    lanes = att_buf.shape[2]
    part_top = parts[..., lanes + 1 : lanes + 2]
    top = jnp.max(part_top, axis=0)
    scale = jnp.exp(part_top - top[None])
    total = jnp.sum(parts[..., lanes : lanes + 1] * scale, axis=0)
    mixture = jnp.sum(parts[..., :lanes] * scale, axis=0)
    att_buf[...] = (mixture / total).astype(att_buf.dtype)
    units = down_ref.shape[0]

    def phase(p, src_of, dst_of):
        def outgoing(d):
            j = lax.rem(me + d, n)
            return pltpu.make_async_remote_copy(
                src_ref=src_of(j),
                dst_ref=dst_of(me),
                send_sem=send_sem.at[p, j],
                recv_sem=recv_sem.at[p, me],
                device_id={axis: j},
                device_id_type=MESH_ID,
            )

        def incoming(d):
            k = lax.rem(me + n - d, n)
            return pltpu.make_async_remote_copy(
                src_ref=src_of(k),
                dst_ref=dst_of(k),
                send_sem=send_sem.at[p, k],
                recv_sem=recv_sem.at[p, k],
                device_id={axis: k},
                device_id_type=MESH_ID,
            )

        local = pltpu.make_async_copy(src_of(me), dst_of(me), local_sem)
        local.start()

        def start(d, carry):
            outgoing(d).start()
            return carry

        lax.fori_loop(1, n, start, 0)

        def finish(d, carry):
            outgoing(d).wait_send()
            incoming(d).wait_recv()
            return carry

        lax.fori_loop(1, n, finish, 0)
        local.wait()

    def row_block(ref):
        return lambda i: ref.at[pl.ds(i * rows, rows)]

    phase(0, lambda j: att_buf.at[j], row_block(abuf))
    partial = jnp.dot(abuf[...], w_out_ref[...], preferred_element_type=jnp.float32)
    pbuf[...] = partial.astype(jnp.bfloat16)
    phase(1, row_block(pbuf), lambda k: rbuf.at[k])
    summed = jnp.sum(rbuf[...].astype(jnp.float32), axis=0)
    resid = (states_ref[...].astype(jnp.float32) + summed).astype(jnp.bfloat16)
    sbuf[...] = resid
    nbuf[...] = rms_norm(resid.astype(jnp.float32), gain_ref[...].reshape(1, -1))
    phase(2, lambda j: nbuf, row_block(gbuf))
    gate_up = jnp.dot(gbuf[...], gate_ref[...], preferred_element_type=jnp.float32)
    hidden = (jax.nn.silu(gate_up[:, :units]) * gate_up[:, units:]).astype(jnp.bfloat16)
    down = jnp.dot(hidden, down_ref[...], preferred_element_type=jnp.float32)
    qbuf[...] = down.astype(jnp.bfloat16)
    phase(3, row_block(qbuf), lambda k: rbuf2.at[k])
    out_ref[...] = jnp.sum(rbuf2[...].astype(jnp.float32), axis=0)
    resid_ref[...] = sbuf[...]


def tail(part, w_out, states, gain, w_gate_up, w_down, n, sn, cid):
    rows, width = states.shape
    lanes = part.shape[2] - 2
    units = w_gate_up.shape[2]
    vmem = pl.BlockSpec(memory_space=pltpu.VMEM)
    return pl.pallas_call(
        functools.partial(_tail_kernel, n, sn),
        out_shape=(
            jax.ShapeDtypeStruct((rows, width), jnp.float32),
            jax.ShapeDtypeStruct((rows, width), states.dtype),
        ),
        in_specs=[vmem] * 6,
        out_specs=(vmem, vmem),
        scratch_shapes=[
            pltpu.VMEM((sn,) + part.shape, jnp.float32),
            pltpu.VMEM((n, rows, lanes), jnp.bfloat16),
            pltpu.SemaphoreType.DMA((sn,)),
            pltpu.SemaphoreType.DMA((sn,)),
            pltpu.VMEM((n * rows, lanes), jnp.bfloat16),
            pltpu.VMEM((n * rows, width), jnp.bfloat16),
            pltpu.VMEM((n, rows, width), jnp.bfloat16),
            pltpu.VMEM((rows, width), jnp.bfloat16),
            pltpu.VMEM((rows, width), jnp.bfloat16),
            pltpu.VMEM((n * rows, width), jnp.bfloat16),
            pltpu.VMEM((n * rows, width), jnp.bfloat16),
            pltpu.VMEM((n, rows, width), jnp.bfloat16),
            pltpu.SemaphoreType.DMA((4, n)),
            pltpu.SemaphoreType.DMA((4, n)),
            pltpu.SemaphoreType.DMA(()),
        ],
        compiler_params=pltpu.CompilerParams(collective_id=cid, has_side_effects=True),
    )(part, w_out, states, gain, w_gate_up.reshape(width, 2 * units), w_down)


def _head_kernel(
    n, states_ref, gains_ref, w_ref, trig_ref, qkv_ref, recv_ref, x_ref, gbuf, send_sem, recv_sem, local_sem
):
    axis = "tensor"
    me = lax.axis_index(axis)
    rows = x_ref.shape[0]
    block = qkv_ref.shape[1] // 2
    barrier = pltpu.get_barrier_semaphore()

    def greet(d, carry):
        pl.semaphore_signal(
            barrier, 1, device_id={axis: lax.rem(me + d, n)}, device_id_type=MESH_ID
        )
        return carry

    lax.fori_loop(1, n, greet, 0)
    x_ref[...] = rms_norm(states_ref[...].astype(jnp.float32), gains_ref[...].reshape(1, -1))
    pl.semaphore_wait(barrier, n - 1)

    def phase(p, src_of, dst_of):
        def outgoing(d):
            j = lax.rem(me + d, n)
            return pltpu.make_async_remote_copy(
                src_ref=src_of(j),
                dst_ref=dst_of(me),
                send_sem=send_sem.at[p, j],
                recv_sem=recv_sem.at[p, me],
                device_id={axis: j},
                device_id_type=MESH_ID,
            )

        def incoming(d):
            k = lax.rem(me + n - d, n)
            return pltpu.make_async_remote_copy(
                src_ref=src_of(k),
                dst_ref=dst_of(k),
                send_sem=send_sem.at[p, k],
                recv_sem=recv_sem.at[p, k],
                device_id={axis: k},
                device_id_type=MESH_ID,
            )

        local = pltpu.make_async_copy(src_of(me), dst_of(me), local_sem)
        local.start()

        def start(d, carry):
            outgoing(d).start()
            return carry

        lax.fori_loop(1, n, start, 0)

        def finish(d, carry):
            outgoing(d).wait_send()
            incoming(d).wait_recv()
            return carry

        lax.fori_loop(1, n, finish, 0)
        local.wait()

    phase(0, lambda j: x_ref, lambda k: gbuf.at[pl.ds(k * rows, rows)])
    lanes = w_ref.shape[1]
    gathered = gbuf[...]
    contract_last = (((1,), (1,)), ((), ()))
    pair = lax.dot_general(
        gathered,
        w_ref[0:2].reshape(2 * lanes, w_ref.shape[2]),
        contract_last,
        preferred_element_type=jnp.float32,
    )
    value_proj = lax.dot_general(
        gathered, w_ref[2], contract_last, preferred_element_type=jnp.float32
    )
    trig = trig_ref[...]
    half = HEAD_SIZE // 2
    lane = lax.broadcasted_iota(jnp.int32, pair.shape, 1)
    turned = jnp.where(
        lane % HEAD_SIZE < half,
        -pltpu.roll(pair, block - half, 1),
        pltpu.roll(pair, half, 1),
    )
    rotated = pair * trig[:, :block] + turned * trig[:, block:]
    qkv_ref[:, :block] = rotated.astype(qkv_ref.dtype)
    qkv_ref[:, block : block + block // 2] = value_proj.astype(qkv_ref.dtype)
    qkv_ref[:, block + block // 2 :] = jnp.zeros((pair.shape[0], block // 2), qkv_ref.dtype)
    phase(1, lambda j: qkv_ref.at[pl.ds(j * rows, rows)], lambda k: recv_ref.at[k])


def head(states, gains, w_ext, trig, n, cid):
    rows, width = states.shape
    cols = w_ext.shape[1] * 4
    vmem = pl.BlockSpec(memory_space=pltpu.VMEM)
    return pl.pallas_call(
        functools.partial(_head_kernel, n),
        out_shape=(
            jax.ShapeDtypeStruct((n * rows, cols), jnp.bfloat16),
            jax.ShapeDtypeStruct((n, rows, cols), jnp.bfloat16),
        ),
        in_specs=[vmem] * 4,
        out_specs=(vmem, vmem),
        scratch_shapes=[
            pltpu.VMEM((rows, width), jnp.bfloat16),
            pltpu.VMEM((n * rows, width), jnp.bfloat16),
            pltpu.SemaphoreType.DMA((2, n)),
            pltpu.SemaphoreType.DMA((2, n)),
            pltpu.SemaphoreType.DMA(()),
        ],
        compiler_params=pltpu.CompilerParams(
            collective_id=cid, has_side_effects=True, vmem_limit_bytes=8 * 1024 * 1024
        ),
    )(states, gains, w_ext, trig)


def per_device(
    states,
    attn_gain,
    w_qkv,
    w_out,
    mlp_gain,
    w_gate_up,
    w_down,
    key_cache,
    value_cache,
    sink_keys,
    sink_values,
    cache_len,
    slot_mask,
    slot_pos,
    new_pos,
    tn,
    sn,
):
    rows = states.shape[0]
    width = states.shape[1]
    row_start = lax.axis_index("tensor") * rows
    floats = states.astype(jnp.float32)
    lanes = w_qkv.shape[2]
    heads_here = lanes // HEAD_SIZE
    half = HEAD_SIZE // 2
    inverse = jnp.exp(
        -jnp.log(jnp.float32(130000.0)) * jnp.arange(half, dtype=jnp.float32) * (2.0 / HEAD_SIZE)
    )
    angle = new_pos.astype(jnp.float32)[:, None] * inverse[None, :]
    angle = jnp.concatenate([angle] * (4 * heads_here), axis=-1)
    trig = jnp.concatenate([jnp.cos(angle), jnp.sin(angle)], axis=-1)
    sink_rows = sink_keys.astype(jnp.float32).reshape(
        rows, lanes * tn // HEAD_SIZE, HEAD_SIZE, sink_keys.shape[2]
    )
    states, sink_rows = lax.optimization_barrier((states, sink_rows))
    qkv_all, mine = head(states, attn_gain, jnp.transpose(w_qkv, (1, 2, 0)), trig, tn, 0)
    batch = qkv_all.shape[0]
    keys_all = qkv_all[:, lanes : 2 * lanes]
    values_all = qkv_all[:, 2 * lanes : 3 * lanes]
    mine = mine.reshape(tn, rows, 4, heads_here, HEAD_SIZE)
    mine = jnp.transpose(mine, (1, 2, 0, 3, 4)).reshape(rows, 4, tn * heads_here, HEAD_SIZE)
    queries = mine[:, 0]
    keys_new = mine[:, 1]
    values_new = mine[:, 2]
    all_heads = queries.shape[1]
    own_len = lax.dynamic_slice_in_dim(cache_len, row_start, rows, 0)
    own_pos = lax.dynamic_slice_in_dim(new_pos, row_start, rows, 0)
    window_here = key_cache.shape[2]
    seq_index = lax.axis_index("seq")
    slots = seq_index * window_here + jnp.arange(window_here, dtype=jnp.int32)
    live = (slots[None, :] < own_len[:, None]) & (slot_mask == 1)
    live = live & (slot_pos < own_pos[:, None]) & (own_pos[:, None] - slot_pos < WINDOW)
    live = live[:, None, :]
    first_shard = seq_index == 0
    kwin = key_cache.reshape(rows, all_heads, HEAD_SIZE, window_here)
    vwin = value_cache.reshape(rows, all_heads, HEAD_SIZE, window_here)
    sink_key_rows = sink_keys.reshape(rows, all_heads, HEAD_SIZE, sink_keys.shape[2])
    vsink = sink_values.reshape(rows, all_heads, HEAD_SIZE, sink_values.shape[2])
    score_win = (
        jnp.einsum("bhd,bhds->bhs", queries, kwin, preferred_element_type=jnp.float32) * 0.125
    )
    score_win = jnp.where(live, score_win, NEG)
    score_sink = (
        jnp.sum(
            queries.astype(jnp.float32)[..., None] * sink_rows, axis=2
        )
        * 0.125
    )
    score_sink = jnp.where(first_shard, score_sink, NEG)
    score_new = jnp.sum(queries.astype(jnp.float32) * keys_new.astype(jnp.float32), axis=-1) * 0.125
    score_new = jnp.where(first_shard, score_new, NEG)
    local_top = jnp.maximum(
        jnp.maximum(jnp.max(score_win, axis=-1), jnp.max(score_sink, axis=-1)), score_new
    )
    weight_win = jnp.where(live, jnp.exp(score_win - local_top[..., None]), 0.0)
    weight_sink = jnp.where(first_shard, jnp.exp(score_sink - local_top[..., None]), 0.0)
    weight_new = jnp.where(first_shard, jnp.exp(score_new - local_top), 0.0)
    total = jnp.sum(weight_win, axis=-1) + jnp.sum(weight_sink, axis=-1) + weight_new
    mixture = jnp.einsum(
        "bhs,bhds->bhd", weight_win.astype(jnp.bfloat16), vwin, preferred_element_type=jnp.float32
    )
    mixture = mixture + jnp.sum(
        undo_round(weight_sink)[:, :, None, :] * vsink.astype(jnp.float32), axis=-1
    )
    mixture = mixture + undo_round(weight_new)[..., None] * values_new.astype(jnp.float32)
    packed = jnp.concatenate([mixture, total[..., None], local_top[..., None]], axis=-1)
    packed = jnp.transpose(packed, (1, 0, 2))
    mlp_out, resid_part = tail(packed, w_out, states, mlp_gain, w_gate_up, w_down, tn, sn, 3)
    out_states = (resid_part.astype(jnp.float32) + mlp_out).astype(jnp.bfloat16)
    return (out_states, keys_all, values_all)


def solution(mesh):
    in_specs = (
        P("tensor", None),
        P(),
        P(None, None, "tensor"),
        P("tensor", None),
        P(),
        P(None, None, "tensor"),
        P("tensor", None),
        P("tensor", None, "seq"),
        P("tensor", None, "seq"),
        P("tensor", None, None),
        P("tensor", None, None),
        P(),
        P("tensor", "seq"),
        P("tensor", "seq"),
        P(),
    )
    out_specs = (P("tensor", None), P(None, "tensor"), P(None, "tensor"))
    body = functools.partial(per_device, tn=mesh.shape["tensor"], sn=mesh.shape["seq"])
    return jax.shard_map(
        body, mesh=mesh, in_specs=in_specs, out_specs=out_specs, check_vma=False
    )
```

```python
import functools

import jax
import jax.numpy as jnp
from jax import lax
from jax.experimental import pallas as pl
from jax.experimental.pallas import tpu as pltpu
from jax.sharding import PartitionSpec as P

HEAD_SIZE = 64
WINDOW = 4096


NEG = -1e30
MESH_ID = pl.DeviceIdType.MESH


def rms_norm(values, gain):
    meansq = jnp.mean(values * values, axis=-1, keepdims=True)
    return (values * lax.rsqrt(meansq + 1e-05) * gain.astype(jnp.float32)).astype(jnp.bfloat16)


def rotary(tensor, cosine, sine):
    half = tensor.shape[-1] // 2
    turned = jnp.concatenate([-tensor[..., half:], tensor[..., :half]], axis=-1)
    return tensor * cosine + turned * sine


def undo_round(weights):
    rounded = lax.optimization_barrier(weights.astype(jnp.bfloat16))
    return rounded.astype(jnp.float32)


def _exchange_kernel(n, axis, gather, x_ref, y_ref, send_sem, recv_sem, local_sem):
    me = lax.axis_index(axis)
    barrier = pltpu.get_barrier_semaphore()

    def greet(d, carry):
        peer = lax.rem(me + d, n)
        pl.semaphore_signal(barrier, 1, device_id={axis: peer}, device_id_type=MESH_ID)
        return carry

    lax.fori_loop(1, n, greet, 0)
    pl.semaphore_wait(barrier, n - 1)

    def source(j):
        return x_ref if gather else x_ref.at[j]

    def outgoing(d):
        j = lax.rem(me + d, n)
        return pltpu.make_async_remote_copy(
            src_ref=source(j),
            dst_ref=y_ref.at[me],
            send_sem=send_sem.at[j],
            recv_sem=recv_sem.at[me],
            device_id={axis: j},
            device_id_type=MESH_ID,
        )

    def incoming(d):
        k = lax.rem(me + n - d, n)
        return pltpu.make_async_remote_copy(
            src_ref=source(k),
            dst_ref=y_ref.at[k],
            send_sem=send_sem.at[k],
            recv_sem=recv_sem.at[k],
            device_id={axis: k},
            device_id_type=MESH_ID,
        )

    local = pltpu.make_async_copy(source(me), y_ref.at[me], local_sem)
    local.start()

    def start(d, carry):
        outgoing(d).start()
        return carry

    lax.fori_loop(1, n, start, 0)

    def finish(d, carry):
        outgoing(d).wait_send()
        incoming(d).wait_recv()
        return carry

    lax.fori_loop(1, n, finish, 0)
    local.wait()


def exchange(x, axis, n, cid, gather=False):
    piece = x.shape if gather else x.shape[1:]
    return pl.pallas_call(
        functools.partial(_exchange_kernel, n, axis, gather),
        out_shape=jax.ShapeDtypeStruct((n,) + tuple(piece), x.dtype),
        in_specs=[pl.BlockSpec(memory_space=pl.ANY)],
        out_specs=pl.BlockSpec(memory_space=pl.ANY),
        scratch_shapes=[
            pltpu.SemaphoreType.DMA((n,)),
            pltpu.SemaphoreType.DMA((n,)),
            pltpu.SemaphoreType.DMA(()),
        ],
        compiler_params=pltpu.CompilerParams(collective_id=cid, has_side_effects=True),
    )(x)


def _tail_kernel(
    n,
    sn,
    part_ref,
    w_out_ref,
    states_ref,
    gain_ref,
    gate_ref,
    down_ref,
    out_ref,
    seq_buf,
    att_buf,
    seq_send,
    seq_recv,
    abuf,
    pbuf,
    rbuf,
    sbuf,
    nbuf,
    gbuf,
    qbuf,
    rbuf2,
    send_sem,
    recv_sem,
    local_sem,
):
    axis = "tensor"
    me = lax.axis_index(axis)
    seq_me = lax.axis_index("seq")
    rows = states_ref.shape[0]
    barrier = pltpu.get_barrier_semaphore()

    def greet(d, carry):
        pl.semaphore_signal(
            barrier, 1, device_id={axis: lax.rem(me + d, n)}, device_id_type=MESH_ID
        )
        return carry

    lax.fori_loop(1, n, greet, 0)

    def greet_seq(d, carry):
        pl.semaphore_signal(
            barrier, 1, device_id={"seq": lax.rem(seq_me + d, sn)}, device_id_type=MESH_ID
        )
        return carry

    lax.fori_loop(1, sn, greet_seq, 0)
    pl.semaphore_wait(barrier, n - 1 + sn - 1)

    def seq_out(d):
        j = lax.rem(seq_me + d, sn)
        return pltpu.make_async_remote_copy(
            src_ref=part_ref,
            dst_ref=seq_buf.at[seq_me],
            send_sem=seq_send.at[j],
            recv_sem=seq_recv.at[seq_me],
            device_id={"seq": j},
            device_id_type=MESH_ID,
        )

    def seq_in(d):
        k = lax.rem(seq_me + sn - d, sn)
        return pltpu.make_async_remote_copy(
            src_ref=part_ref,
            dst_ref=seq_buf.at[k],
            send_sem=seq_send.at[k],
            recv_sem=seq_recv.at[k],
            device_id={"seq": k},
            device_id_type=MESH_ID,
        )

    seq_local = pltpu.make_async_copy(part_ref, seq_buf.at[seq_me], local_sem)
    seq_local.start()

    def seq_start(d, carry):
        seq_out(d).start()
        return carry

    lax.fori_loop(1, sn, seq_start, 0)

    def seq_finish(d, carry):
        seq_out(d).wait_send()
        seq_in(d).wait_recv()
        return carry

    lax.fori_loop(1, sn, seq_finish, 0)
    seq_local.wait()
    parts = seq_buf[...]
    lanes = att_buf.shape[2]
    part_top = parts[..., lanes + 1 : lanes + 2]
    top = jnp.max(part_top, axis=0)
    scale = jnp.exp(part_top - top[None])
    total = jnp.sum(parts[..., lanes : lanes + 1] * scale, axis=0)
    mixture = jnp.sum(parts[..., :lanes] * scale, axis=0)
    att_buf[...] = (mixture / total).astype(att_buf.dtype)
    units = down_ref.shape[0]

    def phase(p, src_of, dst_of):
        def outgoing(d):
            j = lax.rem(me + d, n)
            return pltpu.make_async_remote_copy(
                src_ref=src_of(j),
                dst_ref=dst_of(me),
                send_sem=send_sem.at[p, j],
                recv_sem=recv_sem.at[p, me],
                device_id={axis: j},
                device_id_type=MESH_ID,
            )

        def incoming(d):
            k = lax.rem(me + n - d, n)
            return pltpu.make_async_remote_copy(
                src_ref=src_of(k),
                dst_ref=dst_of(k),
                send_sem=send_sem.at[p, k],
                recv_sem=recv_sem.at[p, k],
                device_id={axis: k},
                device_id_type=MESH_ID,
            )

        local = pltpu.make_async_copy(src_of(me), dst_of(me), local_sem)
        local.start()

        def start(d, carry):
            outgoing(d).start()
            return carry

        lax.fori_loop(1, n, start, 0)

        def finish(d, carry):
            outgoing(d).wait_send()
            incoming(d).wait_recv()
            return carry

        lax.fori_loop(1, n, finish, 0)
        local.wait()

    def row_block(ref):
        return lambda i: ref.at[pl.ds(i * rows, rows)]

    phase(0, lambda j: att_buf.at[j], row_block(abuf))
    partial = jnp.dot(abuf[...], w_out_ref[...], preferred_element_type=jnp.float32)
    pbuf[...] = partial.astype(jnp.bfloat16)
    phase(1, row_block(pbuf), lambda k: rbuf.at[k])
    summed = jnp.sum(rbuf[...].astype(jnp.float32), axis=0)
    resid = (states_ref[...].astype(jnp.float32) + summed).astype(jnp.bfloat16)
    sbuf[...] = resid
    nbuf[...] = rms_norm(resid.astype(jnp.float32), gain_ref[...].reshape(1, -1))
    phase(2, lambda j: nbuf, row_block(gbuf))
    gate_up = jnp.dot(gbuf[...], gate_ref[...], preferred_element_type=jnp.float32)
    hidden = (jax.nn.silu(gate_up[:, :units]) * gate_up[:, units:]).astype(jnp.bfloat16)
    down = jnp.dot(hidden, down_ref[...], preferred_element_type=jnp.float32)
    qbuf[...] = down.astype(jnp.bfloat16)
    phase(3, row_block(qbuf), lambda k: rbuf2.at[k])
    summed2 = jnp.sum(rbuf2[...].astype(jnp.float32), axis=0)
    out_ref[...] = (sbuf[...].astype(jnp.float32) + summed2).astype(out_ref.dtype)


def tail(part, w_out, states, gain, w_gate_up, w_down, n, sn, cid):
    rows, width = states.shape
    lanes = part.shape[2] - 2
    units = w_gate_up.shape[2]
    vmem = pl.BlockSpec(memory_space=pltpu.VMEM)
    return pl.pallas_call(
        functools.partial(_tail_kernel, n, sn),
        out_shape=jax.ShapeDtypeStruct((rows, width), states.dtype),
        in_specs=[vmem] * 6,
        out_specs=vmem,
        scratch_shapes=[
            pltpu.VMEM((sn,) + part.shape, jnp.float32),
            pltpu.VMEM((n, rows, lanes), jnp.bfloat16),
            pltpu.SemaphoreType.DMA((sn,)),
            pltpu.SemaphoreType.DMA((sn,)),
            pltpu.VMEM((n * rows, lanes), jnp.bfloat16),
            pltpu.VMEM((n * rows, width), jnp.bfloat16),
            pltpu.VMEM((n, rows, width), jnp.bfloat16),
            pltpu.VMEM((rows, width), jnp.bfloat16),
            pltpu.VMEM((rows, width), jnp.bfloat16),
            pltpu.VMEM((n * rows, width), jnp.bfloat16),
            pltpu.VMEM((n * rows, width), jnp.bfloat16),
            pltpu.VMEM((n, rows, width), jnp.bfloat16),
            pltpu.SemaphoreType.DMA((4, n)),
            pltpu.SemaphoreType.DMA((4, n)),
            pltpu.SemaphoreType.DMA(()),
        ],
        compiler_params=pltpu.CompilerParams(
            collective_id=cid, has_side_effects=True, vmem_limit_bytes=32 * 1024 * 1024
        ),
    )(part, w_out, states, gain, w_gate_up.reshape(width, 2 * units), w_down)


def _head_kernel(
    n, states_ref, gains_ref, w_ref, trig_ref, qkv_ref, recv_ref, x_ref, gbuf, send_sem, recv_sem, local_sem
):
    axis = "tensor"
    me = lax.axis_index(axis)
    rows = x_ref.shape[0]
    block = qkv_ref.shape[1] // 2
    x_ref[...] = rms_norm(states_ref[...].astype(jnp.float32), gains_ref[...].reshape(1, -1))
    barrier = pltpu.get_barrier_semaphore()

    def greet(d, carry):
        pl.semaphore_signal(
            barrier, 1, device_id={axis: lax.rem(me + d, n)}, device_id_type=MESH_ID
        )
        return carry

    lax.fori_loop(1, n, greet, 0)
    pl.semaphore_wait(barrier, n - 1)

    def phase(p, src_of, dst_of):
        def outgoing(d):
            j = lax.rem(me + d, n)
            return pltpu.make_async_remote_copy(
                src_ref=src_of(j),
                dst_ref=dst_of(me),
                send_sem=send_sem.at[p, j],
                recv_sem=recv_sem.at[p, me],
                device_id={axis: j},
                device_id_type=MESH_ID,
            )

        def incoming(d):
            k = lax.rem(me + n - d, n)
            return pltpu.make_async_remote_copy(
                src_ref=src_of(k),
                dst_ref=dst_of(k),
                send_sem=send_sem.at[p, k],
                recv_sem=recv_sem.at[p, k],
                device_id={axis: k},
                device_id_type=MESH_ID,
            )

        local = pltpu.make_async_copy(src_of(me), dst_of(me), local_sem)
        local.start()

        def start(d, carry):
            outgoing(d).start()
            return carry

        lax.fori_loop(1, n, start, 0)

        def finish(d, carry):
            outgoing(d).wait_send()
            incoming(d).wait_recv()
            return carry

        lax.fori_loop(1, n, finish, 0)
        local.wait()

    phase(0, lambda j: x_ref, lambda k: gbuf.at[pl.ds(k * rows, rows)])
    lanes = w_ref.shape[1]
    gathered = gbuf[...]
    contract_last = (((1,), (1,)), ((), ()))
    pair = lax.dot_general(
        gathered,
        w_ref[0:2].reshape(2 * lanes, w_ref.shape[2]),
        contract_last,
        preferred_element_type=jnp.float32,
    )
    value_proj = lax.dot_general(
        gathered, w_ref[2], contract_last, preferred_element_type=jnp.float32
    )
    trig = trig_ref[...]
    half = HEAD_SIZE // 2
    lane = lax.broadcasted_iota(jnp.int32, pair.shape, 1)
    turned = jnp.where(
        lane % HEAD_SIZE < half,
        -pltpu.roll(pair, block - half, 1),
        pltpu.roll(pair, half, 1),
    )
    rotated = pair * trig[:, :block] + turned * trig[:, block:]
    qkv_ref[:, :block] = rotated.astype(qkv_ref.dtype)
    qkv_ref[:, block : block + block // 2] = value_proj.astype(qkv_ref.dtype)
    qkv_ref[:, block + block // 2 :] = jnp.zeros((pair.shape[0], block // 2), qkv_ref.dtype)
    phase(1, lambda j: qkv_ref.at[pl.ds(j * rows, rows)], lambda k: recv_ref.at[k])


def head(states, gains, w_ext, trig, n, cid):
    rows, width = states.shape
    cols = w_ext.shape[1] * 4
    vmem = pl.BlockSpec(memory_space=pltpu.VMEM)
    return pl.pallas_call(
        functools.partial(_head_kernel, n),
        out_shape=(
            jax.ShapeDtypeStruct((n * rows, cols), jnp.bfloat16),
            jax.ShapeDtypeStruct((n, rows, cols), jnp.bfloat16),
        ),
        in_specs=[vmem] * 4,
        out_specs=(vmem, vmem),
        scratch_shapes=[
            pltpu.VMEM((rows, width), jnp.bfloat16),
            pltpu.VMEM((n * rows, width), jnp.bfloat16),
            pltpu.SemaphoreType.DMA((2, n)),
            pltpu.SemaphoreType.DMA((2, n)),
            pltpu.SemaphoreType.DMA(()),
        ],
        compiler_params=pltpu.CompilerParams(
            collective_id=cid, has_side_effects=True, vmem_limit_bytes=8 * 1024 * 1024
        ),
    )(states, gains, w_ext, trig)


def per_device(
    states,
    attn_gain,
    w_qkv,
    w_out,
    mlp_gain,
    w_gate_up,
    w_down,
    key_cache,
    value_cache,
    sink_keys,
    sink_values,
    cache_len,
    slot_mask,
    slot_pos,
    new_pos,
    tn,
    sn,
):
    rows = states.shape[0]
    width = states.shape[1]
    row_start = lax.axis_index("tensor") * rows
    floats = states.astype(jnp.float32)
    lanes = w_qkv.shape[2]
    heads_here = lanes // HEAD_SIZE
    half = HEAD_SIZE // 2
    inverse = jnp.exp(
        -jnp.log(jnp.float32(130000.0)) * jnp.arange(half, dtype=jnp.float32) * (2.0 / HEAD_SIZE)
    )
    angle = new_pos.astype(jnp.float32)[:, None] * inverse[None, :]
    angle = jnp.concatenate([angle] * (4 * heads_here), axis=-1)
    trig = jnp.concatenate([jnp.cos(angle), jnp.sin(angle)], axis=-1)
    sink_rows = sink_keys.astype(jnp.float32).reshape(
        rows, lanes * tn // HEAD_SIZE, HEAD_SIZE, sink_keys.shape[2]
    )
    states, sink_rows = lax.optimization_barrier((states, sink_rows))
    qkv_all, mine = head(states, attn_gain, jnp.transpose(w_qkv, (1, 2, 0)), trig, tn, 0)
    batch = qkv_all.shape[0]
    keys_all = qkv_all[:, lanes : 2 * lanes]
    values_all = qkv_all[:, 2 * lanes : 3 * lanes]
    mine = mine.reshape(tn, rows, 4, heads_here, HEAD_SIZE)
    mine = jnp.transpose(mine, (1, 2, 0, 3, 4)).reshape(rows, 4, tn * heads_here, HEAD_SIZE)
    queries = mine[:, 0]
    keys_new = mine[:, 1]
    values_new = mine[:, 2]
    all_heads = queries.shape[1]
    own_len = lax.dynamic_slice_in_dim(cache_len, row_start, rows, 0)
    own_pos = lax.dynamic_slice_in_dim(new_pos, row_start, rows, 0)
    window_here = key_cache.shape[2]
    seq_index = lax.axis_index("seq")
    slots = seq_index * window_here + jnp.arange(window_here, dtype=jnp.int32)
    live = (slots[None, :] < own_len[:, None]) & (slot_mask == 1)
    live = live & (slot_pos < own_pos[:, None]) & (own_pos[:, None] - slot_pos < WINDOW)
    live = live[:, None, :]
    first_shard = seq_index == 0
    kwin = key_cache.reshape(rows, all_heads, HEAD_SIZE, window_here)
    vwin = value_cache.reshape(rows, all_heads, HEAD_SIZE, window_here)
    sink_key_rows = sink_keys.reshape(rows, all_heads, HEAD_SIZE, sink_keys.shape[2])
    vsink = sink_values.reshape(rows, all_heads, HEAD_SIZE, sink_values.shape[2])
    score_win = (
        jnp.einsum("bhd,bhds->bhs", queries, kwin, preferred_element_type=jnp.float32) * 0.125
    )
    score_win = jnp.where(live, score_win, NEG)
    score_sink = (
        jnp.sum(
            queries.astype(jnp.float32)[..., None] * sink_rows, axis=2
        )
        * 0.125
    )
    score_sink = jnp.where(first_shard, score_sink, NEG)
    score_new = jnp.sum(queries.astype(jnp.float32) * keys_new.astype(jnp.float32), axis=-1) * 0.125
    score_new = jnp.where(first_shard, score_new, NEG)
    local_top = jnp.maximum(
        jnp.maximum(jnp.max(score_win, axis=-1), jnp.max(score_sink, axis=-1)), score_new
    )
    weight_win = jnp.where(live, jnp.exp(score_win - local_top[..., None]), 0.0)
    weight_sink = jnp.where(first_shard, jnp.exp(score_sink - local_top[..., None]), 0.0)
    weight_new = jnp.where(first_shard, jnp.exp(score_new - local_top), 0.0)
    total = jnp.sum(weight_win, axis=-1) + jnp.sum(weight_sink, axis=-1) + weight_new
    mixture = jnp.einsum(
        "bhs,bhds->bhd", weight_win.astype(jnp.bfloat16), vwin, preferred_element_type=jnp.float32
    )
    mixture = mixture + jnp.sum(
        undo_round(weight_sink)[:, :, None, :] * vsink.astype(jnp.float32), axis=-1
    )
    mixture = mixture + undo_round(weight_new)[..., None] * values_new.astype(jnp.float32)
    packed = jnp.concatenate([mixture, total[..., None], local_top[..., None]], axis=-1)
    packed = jnp.transpose(packed, (1, 0, 2))
    out_states = tail(packed, w_out, states, mlp_gain, w_gate_up, w_down, tn, sn, 3)
    return (out_states, keys_all, values_all)


def solution(mesh):
    in_specs = (
        P("tensor", None),
        P(),
        P(None, None, "tensor"),
        P("tensor", None),
        P(),
        P(None, None, "tensor"),
        P("tensor", None),
        P("tensor", None, "seq"),
        P("tensor", None, "seq"),
        P("tensor", None, None),
        P("tensor", None, None),
        P(),
        P("tensor", "seq"),
        P("tensor", "seq"),
        P(),
    )
    out_specs = (P("tensor", None), P(None, "tensor"), P(None, "tensor"))
    body = functools.partial(per_device, tn=mesh.shape["tensor"], sn=mesh.shape["seq"])
    return jax.shard_map(
        body, mesh=mesh, in_specs=in_specs, out_specs=out_specs, check_vma=False
    )
```

```python
import functools

import jax
import jax.numpy as jnp
from jax import lax
from jax.experimental import pallas as pl
from jax.experimental.pallas import tpu as pltpu
from jax.sharding import PartitionSpec as P

HEAD_SIZE = 64
WINDOW = 4096


NEG = -1e30
MESH_ID = pl.DeviceIdType.MESH


def rms_norm(values, gain):
    meansq = jnp.mean(values * values, axis=-1, keepdims=True)
    return (values * lax.rsqrt(meansq + 1e-05) * gain.astype(jnp.float32)).astype(jnp.bfloat16)


def rotary(tensor, cosine, sine):
    half = tensor.shape[-1] // 2
    turned = jnp.concatenate([-tensor[..., half:], tensor[..., :half]], axis=-1)
    return tensor * cosine + turned * sine


def undo_round(weights):
    rounded = lax.optimization_barrier(weights.astype(jnp.bfloat16))
    return rounded.astype(jnp.float32)


def _exchange_kernel(n, axis, gather, x_ref, y_ref, send_sem, recv_sem, local_sem):
    me = lax.axis_index(axis)
    barrier = pltpu.get_barrier_semaphore()

    def greet(d, carry):
        peer = lax.rem(me + d, n)
        pl.semaphore_signal(barrier, 1, device_id={axis: peer}, device_id_type=MESH_ID)
        return carry

    lax.fori_loop(1, n, greet, 0)
    pl.semaphore_wait(barrier, n - 1)

    def source(j):
        return x_ref if gather else x_ref.at[j]

    def outgoing(d):
        j = lax.rem(me + d, n)
        return pltpu.make_async_remote_copy(
            src_ref=source(j),
            dst_ref=y_ref.at[me],
            send_sem=send_sem.at[j],
            recv_sem=recv_sem.at[me],
            device_id={axis: j},
            device_id_type=MESH_ID,
        )

    def incoming(d):
        k = lax.rem(me + n - d, n)
        return pltpu.make_async_remote_copy(
            src_ref=source(k),
            dst_ref=y_ref.at[k],
            send_sem=send_sem.at[k],
            recv_sem=recv_sem.at[k],
            device_id={axis: k},
            device_id_type=MESH_ID,
        )

    local = pltpu.make_async_copy(source(me), y_ref.at[me], local_sem)
    local.start()

    def start(d, carry):
        outgoing(d).start()
        return carry

    lax.fori_loop(1, n, start, 0)

    def finish(d, carry):
        outgoing(d).wait_send()
        incoming(d).wait_recv()
        return carry

    lax.fori_loop(1, n, finish, 0)
    local.wait()


def exchange(x, axis, n, cid, gather=False):
    piece = x.shape if gather else x.shape[1:]
    return pl.pallas_call(
        functools.partial(_exchange_kernel, n, axis, gather),
        out_shape=jax.ShapeDtypeStruct((n,) + tuple(piece), x.dtype),
        in_specs=[pl.BlockSpec(memory_space=pl.ANY)],
        out_specs=pl.BlockSpec(memory_space=pl.ANY),
        scratch_shapes=[
            pltpu.SemaphoreType.DMA((n,)),
            pltpu.SemaphoreType.DMA((n,)),
            pltpu.SemaphoreType.DMA(()),
        ],
        compiler_params=pltpu.CompilerParams(collective_id=cid, has_side_effects=True),
    )(x)


def _tail_kernel(
    n,
    sn,
    part_ref,
    w_out_ref,
    states_ref,
    gain_ref,
    gate_ref,
    down_ref,
    out_ref,
    seq_buf,
    att_buf,
    seq_send,
    seq_recv,
    abuf,
    pbuf,
    rbuf,
    sbuf,
    nbuf,
    gbuf,
    qbuf,
    rbuf2,
    send_sem,
    recv_sem,
    local_sem,
):
    axis = "tensor"
    me = lax.axis_index(axis)
    seq_me = lax.axis_index("seq")
    rows = states_ref.shape[0]
    barrier = pltpu.get_barrier_semaphore()

    def greet(d, carry):
        pl.semaphore_signal(
            barrier, 1, device_id={axis: lax.rem(me + d, n)}, device_id_type=MESH_ID
        )
        return carry

    lax.fori_loop(1, n, greet, 0)

    def greet_seq(d, carry):
        pl.semaphore_signal(
            barrier, 1, device_id={"seq": lax.rem(seq_me + d, sn)}, device_id_type=MESH_ID
        )
        return carry

    lax.fori_loop(1, sn, greet_seq, 0)
    pl.semaphore_wait(barrier, n - 1 + sn - 1)

    def seq_out(d):
        j = lax.rem(seq_me + d, sn)
        return pltpu.make_async_remote_copy(
            src_ref=part_ref,
            dst_ref=seq_buf.at[seq_me],
            send_sem=seq_send.at[j],
            recv_sem=seq_recv.at[seq_me],
            device_id={"seq": j},
            device_id_type=MESH_ID,
        )

    def seq_in(d):
        k = lax.rem(seq_me + sn - d, sn)
        return pltpu.make_async_remote_copy(
            src_ref=part_ref,
            dst_ref=seq_buf.at[k],
            send_sem=seq_send.at[k],
            recv_sem=seq_recv.at[k],
            device_id={"seq": k},
            device_id_type=MESH_ID,
        )

    seq_local = pltpu.make_async_copy(part_ref, seq_buf.at[seq_me], local_sem)
    seq_local.start()

    def seq_start(d, carry):
        seq_out(d).start()
        return carry

    lax.fori_loop(1, sn, seq_start, 0)

    def seq_finish(d, carry):
        seq_out(d).wait_send()
        seq_in(d).wait_recv()
        return carry

    lax.fori_loop(1, sn, seq_finish, 0)
    seq_local.wait()
    parts = seq_buf[...]
    lanes = att_buf.shape[2]
    part_top = parts[..., lanes + 1 : lanes + 2]
    top = jnp.max(part_top, axis=0)
    scale = jnp.exp(part_top - top[None])
    total = jnp.sum(parts[..., lanes : lanes + 1] * scale, axis=0)
    mixture = jnp.sum(parts[..., :lanes] * scale, axis=0)
    att_buf[...] = (mixture / total).astype(att_buf.dtype)
    units = down_ref.shape[0]

    def phase(p, src_of, dst_of):
        def outgoing(d):
            j = lax.rem(me + d, n)
            return pltpu.make_async_remote_copy(
                src_ref=src_of(j),
                dst_ref=dst_of(me),
                send_sem=send_sem.at[p, j],
                recv_sem=recv_sem.at[p, me],
                device_id={axis: j},
                device_id_type=MESH_ID,
            )

        def incoming(d):
            k = lax.rem(me + n - d, n)
            return pltpu.make_async_remote_copy(
                src_ref=src_of(k),
                dst_ref=dst_of(k),
                send_sem=send_sem.at[p, k],
                recv_sem=recv_sem.at[p, k],
                device_id={axis: k},
                device_id_type=MESH_ID,
            )

        local = pltpu.make_async_copy(src_of(me), dst_of(me), local_sem)
        local.start()

        def start(d, carry):
            outgoing(d).start()
            return carry

        lax.fori_loop(1, n, start, 0)

        def finish(d, carry):
            outgoing(d).wait_send()
            incoming(d).wait_recv()
            return carry

        lax.fori_loop(1, n, finish, 0)
        local.wait()

    def row_block(ref):
        return lambda i: ref.at[pl.ds(i * rows, rows)]

    phase(0, lambda j: att_buf.at[j], row_block(abuf))
    partial = jnp.dot(abuf[...], w_out_ref[...], preferred_element_type=jnp.float32)
    pbuf[...] = partial.astype(jnp.bfloat16)
    phase(1, row_block(pbuf), lambda k: rbuf.at[k])
    summed = jnp.sum(rbuf[...].astype(jnp.float32), axis=0)
    resid = (states_ref[...].astype(jnp.float32) + summed).astype(jnp.bfloat16)
    sbuf[...] = resid
    nbuf[...] = rms_norm(resid.astype(jnp.float32), gain_ref[...].reshape(1, -1))
    phase(2, lambda j: nbuf, row_block(gbuf))
    gate_up = jnp.dot(gbuf[...], gate_ref[...], preferred_element_type=jnp.float32)
    hidden = (jax.nn.silu(gate_up[:, :units]) * gate_up[:, units:]).astype(jnp.bfloat16)
    down = jnp.dot(hidden, down_ref[...], preferred_element_type=jnp.float32)
    qbuf[...] = down.astype(jnp.bfloat16)
    phase(3, row_block(qbuf), lambda k: rbuf2.at[k])
    summed2 = jnp.sum(rbuf2[...].astype(jnp.float32), axis=0)
    out_ref[...] = (sbuf[...].astype(jnp.float32) + summed2).astype(out_ref.dtype)


def tail(part, w_out, states, gain, w_gate_up, w_down, n, sn, cid):
    rows, width = states.shape
    lanes = part.shape[2] - 2
    units = w_gate_up.shape[2]
    vmem = pl.BlockSpec(memory_space=pltpu.VMEM)
    return pl.pallas_call(
        functools.partial(_tail_kernel, n, sn),
        out_shape=jax.ShapeDtypeStruct((rows, width), states.dtype),
        in_specs=[vmem] * 6,
        out_specs=vmem,
        scratch_shapes=[
            pltpu.VMEM((sn,) + part.shape, jnp.float32),
            pltpu.VMEM((n, rows, lanes), jnp.bfloat16),
            pltpu.SemaphoreType.DMA((sn,)),
            pltpu.SemaphoreType.DMA((sn,)),
            pltpu.VMEM((n * rows, lanes), jnp.bfloat16),
            pltpu.VMEM((n * rows, width), jnp.bfloat16),
            pltpu.VMEM((n, rows, width), jnp.bfloat16),
            pltpu.VMEM((rows, width), jnp.bfloat16),
            pltpu.VMEM((rows, width), jnp.bfloat16),
            pltpu.VMEM((n * rows, width), jnp.bfloat16),
            pltpu.VMEM((n * rows, width), jnp.bfloat16),
            pltpu.VMEM((n, rows, width), jnp.bfloat16),
            pltpu.SemaphoreType.DMA((4, n)),
            pltpu.SemaphoreType.DMA((4, n)),
            pltpu.SemaphoreType.DMA(()),
        ],
        compiler_params=pltpu.CompilerParams(collective_id=cid, has_side_effects=True),
    )(part, w_out, states, gain, w_gate_up.reshape(width, 2 * units), w_down)


def _head_kernel(
    n, states_ref, gains_ref, w_ref, trig_ref, qkv_ref, recv_ref, x_ref, gbuf, send_sem, recv_sem, local_sem
):
    axis = "tensor"
    me = lax.axis_index(axis)
    rows = x_ref.shape[0]
    block = qkv_ref.shape[1] // 2
    x_ref[...] = rms_norm(states_ref[...].astype(jnp.float32), gains_ref[...].reshape(1, -1))
    barrier = pltpu.get_barrier_semaphore()

    def greet(d, carry):
        pl.semaphore_signal(
            barrier, 1, device_id={axis: lax.rem(me + d, n)}, device_id_type=MESH_ID
        )
        return carry

    lax.fori_loop(1, n, greet, 0)
    pl.semaphore_wait(barrier, n - 1)

    def phase(p, src_of, dst_of):
        def outgoing(d):
            j = lax.rem(me + d, n)
            return pltpu.make_async_remote_copy(
                src_ref=src_of(j),
                dst_ref=dst_of(me),
                send_sem=send_sem.at[p, j],
                recv_sem=recv_sem.at[p, me],
                device_id={axis: j},
                device_id_type=MESH_ID,
            )

        def incoming(d):
            k = lax.rem(me + n - d, n)
            return pltpu.make_async_remote_copy(
                src_ref=src_of(k),
                dst_ref=dst_of(k),
                send_sem=send_sem.at[p, k],
                recv_sem=recv_sem.at[p, k],
                device_id={axis: k},
                device_id_type=MESH_ID,
            )

        local = pltpu.make_async_copy(src_of(me), dst_of(me), local_sem)
        local.start()

        def start(d, carry):
            outgoing(d).start()
            return carry

        lax.fori_loop(1, n, start, 0)

        def finish(d, carry):
            outgoing(d).wait_send()
            incoming(d).wait_recv()
            return carry

        lax.fori_loop(1, n, finish, 0)
        local.wait()

    phase(0, lambda j: x_ref, lambda k: gbuf.at[pl.ds(k * rows, rows)])
    lanes = w_ref.shape[1]
    gathered = gbuf[...]
    contract_last = (((1,), (1,)), ((), ()))
    pair = lax.dot_general(
        gathered,
        w_ref[0:2].reshape(2 * lanes, w_ref.shape[2]),
        contract_last,
        preferred_element_type=jnp.float32,
    )
    value_proj = lax.dot_general(
        gathered, w_ref[2], contract_last, preferred_element_type=jnp.float32
    )
    trig = trig_ref[...]
    half = HEAD_SIZE // 2
    lane = lax.broadcasted_iota(jnp.int32, pair.shape, 1)
    turned = jnp.where(
        lane % HEAD_SIZE < half,
        -pltpu.roll(pair, block - half, 1),
        pltpu.roll(pair, half, 1),
    )
    rotated = pair * trig[:, :block] + turned * trig[:, block:]
    qkv_ref[:, :block] = rotated.astype(qkv_ref.dtype)
    qkv_ref[:, block : block + block // 2] = value_proj.astype(qkv_ref.dtype)
    qkv_ref[:, block + block // 2 :] = jnp.zeros((pair.shape[0], block // 2), qkv_ref.dtype)
    phase(1, lambda j: qkv_ref.at[pl.ds(j * rows, rows)], lambda k: recv_ref.at[k])


def head(states, gains, w_ext, trig, n, cid):
    rows, width = states.shape
    cols = w_ext.shape[1] * 4
    vmem = pl.BlockSpec(memory_space=pltpu.VMEM)
    return pl.pallas_call(
        functools.partial(_head_kernel, n),
        out_shape=(
            jax.ShapeDtypeStruct((n * rows, cols), jnp.bfloat16),
            jax.ShapeDtypeStruct((n, rows, cols), jnp.bfloat16),
        ),
        in_specs=[vmem] * 4,
        out_specs=(vmem, vmem),
        scratch_shapes=[
            pltpu.VMEM((rows, width), jnp.bfloat16),
            pltpu.VMEM((n * rows, width), jnp.bfloat16),
            pltpu.SemaphoreType.DMA((2, n)),
            pltpu.SemaphoreType.DMA((2, n)),
            pltpu.SemaphoreType.DMA(()),
        ],
        compiler_params=pltpu.CompilerParams(
            collective_id=cid, has_side_effects=True, vmem_limit_bytes=8 * 1024 * 1024
        ),
    )(states, gains, w_ext, trig)


def per_device(
    states,
    attn_gain,
    w_qkv,
    w_out,
    mlp_gain,
    w_gate_up,
    w_down,
    key_cache,
    value_cache,
    sink_keys,
    sink_values,
    cache_len,
    slot_mask,
    slot_pos,
    new_pos,
    tn,
    sn,
):
    rows = states.shape[0]
    width = states.shape[1]
    row_start = lax.axis_index("tensor") * rows
    floats = states.astype(jnp.float32)
    lanes = w_qkv.shape[2]
    heads_here = lanes // HEAD_SIZE
    half = HEAD_SIZE // 2
    inverse = jnp.exp(
        -jnp.log(jnp.float32(130000.0)) * jnp.arange(half, dtype=jnp.float32) * (2.0 / HEAD_SIZE)
    )
    angle = new_pos.astype(jnp.float32)[:, None] * inverse[None, :]
    angle = jnp.concatenate([angle] * (4 * heads_here), axis=-1)
    trig = jnp.concatenate([jnp.cos(angle), jnp.sin(angle)], axis=-1)
    sink_rows = sink_keys.astype(jnp.float32).reshape(
        rows, lanes * tn // HEAD_SIZE, HEAD_SIZE, sink_keys.shape[2]
    )
    states, sink_rows = lax.optimization_barrier((states, sink_rows))
    qkv_all, mine = head(states, attn_gain, jnp.transpose(w_qkv, (1, 2, 0)), trig, tn, 0)
    batch = qkv_all.shape[0]
    keys_all = qkv_all[:, lanes : 2 * lanes]
    values_all = qkv_all[:, 2 * lanes : 3 * lanes]
    mine = mine.reshape(tn, rows, 4, heads_here, HEAD_SIZE)
    mine = jnp.transpose(mine, (1, 2, 0, 3, 4)).reshape(rows, 4, tn * heads_here, HEAD_SIZE)
    queries = mine[:, 0]
    keys_new = mine[:, 1]
    values_new = mine[:, 2]
    all_heads = queries.shape[1]
    pick = jnp.arange(cache_len.shape[0], dtype=jnp.int32)[None, :] == (
        row_start + jnp.arange(rows, dtype=jnp.int32)
    )[:, None]
    own_len = jnp.sum(jnp.where(pick, cache_len[None, :], 0), axis=1)
    own_pos = jnp.sum(jnp.where(pick, new_pos[None, :], 0), axis=1)
    window_here = key_cache.shape[2]
    seq_index = lax.axis_index("seq")
    slots = seq_index * window_here + jnp.arange(window_here, dtype=jnp.int32)
    live = (slots[None, :] < own_len[:, None]) & (slot_mask == 1)
    live = live & (slot_pos < own_pos[:, None]) & (own_pos[:, None] - slot_pos < WINDOW)
    live = live[:, None, :]
    first_shard = seq_index == 0
    kwin = key_cache.reshape(rows, all_heads, HEAD_SIZE, window_here)
    vwin = value_cache.reshape(rows, all_heads, HEAD_SIZE, window_here)
    sink_key_rows = sink_keys.reshape(rows, all_heads, HEAD_SIZE, sink_keys.shape[2])
    vsink = sink_values.reshape(rows, all_heads, HEAD_SIZE, sink_values.shape[2])
    score_win = (
        jnp.einsum("bhd,bhds->bhs", queries, kwin, preferred_element_type=jnp.float32) * 0.125
    )
    score_win = jnp.where(live, score_win, NEG)
    score_sink = (
        jnp.sum(
            queries.astype(jnp.float32)[..., None] * sink_rows, axis=2
        )
        * 0.125
    )
    score_sink = jnp.where(first_shard, score_sink, NEG)
    score_new = jnp.sum(queries.astype(jnp.float32) * keys_new.astype(jnp.float32), axis=-1) * 0.125
    score_new = jnp.where(first_shard, score_new, NEG)
    local_top = jnp.maximum(
        jnp.maximum(jnp.max(score_win, axis=-1), jnp.max(score_sink, axis=-1)), score_new
    )
    weight_win = jnp.where(live, jnp.exp(score_win - local_top[..., None]), 0.0)
    weight_sink = jnp.where(first_shard, jnp.exp(score_sink - local_top[..., None]), 0.0)
    weight_new = jnp.where(first_shard, jnp.exp(score_new - local_top), 0.0)
    total = jnp.sum(weight_win, axis=-1) + jnp.sum(weight_sink, axis=-1) + weight_new
    mixture = jnp.einsum(
        "bhs,bhds->bhd", weight_win.astype(jnp.bfloat16), vwin, preferred_element_type=jnp.float32
    )
    mixture = mixture + jnp.sum(
        undo_round(weight_sink)[:, :, None, :] * vsink.astype(jnp.float32), axis=-1
    )
    mixture = mixture + undo_round(weight_new)[..., None] * values_new.astype(jnp.float32)
    packed = jnp.concatenate([mixture, total[..., None], local_top[..., None]], axis=-1)
    packed = jnp.transpose(packed, (1, 0, 2))
    out_states = tail(packed, w_out, states, mlp_gain, w_gate_up, w_down, tn, sn, 3)
    return (out_states, keys_all, values_all)


def solution(mesh):
    in_specs = (
        P("tensor", None),
        P(),
        P(None, None, "tensor"),
        P("tensor", None),
        P(),
        P(None, None, "tensor"),
        P("tensor", None),
        P("tensor", None, "seq"),
        P("tensor", None, "seq"),
        P("tensor", None, None),
        P("tensor", None, None),
        P(),
        P("tensor", "seq"),
        P("tensor", "seq"),
        P(),
    )
    out_specs = (P("tensor", None), P(None, "tensor"), P(None, "tensor"))
    body = functools.partial(per_device, tn=mesh.shape["tensor"], sn=mesh.shape["seq"])
    return jax.shard_map(
        body, mesh=mesh, in_specs=in_specs, out_specs=out_specs, check_vma=False
    )
```

```python
import functools

import jax
import jax.numpy as jnp
from jax import lax
from jax.experimental import pallas as pl
from jax.experimental.pallas import tpu as pltpu
from jax.sharding import PartitionSpec as P

HEAD_SIZE = 64
WINDOW = 4096


NEG = -1e30
MESH_ID = pl.DeviceIdType.MESH


def rms_norm(values, gain):
    meansq = jnp.mean(values * values, axis=-1, keepdims=True)
    return (values * lax.rsqrt(meansq + 1e-05) * gain.astype(jnp.float32)).astype(jnp.bfloat16)


def rotary(tensor, cosine, sine):
    half = tensor.shape[-1] // 2
    turned = jnp.concatenate([-tensor[..., half:], tensor[..., :half]], axis=-1)
    return tensor * cosine + turned * sine


def undo_round(weights):
    rounded = lax.optimization_barrier(weights.astype(jnp.bfloat16))
    return rounded.astype(jnp.float32)


def _exchange_kernel(n, axis, gather, x_ref, y_ref, send_sem, recv_sem, local_sem):
    me = lax.axis_index(axis)
    barrier = pltpu.get_barrier_semaphore()

    def greet(d, carry):
        peer = lax.rem(me + d, n)
        pl.semaphore_signal(barrier, 1, device_id={axis: peer}, device_id_type=MESH_ID)
        return carry

    lax.fori_loop(1, n, greet, 0)
    pl.semaphore_wait(barrier, n - 1)

    def source(j):
        return x_ref if gather else x_ref.at[j]

    def outgoing(d):
        j = lax.rem(me + d, n)
        return pltpu.make_async_remote_copy(
            src_ref=source(j),
            dst_ref=y_ref.at[me],
            send_sem=send_sem.at[j],
            recv_sem=recv_sem.at[me],
            device_id={axis: j},
            device_id_type=MESH_ID,
        )

    def incoming(d):
        k = lax.rem(me + n - d, n)
        return pltpu.make_async_remote_copy(
            src_ref=source(k),
            dst_ref=y_ref.at[k],
            send_sem=send_sem.at[k],
            recv_sem=recv_sem.at[k],
            device_id={axis: k},
            device_id_type=MESH_ID,
        )

    local = pltpu.make_async_copy(source(me), y_ref.at[me], local_sem)
    local.start()

    def start(d, carry):
        outgoing(d).start()
        return carry

    lax.fori_loop(1, n, start, 0)

    def finish(d, carry):
        outgoing(d).wait_send()
        incoming(d).wait_recv()
        return carry

    lax.fori_loop(1, n, finish, 0)
    local.wait()


def exchange(x, axis, n, cid, gather=False):
    piece = x.shape if gather else x.shape[1:]
    return pl.pallas_call(
        functools.partial(_exchange_kernel, n, axis, gather),
        out_shape=jax.ShapeDtypeStruct((n,) + tuple(piece), x.dtype),
        in_specs=[pl.BlockSpec(memory_space=pl.ANY)],
        out_specs=pl.BlockSpec(memory_space=pl.ANY),
        scratch_shapes=[
            pltpu.SemaphoreType.DMA((n,)),
            pltpu.SemaphoreType.DMA((n,)),
            pltpu.SemaphoreType.DMA(()),
        ],
        compiler_params=pltpu.CompilerParams(collective_id=cid, has_side_effects=True),
    )(x)


def _tail_kernel(
    n,
    sn,
    part_ref,
    w_out_ref,
    states_ref,
    gain_ref,
    gate_ref,
    down_ref,
    out_ref,
    seq_buf,
    att_buf,
    seq_send,
    seq_recv,
    abuf,
    pbuf,
    rbuf,
    sbuf,
    nbuf,
    gbuf,
    qbuf,
    rbuf2,
    send_sem,
    recv_sem,
    local_sem,
):
    axis = "tensor"
    me = lax.axis_index(axis)
    seq_me = lax.axis_index("seq")
    rows = states_ref.shape[0]
    barrier = pltpu.get_barrier_semaphore()

    def greet(d, carry):
        pl.semaphore_signal(
            barrier, 1, device_id={axis: lax.rem(me + d, n)}, device_id_type=MESH_ID
        )
        return carry

    lax.fori_loop(1, n, greet, 0)

    def greet_seq(d, carry):
        pl.semaphore_signal(
            barrier, 1, device_id={"seq": lax.rem(seq_me + d, sn)}, device_id_type=MESH_ID
        )
        return carry

    lax.fori_loop(1, sn, greet_seq, 0)
    pl.semaphore_wait(barrier, n - 1 + sn - 1)

    def seq_out(d):
        j = lax.rem(seq_me + d, sn)
        return pltpu.make_async_remote_copy(
            src_ref=part_ref,
            dst_ref=seq_buf.at[seq_me],
            send_sem=seq_send.at[j],
            recv_sem=seq_recv.at[seq_me],
            device_id={"seq": j},
            device_id_type=MESH_ID,
        )

    def seq_in(d):
        k = lax.rem(seq_me + sn - d, sn)
        return pltpu.make_async_remote_copy(
            src_ref=part_ref,
            dst_ref=seq_buf.at[k],
            send_sem=seq_send.at[k],
            recv_sem=seq_recv.at[k],
            device_id={"seq": k},
            device_id_type=MESH_ID,
        )

    seq_local = pltpu.make_async_copy(part_ref, seq_buf.at[seq_me], local_sem)
    seq_local.start()

    def seq_start(d, carry):
        seq_out(d).start()
        return carry

    lax.fori_loop(1, sn, seq_start, 0)

    def seq_finish(d, carry):
        seq_out(d).wait_send()
        seq_in(d).wait_recv()
        return carry

    lax.fori_loop(1, sn, seq_finish, 0)
    seq_local.wait()
    parts = seq_buf[...]
    lanes = att_buf.shape[2]
    part_top = parts[..., lanes + 1 : lanes + 2]
    top = jnp.max(part_top, axis=0)
    scale = jnp.exp(part_top - top[None])
    total = jnp.sum(parts[..., lanes : lanes + 1] * scale, axis=0)
    mixture = jnp.sum(parts[..., :lanes] * scale, axis=0)
    att_buf[...] = (mixture / total).astype(att_buf.dtype)
    units = down_ref.shape[0]

    def phase(p, src_of, dst_of):
        def outgoing(d):
            j = lax.rem(me + d, n)
            return pltpu.make_async_remote_copy(
                src_ref=src_of(j),
                dst_ref=dst_of(me),
                send_sem=send_sem.at[p, j],
                recv_sem=recv_sem.at[p, me],
                device_id={axis: j},
                device_id_type=MESH_ID,
            )

        def incoming(d):
            k = lax.rem(me + n - d, n)
            return pltpu.make_async_remote_copy(
                src_ref=src_of(k),
                dst_ref=dst_of(k),
                send_sem=send_sem.at[p, k],
                recv_sem=recv_sem.at[p, k],
                device_id={axis: k},
                device_id_type=MESH_ID,
            )

        local = pltpu.make_async_copy(src_of(me), dst_of(me), local_sem)
        local.start()

        def start(d, carry):
            outgoing(d).start()
            return carry

        lax.fori_loop(1, n, start, 0)

        def finish(d, carry):
            outgoing(d).wait_send()
            incoming(d).wait_recv()
            return carry

        lax.fori_loop(1, n, finish, 0)
        local.wait()

    def row_block(ref):
        return lambda i: ref.at[pl.ds(i * rows, rows)]

    phase(0, lambda j: att_buf.at[j], row_block(abuf))
    partial = jnp.dot(abuf[...], w_out_ref[...], preferred_element_type=jnp.float32)
    pbuf[...] = partial.astype(jnp.bfloat16)
    phase(1, row_block(pbuf), lambda k: rbuf.at[k])
    summed = jnp.sum(rbuf[...].astype(jnp.float32), axis=0)
    resid = (states_ref[...].astype(jnp.float32) + summed).astype(jnp.bfloat16)
    sbuf[...] = resid
    nbuf[...] = rms_norm(resid.astype(jnp.float32), gain_ref[...].reshape(1, -1))
    phase(2, lambda j: nbuf, row_block(gbuf))
    gathered = gbuf[...]
    gate = jnp.dot(gathered, gate_ref[:, 0, :], preferred_element_type=jnp.float32)
    up = jnp.dot(gathered, gate_ref[:, 1, :], preferred_element_type=jnp.float32)
    hidden = (jax.nn.silu(gate) * up).astype(jnp.bfloat16)
    down = jnp.dot(hidden, down_ref[...], preferred_element_type=jnp.float32)
    qbuf[...] = down.astype(jnp.bfloat16)
    phase(3, row_block(qbuf), lambda k: rbuf2.at[k])
    summed2 = jnp.sum(rbuf2[...].astype(jnp.float32), axis=0)
    out_ref[...] = (sbuf[...].astype(jnp.float32) + summed2).astype(out_ref.dtype)


def tail(part, w_out, states, gain, w_gate_up, w_down, n, sn, cid):
    rows, width = states.shape
    lanes = part.shape[2] - 2
    units = w_gate_up.shape[2]
    vmem = pl.BlockSpec(memory_space=pltpu.VMEM)
    return pl.pallas_call(
        functools.partial(_tail_kernel, n, sn),
        out_shape=jax.ShapeDtypeStruct((rows, width), states.dtype),
        in_specs=[vmem] * 6,
        out_specs=vmem,
        scratch_shapes=[
            pltpu.VMEM((sn,) + part.shape, jnp.float32),
            pltpu.VMEM((n, rows, lanes), jnp.bfloat16),
            pltpu.SemaphoreType.DMA((sn,)),
            pltpu.SemaphoreType.DMA((sn,)),
            pltpu.VMEM((n * rows, lanes), jnp.bfloat16),
            pltpu.VMEM((n * rows, width), jnp.bfloat16),
            pltpu.VMEM((n, rows, width), jnp.bfloat16),
            pltpu.VMEM((rows, width), jnp.bfloat16),
            pltpu.VMEM((rows, width), jnp.bfloat16),
            pltpu.VMEM((n * rows, width), jnp.bfloat16),
            pltpu.VMEM((n * rows, width), jnp.bfloat16),
            pltpu.VMEM((n, rows, width), jnp.bfloat16),
            pltpu.SemaphoreType.DMA((4, n)),
            pltpu.SemaphoreType.DMA((4, n)),
            pltpu.SemaphoreType.DMA(()),
        ],
        compiler_params=pltpu.CompilerParams(collective_id=cid, has_side_effects=True),
    )(part, w_out, states, gain, w_gate_up, w_down)


def _head_kernel(
    n, states_ref, gains_ref, w_ref, trig_ref, qkv_ref, recv_ref, x_ref, gbuf, send_sem, recv_sem, local_sem
):
    axis = "tensor"
    me = lax.axis_index(axis)
    rows = x_ref.shape[0]
    block = qkv_ref.shape[1] // 2
    x_ref[...] = rms_norm(states_ref[...].astype(jnp.float32), gains_ref[...].reshape(1, -1))
    barrier = pltpu.get_barrier_semaphore()

    def greet(d, carry):
        pl.semaphore_signal(
            barrier, 1, device_id={axis: lax.rem(me + d, n)}, device_id_type=MESH_ID
        )
        return carry

    lax.fori_loop(1, n, greet, 0)
    pl.semaphore_wait(barrier, n - 1)

    def phase(p, src_of, dst_of):
        def outgoing(d):
            j = lax.rem(me + d, n)
            return pltpu.make_async_remote_copy(
                src_ref=src_of(j),
                dst_ref=dst_of(me),
                send_sem=send_sem.at[p, j],
                recv_sem=recv_sem.at[p, me],
                device_id={axis: j},
                device_id_type=MESH_ID,
            )

        def incoming(d):
            k = lax.rem(me + n - d, n)
            return pltpu.make_async_remote_copy(
                src_ref=src_of(k),
                dst_ref=dst_of(k),
                send_sem=send_sem.at[p, k],
                recv_sem=recv_sem.at[p, k],
                device_id={axis: k},
                device_id_type=MESH_ID,
            )

        local = pltpu.make_async_copy(src_of(me), dst_of(me), local_sem)
        local.start()

        def start(d, carry):
            outgoing(d).start()
            return carry

        lax.fori_loop(1, n, start, 0)

        def finish(d, carry):
            outgoing(d).wait_send()
            incoming(d).wait_recv()
            return carry

        lax.fori_loop(1, n, finish, 0)
        local.wait()

    phase(0, lambda j: x_ref, lambda k: gbuf.at[pl.ds(k * rows, rows)])
    lanes = w_ref.shape[1]
    gathered = gbuf[...]
    contract_last = (((1,), (1,)), ((), ()))
    pair = lax.dot_general(
        gathered,
        w_ref[0:2].reshape(2 * lanes, w_ref.shape[2]),
        contract_last,
        preferred_element_type=jnp.float32,
    )
    value_proj = lax.dot_general(
        gathered, w_ref[2], contract_last, preferred_element_type=jnp.float32
    )
    trig = trig_ref[...]
    half = HEAD_SIZE // 2
    lane = lax.broadcasted_iota(jnp.int32, pair.shape, 1)
    turned = jnp.where(
        lane % HEAD_SIZE < half,
        -pltpu.roll(pair, block - half, 1),
        pltpu.roll(pair, half, 1),
    )
    rotated = pair * trig[:, :block] + turned * trig[:, block:]
    qkv_ref[:, :block] = rotated.astype(qkv_ref.dtype)
    qkv_ref[:, block : block + block // 2] = value_proj.astype(qkv_ref.dtype)
    qkv_ref[:, block + block // 2 :] = jnp.zeros((pair.shape[0], block // 2), qkv_ref.dtype)
    phase(1, lambda j: qkv_ref.at[pl.ds(j * rows, rows)], lambda k: recv_ref.at[k])


def head(states, gains, w_ext, trig, n, cid):
    rows, width = states.shape
    cols = w_ext.shape[1] * 4
    vmem = pl.BlockSpec(memory_space=pltpu.VMEM)
    return pl.pallas_call(
        functools.partial(_head_kernel, n),
        out_shape=(
            jax.ShapeDtypeStruct((n * rows, cols), jnp.bfloat16),
            jax.ShapeDtypeStruct((n, rows, cols), jnp.bfloat16),
        ),
        in_specs=[vmem] * 4,
        out_specs=(vmem, vmem),
        scratch_shapes=[
            pltpu.VMEM((rows, width), jnp.bfloat16),
            pltpu.VMEM((n * rows, width), jnp.bfloat16),
            pltpu.SemaphoreType.DMA((2, n)),
            pltpu.SemaphoreType.DMA((2, n)),
            pltpu.SemaphoreType.DMA(()),
        ],
        compiler_params=pltpu.CompilerParams(
            collective_id=cid, has_side_effects=True, vmem_limit_bytes=8 * 1024 * 1024
        ),
    )(states, gains, w_ext, trig)


def per_device(
    states,
    attn_gain,
    w_qkv,
    w_out,
    mlp_gain,
    w_gate_up,
    w_down,
    key_cache,
    value_cache,
    sink_keys,
    sink_values,
    cache_len,
    slot_mask,
    slot_pos,
    new_pos,
    tn,
    sn,
):
    rows = states.shape[0]
    width = states.shape[1]
    row_start = lax.axis_index("tensor") * rows
    floats = states.astype(jnp.float32)
    lanes = w_qkv.shape[2]
    heads_here = lanes // HEAD_SIZE
    half = HEAD_SIZE // 2
    inverse = jnp.exp(
        -jnp.log(jnp.float32(130000.0)) * jnp.arange(half, dtype=jnp.float32) * (2.0 / HEAD_SIZE)
    )
    angle = new_pos.astype(jnp.float32)[:, None] * inverse[None, :]
    angle = jnp.concatenate([angle] * (4 * heads_here), axis=-1)
    trig = jnp.concatenate([jnp.cos(angle), jnp.sin(angle)], axis=-1)
    sink_rows = sink_keys.astype(jnp.float32).reshape(
        rows, lanes * tn // HEAD_SIZE, HEAD_SIZE, sink_keys.shape[2]
    )
    states, sink_rows = lax.optimization_barrier((states, sink_rows))
    qkv_all, mine = head(states, attn_gain, jnp.transpose(w_qkv, (1, 2, 0)), trig, tn, 0)
    batch = qkv_all.shape[0]
    keys_all = qkv_all[:, lanes : 2 * lanes]
    values_all = qkv_all[:, 2 * lanes : 3 * lanes]
    mine = mine.reshape(tn, rows, 4, heads_here, HEAD_SIZE)
    mine = jnp.transpose(mine, (1, 2, 0, 3, 4)).reshape(rows, 4, tn * heads_here, HEAD_SIZE)
    queries = mine[:, 0]
    keys_new = mine[:, 1]
    values_new = mine[:, 2]
    all_heads = queries.shape[1]
    pick = jnp.arange(cache_len.shape[0], dtype=jnp.int32)[None, :] == (
        row_start + jnp.arange(rows, dtype=jnp.int32)
    )[:, None]
    own_len = jnp.sum(jnp.where(pick, cache_len[None, :], 0), axis=1)
    own_pos = jnp.sum(jnp.where(pick, new_pos[None, :], 0), axis=1)
    window_here = key_cache.shape[2]
    seq_index = lax.axis_index("seq")
    slots = seq_index * window_here + jnp.arange(window_here, dtype=jnp.int32)
    live = (slots[None, :] < own_len[:, None]) & (slot_mask == 1)
    live = live & (slot_pos < own_pos[:, None]) & (own_pos[:, None] - slot_pos < WINDOW)
    live = live[:, None, :]
    first_shard = seq_index == 0
    kwin = key_cache.reshape(rows, all_heads, HEAD_SIZE, window_here)
    vwin = value_cache.reshape(rows, all_heads, HEAD_SIZE, window_here)
    sink_key_rows = sink_keys.reshape(rows, all_heads, HEAD_SIZE, sink_keys.shape[2])
    vsink = sink_values.reshape(rows, all_heads, HEAD_SIZE, sink_values.shape[2])
    score_win = (
        jnp.einsum("bhd,bhds->bhs", queries, kwin, preferred_element_type=jnp.float32) * 0.125
    )
    score_win = jnp.where(live, score_win, NEG)
    score_sink = (
        jnp.sum(
            queries.astype(jnp.float32)[..., None] * sink_rows, axis=2
        )
        * 0.125
    )
    score_sink = jnp.where(first_shard, score_sink, NEG)
    score_new = jnp.sum(queries.astype(jnp.float32) * keys_new.astype(jnp.float32), axis=-1) * 0.125
    score_new = jnp.where(first_shard, score_new, NEG)
    local_top = jnp.maximum(
        jnp.maximum(jnp.max(score_win, axis=-1), jnp.max(score_sink, axis=-1)), score_new
    )
    weight_win = jnp.where(live, jnp.exp(score_win - local_top[..., None]), 0.0)
    weight_sink = jnp.where(first_shard, jnp.exp(score_sink - local_top[..., None]), 0.0)
    weight_new = jnp.where(first_shard, jnp.exp(score_new - local_top), 0.0)
    total = jnp.sum(weight_win, axis=-1) + jnp.sum(weight_sink, axis=-1) + weight_new
    mixture = jnp.einsum(
        "bhs,bhds->bhd", weight_win.astype(jnp.bfloat16), vwin, preferred_element_type=jnp.float32
    )
    mixture = mixture + jnp.sum(
        undo_round(weight_sink)[:, :, None, :] * vsink.astype(jnp.float32), axis=-1
    )
    mixture = mixture + undo_round(weight_new)[..., None] * values_new.astype(jnp.float32)
    packed = jnp.concatenate([mixture, total[..., None], local_top[..., None]], axis=-1)
    packed = jnp.transpose(packed, (1, 0, 2))
    out_states = tail(packed, w_out, states, mlp_gain, w_gate_up, w_down, tn, sn, 3)
    return (out_states, keys_all, values_all)


def solution(mesh):
    in_specs = (
        P("tensor", None),
        P(),
        P(None, None, "tensor"),
        P("tensor", None),
        P(),
        P(None, None, "tensor"),
        P("tensor", None),
        P("tensor", None, "seq"),
        P("tensor", None, "seq"),
        P("tensor", None, None),
        P("tensor", None, None),
        P(),
        P("tensor", "seq"),
        P("tensor", "seq"),
        P(),
    )
    out_specs = (P("tensor", None), P(None, "tensor"), P(None, "tensor"))
    body = functools.partial(per_device, tn=mesh.shape["tensor"], sn=mesh.shape["seq"])
    return jax.shard_map(
        body, mesh=mesh, in_specs=in_specs, out_specs=out_specs, check_vma=False
    )
```

```python
import functools

import jax
import jax.numpy as jnp
from jax import lax
from jax.experimental import pallas as pl
from jax.experimental.pallas import tpu as pltpu
from jax.sharding import PartitionSpec as P

HEAD_SIZE = 64
WINDOW = 4096


NEG = -1e30
MESH_ID = pl.DeviceIdType.MESH


def rms_norm(values, gain):
    meansq = jnp.mean(values * values, axis=-1, keepdims=True)
    return (values * lax.rsqrt(meansq + 1e-05) * gain.astype(jnp.float32)).astype(jnp.bfloat16)


def rotary(tensor, cosine, sine):
    half = tensor.shape[-1] // 2
    turned = jnp.concatenate([-tensor[..., half:], tensor[..., :half]], axis=-1)
    return tensor * cosine + turned * sine


def undo_round(weights):
    rounded = lax.optimization_barrier(weights.astype(jnp.bfloat16))
    return rounded.astype(jnp.float32)


def _exchange_kernel(n, axis, gather, x_ref, y_ref, send_sem, recv_sem, local_sem):
    me = lax.axis_index(axis)
    barrier = pltpu.get_barrier_semaphore()

    def greet(d, carry):
        peer = lax.rem(me + d, n)
        pl.semaphore_signal(barrier, 1, device_id={axis: peer}, device_id_type=MESH_ID)
        return carry

    lax.fori_loop(1, n, greet, 0)
    pl.semaphore_wait(barrier, n - 1)

    def source(j):
        return x_ref if gather else x_ref.at[j]

    def outgoing(d):
        j = lax.rem(me + d, n)
        return pltpu.make_async_remote_copy(
            src_ref=source(j),
            dst_ref=y_ref.at[me],
            send_sem=send_sem.at[j],
            recv_sem=recv_sem.at[me],
            device_id={axis: j},
            device_id_type=MESH_ID,
        )

    def incoming(d):
        k = lax.rem(me + n - d, n)
        return pltpu.make_async_remote_copy(
            src_ref=source(k),
            dst_ref=y_ref.at[k],
            send_sem=send_sem.at[k],
            recv_sem=recv_sem.at[k],
            device_id={axis: k},
            device_id_type=MESH_ID,
        )

    local = pltpu.make_async_copy(source(me), y_ref.at[me], local_sem)
    local.start()

    def start(d, carry):
        outgoing(d).start()
        return carry

    lax.fori_loop(1, n, start, 0)

    def finish(d, carry):
        outgoing(d).wait_send()
        incoming(d).wait_recv()
        return carry

    lax.fori_loop(1, n, finish, 0)
    local.wait()


def exchange(x, axis, n, cid, gather=False):
    piece = x.shape if gather else x.shape[1:]
    return pl.pallas_call(
        functools.partial(_exchange_kernel, n, axis, gather),
        out_shape=jax.ShapeDtypeStruct((n,) + tuple(piece), x.dtype),
        in_specs=[pl.BlockSpec(memory_space=pl.ANY)],
        out_specs=pl.BlockSpec(memory_space=pl.ANY),
        scratch_shapes=[
            pltpu.SemaphoreType.DMA((n,)),
            pltpu.SemaphoreType.DMA((n,)),
            pltpu.SemaphoreType.DMA(()),
        ],
        compiler_params=pltpu.CompilerParams(collective_id=cid, has_side_effects=True),
    )(x)


def _tail_kernel(
    n,
    sn,
    part_ref,
    w_out_ref,
    states_ref,
    gain_ref,
    gate_ref,
    down_ref,
    out_ref,
    seq_buf,
    att_buf,
    seq_send,
    seq_recv,
    abuf,
    pbuf,
    rbuf,
    sbuf,
    nbuf,
    gbuf,
    qbuf,
    rbuf2,
    send_sem,
    recv_sem,
    local_sem,
):
    axis = "tensor"
    me = lax.axis_index(axis)
    seq_me = lax.axis_index("seq")
    rows = states_ref.shape[0]
    barrier = pltpu.get_barrier_semaphore()

    def greet(d, carry):
        pl.semaphore_signal(
            barrier, 1, device_id={axis: lax.rem(me + d, n)}, device_id_type=MESH_ID
        )
        return carry

    lax.fori_loop(1, n, greet, 0)

    def greet_seq(d, carry):
        pl.semaphore_signal(
            barrier, 1, device_id={"seq": lax.rem(seq_me + d, sn)}, device_id_type=MESH_ID
        )
        return carry

    lax.fori_loop(1, sn, greet_seq, 0)
    pl.semaphore_wait(barrier, n - 1 + sn - 1)

    def seq_out(d):
        j = lax.rem(seq_me + d, sn)
        return pltpu.make_async_remote_copy(
            src_ref=part_ref,
            dst_ref=seq_buf.at[seq_me],
            send_sem=seq_send.at[j],
            recv_sem=seq_recv.at[seq_me],
            device_id={"seq": j},
            device_id_type=MESH_ID,
        )

    def seq_in(d):
        k = lax.rem(seq_me + sn - d, sn)
        return pltpu.make_async_remote_copy(
            src_ref=part_ref,
            dst_ref=seq_buf.at[k],
            send_sem=seq_send.at[k],
            recv_sem=seq_recv.at[k],
            device_id={"seq": k},
            device_id_type=MESH_ID,
        )

    seq_local = pltpu.make_async_copy(part_ref, seq_buf.at[seq_me], local_sem)
    seq_local.start()

    def seq_start(d, carry):
        seq_out(d).start()
        return carry

    lax.fori_loop(1, sn, seq_start, 0)

    def seq_finish(d, carry):
        seq_out(d).wait_send()
        seq_in(d).wait_recv()
        return carry

    lax.fori_loop(1, sn, seq_finish, 0)
    seq_local.wait()
    parts = seq_buf[...]
    lanes = att_buf.shape[2]
    part_top = parts[..., lanes + 1 : lanes + 2]
    top = jnp.max(part_top, axis=0)
    scale = jnp.exp(part_top - top[None])
    total = jnp.sum(parts[..., lanes : lanes + 1] * scale, axis=0)
    mixture = jnp.sum(parts[..., :lanes] * scale, axis=0)
    att_buf[...] = (mixture / total).astype(att_buf.dtype)
    units = down_ref.shape[0]

    def phase(p, src_of, dst_of):
        def outgoing(d):
            j = lax.rem(me + d, n)
            return pltpu.make_async_remote_copy(
                src_ref=src_of(j),
                dst_ref=dst_of(me),
                send_sem=send_sem.at[p, j],
                recv_sem=recv_sem.at[p, me],
                device_id={axis: j},
                device_id_type=MESH_ID,
            )

        def incoming(d):
            k = lax.rem(me + n - d, n)
            return pltpu.make_async_remote_copy(
                src_ref=src_of(k),
                dst_ref=dst_of(k),
                send_sem=send_sem.at[p, k],
                recv_sem=recv_sem.at[p, k],
                device_id={axis: k},
                device_id_type=MESH_ID,
            )

        local = pltpu.make_async_copy(src_of(me), dst_of(me), local_sem)
        local.start()

        def start(d, carry):
            outgoing(d).start()
            return carry

        lax.fori_loop(1, n, start, 0)

        def finish(d, carry):
            outgoing(d).wait_send()
            incoming(d).wait_recv()
            return carry

        lax.fori_loop(1, n, finish, 0)
        local.wait()

    def row_block(ref):
        return lambda i: ref.at[pl.ds(i * rows, rows)]

    phase(0, lambda j: att_buf.at[j], row_block(abuf))
    partial = jnp.dot(abuf[...], w_out_ref[...], preferred_element_type=jnp.float32)
    pbuf[...] = partial.astype(jnp.bfloat16)
    phase(1, row_block(pbuf), lambda k: rbuf.at[k])
    summed = jnp.sum(rbuf[...].astype(jnp.float32), axis=0)
    resid = (states_ref[...].astype(jnp.float32) + summed).astype(jnp.bfloat16)
    sbuf[...] = resid
    nbuf[...] = rms_norm(resid.astype(jnp.float32), gain_ref[...].reshape(1, -1))
    phase(2, lambda j: nbuf, row_block(gbuf))
    gate_up = jnp.dot(gbuf[...], gate_ref[...], preferred_element_type=jnp.float32)
    hidden = (jax.nn.silu(gate_up[:, :units]) * gate_up[:, units:]).astype(jnp.bfloat16)
    down = jnp.dot(hidden, down_ref[...], preferred_element_type=jnp.float32)
    qbuf[...] = down.astype(jnp.bfloat16)
    phase(3, row_block(qbuf), lambda k: rbuf2.at[k])
    summed2 = jnp.sum(rbuf2[...].astype(jnp.float32), axis=0)
    out_ref[...] = (sbuf[...].astype(jnp.float32) + summed2).astype(out_ref.dtype)


def tail(part, w_out, states, gain, w_gate_up, w_down, n, sn, cid):
    rows, width = states.shape
    lanes = part.shape[2] - 2
    units = w_gate_up.shape[2]
    vmem = pl.BlockSpec(memory_space=pltpu.VMEM)
    return pl.pallas_call(
        functools.partial(_tail_kernel, n, sn),
        out_shape=jax.ShapeDtypeStruct((rows, width), states.dtype),
        in_specs=[vmem] * 6,
        out_specs=vmem,
        scratch_shapes=[
            pltpu.VMEM((sn,) + part.shape, jnp.float32),
            pltpu.VMEM((n, rows, lanes), jnp.bfloat16),
            pltpu.SemaphoreType.DMA((sn,)),
            pltpu.SemaphoreType.DMA((sn,)),
            pltpu.VMEM((n * rows, lanes), jnp.bfloat16),
            pltpu.VMEM((n * rows, width), jnp.bfloat16),
            pltpu.VMEM((n, rows, width), jnp.bfloat16),
            pltpu.VMEM((rows, width), jnp.bfloat16),
            pltpu.VMEM((rows, width), jnp.bfloat16),
            pltpu.VMEM((n * rows, width), jnp.bfloat16),
            pltpu.VMEM((n * rows, width), jnp.bfloat16),
            pltpu.VMEM((n, rows, width), jnp.bfloat16),
            pltpu.SemaphoreType.DMA((4, n)),
            pltpu.SemaphoreType.DMA((4, n)),
            pltpu.SemaphoreType.DMA(()),
        ],
        compiler_params=pltpu.CompilerParams(collective_id=cid, has_side_effects=True),
    )(part, w_out, states, gain, w_gate_up.reshape(width, 2 * units), w_down)


def _head_kernel(
    n, states_ref, gains_ref, w_ref, trig_ref, qkv_ref, recv_ref, x_ref, gbuf, send_sem, recv_sem, local_sem
):
    axis = "tensor"
    me = lax.axis_index(axis)
    rows = x_ref.shape[0]
    block = qkv_ref.shape[1] // 2
    barrier = pltpu.get_barrier_semaphore()

    def greet(d, carry):
        pl.semaphore_signal(
            barrier, 1, device_id={axis: lax.rem(me + d, n)}, device_id_type=MESH_ID
        )
        return carry

    lax.fori_loop(1, n, greet, 0)
    x_ref[...] = rms_norm(states_ref[...].astype(jnp.float32), gains_ref[...].reshape(1, -1))
    pl.semaphore_wait(barrier, n - 1)

    def phase(p, src_of, dst_of):
        def outgoing(d):
            j = lax.rem(me + d, n)
            return pltpu.make_async_remote_copy(
                src_ref=src_of(j),
                dst_ref=dst_of(me),
                send_sem=send_sem.at[p, j],
                recv_sem=recv_sem.at[p, me],
                device_id={axis: j},
                device_id_type=MESH_ID,
            )

        def incoming(d):
            k = lax.rem(me + n - d, n)
            return pltpu.make_async_remote_copy(
                src_ref=src_of(k),
                dst_ref=dst_of(k),
                send_sem=send_sem.at[p, k],
                recv_sem=recv_sem.at[p, k],
                device_id={axis: k},
                device_id_type=MESH_ID,
            )

        local = pltpu.make_async_copy(src_of(me), dst_of(me), local_sem)
        local.start()

        def start(d, carry):
            outgoing(d).start()
            return carry

        lax.fori_loop(1, n, start, 0)

        def finish(d, carry):
            outgoing(d).wait_send()
            incoming(d).wait_recv()
            return carry

        lax.fori_loop(1, n, finish, 0)
        local.wait()

    phase(0, lambda j: x_ref, lambda k: gbuf.at[pl.ds(k * rows, rows)])
    lanes = w_ref.shape[1]
    gathered = gbuf[...]
    contract_last = (((1,), (1,)), ((), ()))
    pair = lax.dot_general(
        gathered,
        w_ref[0:2].reshape(2 * lanes, w_ref.shape[2]),
        contract_last,
        preferred_element_type=jnp.float32,
    )
    value_proj = lax.dot_general(
        gathered, w_ref[2], contract_last, preferred_element_type=jnp.float32
    )
    trig = trig_ref[...]
    half = HEAD_SIZE // 2
    lane = lax.broadcasted_iota(jnp.int32, pair.shape, 1)
    turned = jnp.where(
        lane % HEAD_SIZE < half,
        -pltpu.roll(pair, block - half, 1),
        pltpu.roll(pair, half, 1),
    )
    rotated = pair * trig[:, :block] + turned * trig[:, block:]
    qkv_ref[:, :block] = rotated.astype(qkv_ref.dtype)
    qkv_ref[:, block : block + block // 2] = value_proj.astype(qkv_ref.dtype)
    qkv_ref[:, block + block // 2 :] = jnp.zeros((pair.shape[0], block // 2), qkv_ref.dtype)
    phase(1, lambda j: qkv_ref.at[pl.ds(j * rows, rows)], lambda k: recv_ref.at[k])


def head(states, gains, w_ext, trig, n, cid):
    rows, width = states.shape
    cols = w_ext.shape[1] * 4
    vmem = pl.BlockSpec(memory_space=pltpu.VMEM)
    return pl.pallas_call(
        functools.partial(_head_kernel, n),
        out_shape=(
            jax.ShapeDtypeStruct((n * rows, cols), jnp.bfloat16),
            jax.ShapeDtypeStruct((n, rows, cols), jnp.bfloat16),
        ),
        in_specs=[vmem] * 4,
        out_specs=(vmem, vmem),
        scratch_shapes=[
            pltpu.VMEM((rows, width), jnp.bfloat16),
            pltpu.VMEM((n * rows, width), jnp.bfloat16),
            pltpu.SemaphoreType.DMA((2, n)),
            pltpu.SemaphoreType.DMA((2, n)),
            pltpu.SemaphoreType.DMA(()),
        ],
        compiler_params=pltpu.CompilerParams(
            collective_id=cid, has_side_effects=True, vmem_limit_bytes=8 * 1024 * 1024
        ),
    )(states, gains, w_ext, trig)


def per_device(
    states,
    attn_gain,
    w_qkv,
    w_out,
    mlp_gain,
    w_gate_up,
    w_down,
    key_cache,
    value_cache,
    sink_keys,
    sink_values,
    cache_len,
    slot_mask,
    slot_pos,
    new_pos,
    tn,
    sn,
):
    rows = states.shape[0]
    width = states.shape[1]
    row_start = lax.axis_index("tensor") * rows
    floats = states.astype(jnp.float32)
    lanes = w_qkv.shape[2]
    heads_here = lanes // HEAD_SIZE
    half = HEAD_SIZE // 2
    inverse = jnp.exp(
        -jnp.log(jnp.float32(130000.0)) * jnp.arange(half, dtype=jnp.float32) * (2.0 / HEAD_SIZE)
    )
    angle = new_pos.astype(jnp.float32)[:, None] * inverse[None, :]
    angle = jnp.concatenate([angle] * (4 * heads_here), axis=-1)
    trig = jnp.concatenate([jnp.cos(angle), jnp.sin(angle)], axis=-1)
    sink_rows = sink_keys.astype(jnp.float32).reshape(
        rows, lanes * tn // HEAD_SIZE, HEAD_SIZE, sink_keys.shape[2]
    )
    states, sink_rows = lax.optimization_barrier((states, sink_rows))
    qkv_all, mine = head(states, attn_gain, jnp.transpose(w_qkv, (1, 2, 0)), trig, tn, 0)
    batch = qkv_all.shape[0]
    keys_all = qkv_all[:, lanes : 2 * lanes]
    values_all = qkv_all[:, 2 * lanes : 3 * lanes]
    mine = mine.reshape(tn, rows, 4, heads_here, HEAD_SIZE)
    mine = jnp.transpose(mine, (1, 2, 0, 3, 4)).reshape(rows, 4, tn * heads_here, HEAD_SIZE)
    queries = mine[:, 0]
    keys_new = mine[:, 1]
    values_new = mine[:, 2]
    all_heads = queries.shape[1]
    pick = jnp.arange(cache_len.shape[0], dtype=jnp.int32)[None, :] == (
        row_start + jnp.arange(rows, dtype=jnp.int32)
    )[:, None]
    own_len = jnp.sum(jnp.where(pick, cache_len[None, :], 0), axis=1)
    own_pos = jnp.sum(jnp.where(pick, new_pos[None, :], 0), axis=1)
    window_here = key_cache.shape[2]
    seq_index = lax.axis_index("seq")
    slots = seq_index * window_here + jnp.arange(window_here, dtype=jnp.int32)
    live = (slots[None, :] < own_len[:, None]) & (slot_mask == 1)
    live = live & (slot_pos < own_pos[:, None]) & (own_pos[:, None] - slot_pos < WINDOW)
    live = live[:, None, :]
    first_shard = seq_index == 0
    kwin = key_cache.reshape(rows, all_heads, HEAD_SIZE, window_here)
    vwin = value_cache.reshape(rows, all_heads, HEAD_SIZE, window_here)
    sink_key_rows = sink_keys.reshape(rows, all_heads, HEAD_SIZE, sink_keys.shape[2])
    vsink = sink_values.reshape(rows, all_heads, HEAD_SIZE, sink_values.shape[2])
    score_win = (
        jnp.einsum("bhd,bhds->bhs", queries, kwin, preferred_element_type=jnp.float32) * 0.125
    )
    score_win = jnp.where(live, score_win, NEG)
    score_sink = (
        jnp.sum(
            queries.astype(jnp.float32)[..., None] * sink_rows, axis=2
        )
        * 0.125
    )
    score_sink = jnp.where(first_shard, score_sink, NEG)
    score_new = jnp.sum(queries.astype(jnp.float32) * keys_new.astype(jnp.float32), axis=-1) * 0.125
    score_new = jnp.where(first_shard, score_new, NEG)
    local_top = jnp.maximum(
        jnp.maximum(jnp.max(score_win, axis=-1), jnp.max(score_sink, axis=-1)), score_new
    )
    weight_win = jnp.where(live, jnp.exp(score_win - local_top[..., None]), 0.0)
    weight_sink = jnp.where(first_shard, jnp.exp(score_sink - local_top[..., None]), 0.0)
    weight_new = jnp.where(first_shard, jnp.exp(score_new - local_top), 0.0)
    total = jnp.sum(weight_win, axis=-1) + jnp.sum(weight_sink, axis=-1) + weight_new
    mixture = jnp.einsum(
        "bhs,bhds->bhd", weight_win.astype(jnp.bfloat16), vwin, preferred_element_type=jnp.float32
    )
    mixture = mixture + jnp.sum(
        undo_round(weight_sink)[:, :, None, :] * vsink.astype(jnp.float32), axis=-1
    )
    mixture = mixture + undo_round(weight_new)[..., None] * values_new.astype(jnp.float32)
    packed = jnp.concatenate([mixture, total[..., None], local_top[..., None]], axis=-1)
    packed = jnp.transpose(packed, (1, 0, 2))
    out_states = tail(packed, w_out, states, mlp_gain, w_gate_up, w_down, tn, sn, 3)
    return (out_states, keys_all, values_all)


def solution(mesh):
    in_specs = (
        P("tensor", None),
        P(),
        P(None, None, "tensor"),
        P("tensor", None),
        P(),
        P(None, None, "tensor"),
        P("tensor", None),
        P("tensor", None, "seq"),
        P("tensor", None, "seq"),
        P("tensor", None, None),
        P("tensor", None, None),
        P(),
        P("tensor", "seq"),
        P("tensor", "seq"),
        P(),
    )
    out_specs = (P("tensor", None), P(None, "tensor"), P(None, "tensor"))
    body = functools.partial(per_device, tn=mesh.shape["tensor"], sn=mesh.shape["seq"])
    return jax.shard_map(
        body, mesh=mesh, in_specs=in_specs, out_specs=out_specs, check_vma=False
    )
```
